32 devices in a mesh: gx: 8 (over z, core), gy: 4 (over y, x).
Axes of the slice: x: 2, y: 2, z: 4, core: 2. Of those that a mesh axis runs over, the one named last changes fastest.
Arguments:
- density: float32 [128, 64, 128], P('gx', 'gy'), may hold values from 0.05 to 1
- void_mask: int32 [128, 64, 128], P('gx', 'gy'), may hold values 0 or 1
- solid_mask: int32 [128, 64, 128], P('gx', 'gy'), may hold values 0 or 1
- fixed_mask: int32 [128, 64, 128], P('gx', 'gy'), may hold values 0 or 1
- load_mask: int32 [128, 64, 128], P('gx', 'gy'), may hold values from 0 to 1
- traction: float32 [3, 128, 64, 128], P(None, 'gx', 'gy'), may hold values from -6 to 6
Outputs:
- new_density: float32 [128, 64, 128], P('gx', 'gy')
- displacement: float32 [3, 128, 64, 128], P(None, 'gx', 'gy')
The draws below stay inside these ranges and needn't reach their ends.
All inputs are finite; a program needn't handle non-finite values. No bound on the sum of `void_mask` or of `solid_mask` or of `fixed_mask` on one device may be relied on, other than what follows from the above.
Results may differ from the reference program's by a relative error of at most 0.0001.
Values sent between devices are 32-bit elements; how exact they have to be, the bound alone decides.
No kernel may reach another device: no remote copies, remote signals or barrier semaphores. Data moves between devices by JAX's collectives and lax.ppermute only.
A program may use at most 64 MiB of HBM per device.

```python
import math
import jax
import jax.numpy as jnp
import numpy as np
from jax import lax

ITERS = 4
NEWTON = 3
NX = 128
NY = 64
NZ = 128


def draw_density(key, part):
    uniform_part = jax.random.uniform(jax.random.fold_in(key, 11), (NX, NY, NZ), jnp.float32)
    first_pos = jnp.arange(NX, dtype=jnp.float32)[:, None, None] / NX
    second_pos = jnp.arange(NY, dtype=jnp.float32)[None, :, None] / NY
    ramp = 0.35 + 0.65 * 0.5 * (first_pos + second_pos)
    return 0.05 + 0.95 * uniform_part * ramp


def draw_load_mask(key, part):
    first_pos = jnp.arange(NX, dtype=jnp.int32)[:, None, None]
    second_pos = jnp.arange(NY, dtype=jnp.int32)[None, :, None]
    threshold = 60 + 240 * (first_pos * NY + second_pos * NX) // (2 * NX * NY)
    draws = jax.random.randint(jax.random.fold_in(key, 7), (NX, NY, NZ), 0, 1000)
    return (draws < threshold).astype(jnp.int32)


def place_ends(entries, stream_key, low, largest):
    dims = entries.shape
    place = [jax.random.randint(jax.random.fold_in(stream_key, axis), (), 0, dims[axis]) for axis in range(len(dims))]
    entries = entries.at[tuple(place)].set(low)
    longest = dims.index(max(dims))
    place[longest] = (place[longest] + 1) % dims[longest]
    return entries.at[tuple(place)].set(largest)


def level_of(rng, dims, shards, smallest, high):
    gain, own = 1.0, jax.random.fold_in(rng, 6)
    for dim, blocks in shards:
        steps = jnp.exp(jax.random.uniform(jax.random.fold_in(own, dim), (blocks,), jnp.float32, smallest / len(shards), high / len(shards)))
        gain = gain * jnp.repeat(steps, dims[dim] // blocks).reshape([-1 if axis == dim else 1 for axis in range(len(dims))])
    return gain


def scatter_about(rng, dims, spread, bound, cuts=(), kind=jnp.bfloat16):
    drawn = jax.random.normal(rng, dims, jnp.float32) * spread
    if len(cuts) > 0:
        drawn = level_of(rng, dims, cuts, -0.22, 0.18) * drawn
    return jnp.clip(drawn, min=-bound, max=bound).astype(kind)


def setup_inputs(seed: int = 0) -> dict:
    key_list = jax.random.split(jax.random.key(seed), 7)
    return {
        "density": draw_density(jax.random.fold_in(key_list[6], 71), 0),
        "void_mask": place_ends((jax.random.randint(key_list[1], (NX, NY, NZ), 0, 12) < 1).astype(jnp.int32), jax.random.fold_in(key_list[1], 1), 0, 1),
        "solid_mask": place_ends((jax.random.randint(key_list[2], (NX, NY, NZ), 0, 12) < 1).astype(jnp.int32), jax.random.fold_in(key_list[2], 1), 0, 1),
        "fixed_mask": place_ends((jax.random.randint(key_list[3], (NX, NY, NZ), 0, 8) < 1).astype(jnp.int32), jax.random.fold_in(key_list[3], 1), 0, 1),
        "load_mask": draw_load_mask(jax.random.fold_in(key_list[6], 71), 0),
        "traction": scatter_about(key_list[5], (3, NX, NY, NZ), 1.0, 6.0, ((1, 8), (2, 4)), jnp.float32),
    }


E_MIN = 0.001
RHO_FLOOR = 0.001
MOVE_LIMIT = 0.2
VOLUME_SHARE = 0.4

def element_matrix():
    poisson = 0.3
    lame_first = poisson / ((1.0 + poisson) * (1.0 - 2.0 * poisson))
    shear_modulus = 1.0 / (2.0 * (1.0 + poisson))
    elastic = np.zeros((6, 6))
    elastic[:3, :3] = lame_first
    for axis_index in range(3):
        elastic[axis_index, axis_index] = lame_first + 2.0 * shear_modulus
        elastic[axis_index + 3, axis_index + 3] = shear_modulus
    gauss_points = [(1.0 - 1.0 / np.sqrt(3.0)) / 2.0, (1.0 + 1.0 / np.sqrt(3.0)) / 2.0]
    stiffness = np.zeros((24, 24))
    for point_x in gauss_points:
        for point_y in gauss_points:
            for point_z in gauss_points:
                strain = np.zeros((6, 24))
                for corner in range(8):
                    corner_x, corner_y, corner_z = (corner % 2, corner // 2 % 2, corner // 4)
                    factor_x = point_x if corner_x else 1.0 - point_x
                    factor_y = point_y if corner_y else 1.0 - point_y
                    factor_z = point_z if corner_z else 1.0 - point_z
                    grad_x = (2 * corner_x - 1) * factor_y * factor_z
                    grad_y = factor_x * (2 * corner_y - 1) * factor_z
                    grad_z = factor_x * factor_y * (2 * corner_z - 1)
                    column = 3 * corner
                    strain[0, column] = grad_x
                    strain[1, column + 1] = grad_y
                    strain[2, column + 2] = grad_z
                    strain[3, column] = grad_y
                    strain[3, column + 1] = grad_x
                    strain[4, column + 1] = grad_z
                    strain[4, column + 2] = grad_y
                    strain[5, column] = grad_z
                    strain[5, column + 2] = grad_x
                stiffness = stiffness + strain.T @ elastic @ strain / 8.0
    return stiffness

def cone_weights():
    offsets = np.arange(-2, 3)
    distance = np.sqrt(offsets[:, None, None] ** 2 + offsets[None, :, None] ** 2 + offsets[None, None, :] ** 2)
    return np.maximum(0.0, 3.0 - distance)

def cone_cosines(freqs, length):
    offsets = jnp.arange(-2, 3, dtype=jnp.int32)
    phases = jnp.mod(freqs[:, None] * offsets[None, :], length).astype(jnp.float32)
    return jnp.cos(phases * (2.0 * math.pi / length))

def next_layer(field):
    return jnp.concatenate([field[..., 1:], jnp.zeros_like(field[..., :1])], -1)

def prior_layer(field):
    return jnp.concatenate([jnp.zeros_like(field[..., :1]), field[..., :-1]], -1)

def node_forces(node_values, element_moduli, stiffness):
    row_count = node_values.shape[1] - 2
    col_count = node_values.shape[2] - 2
    lifted = next_layer(node_values)
    stacks = []
    for corner in range(8):
        corner_x, corner_y, corner_z = (corner % 2, corner // 2 % 2, corner // 4)
        source = lifted if corner_z else node_values
        stacks.append(source[:, corner_x:corner_x + row_count + 1, corner_y:corner_y + col_count + 1, :])
    corners = jnp.concatenate(stacks, 0)
    products = jnp.einsum('pq,qabz->pabz', stiffness, corners, precision=lax.Precision.HIGHEST)
    element_forces = products * element_moduli[None]
    summed = jnp.zeros((3, row_count, col_count, node_values.shape[3]), jnp.float32)
    for corner in range(8):
        corner_x, corner_y, corner_z = (corner % 2, corner // 2 % 2, corner // 4)
        part_forces = element_forces[3 * corner:3 * corner + 3, 1 - corner_x:1 - corner_x + row_count, 1 - corner_y:1 - corner_y + col_count, :]
        if corner_z:
            part_forces = prior_layer(part_forces)
        summed = summed + part_forces
    return summed

def element_energy(node_values, stiffness):
    row_count = node_values.shape[1] - 2
    col_count = node_values.shape[2] - 2
    lifted = next_layer(node_values)
    stacks = []
    for corner in range(8):
        corner_x, corner_y, corner_z = (corner % 2, corner // 2 % 2, corner // 4)
        source = lifted if corner_z else node_values
        stacks.append(source[:, 1 + corner_x:1 + corner_x + row_count, 1 + corner_y:1 + corner_y + col_count, :])
    corners = jnp.concatenate(stacks, 0)
    products = jnp.einsum('pq,qabz->pabz', stiffness, corners, precision=lax.Precision.HIGHEST)
    return lax.optimization_barrier(jnp.sum(corners * products, 0))

def node_diagonal(element_moduli, diag_entries):
    row_count = element_moduli.shape[0] - 1
    col_count = element_moduli.shape[1] - 1
    parts = [jnp.zeros((row_count, col_count, element_moduli.shape[2]), jnp.float32) for component in range(3)]
    for corner in range(8):
        corner_x, corner_y, corner_z = (corner % 2, corner // 2 % 2, corner // 4)
        window = element_moduli[1 - corner_x:1 - corner_x + row_count, 1 - corner_y:1 - corner_y + col_count, :]
        if corner_z:
            window = prior_layer(window)
        for component in range(3):
            parts[component] = parts[component] + window * float(diag_entries[3 * corner + component])
    return jnp.stack(parts)

def forces_blocks(padded, moduli_pad, stiffness, block_width):
    block_count = (padded.shape[1] - 2) // block_width
    starts = jnp.arange(block_count, dtype=jnp.int32) * block_width

    def one_block(block_start):
        node_values = lax.dynamic_slice_in_dim(padded, block_start, block_width + 2, 1)
        element_moduli = lax.dynamic_slice_in_dim(moduli_pad, block_start, block_width + 1, 0)
        return node_forces(node_values, element_moduli, stiffness)
    blocks = lax.map(one_block, starts)
    return jnp.moveaxis(blocks, 0, 1).reshape(3, block_count * block_width, padded.shape[2] - 2, padded.shape[3])

def energy_blocks(padded, stiffness, block_width):
    block_count = (padded.shape[1] - 2) // block_width
    starts = jnp.arange(block_count, dtype=jnp.int32) * block_width

    def one_block(block_start):
        node_values = lax.dynamic_slice_in_dim(padded, block_start, block_width + 2, 1)
        return element_energy(node_values, stiffness)
    blocks = lax.map(one_block, starts)
    return blocks.reshape(block_count * block_width, padded.shape[2] - 2, padded.shape[3])

def reference(density, void_mask, solid_mask, fixed_mask, load_mask, traction):
    table = element_matrix()
    stiffness = jnp.asarray(table, jnp.float32)
    diag_entries = [float(table[index, index]) for index in range(24)]
    rho_phys = jnp.where(solid_mask == 1, 1.0, jnp.where(void_mask == 1, RHO_FLOOR, density)).astype(jnp.float32)
    moduli = E_MIN + rho_phys ** 3 * (1.0 - E_MIN)
    free_mask = (1 - fixed_mask).astype(jnp.float32)
    nodal_loads = free_mask * load_mask.astype(jnp.float32) * traction
    moduli_pad = jnp.pad(moduli, ((1, 0), (1, 0), (0, 0)))
    jacobi = free_mask * node_diagonal(moduli_pad, diag_entries) + (1.0 - free_mask)
    block_width = math.gcd(NX, 8)

    def operate(field):
        padded = jnp.pad(free_mask * field, ((0, 0), (1, 1), (1, 1), (0, 0)))
        return free_mask * forces_blocks(padded, moduli_pad, stiffness, block_width) + (1.0 - free_mask) * field
    solution = jnp.zeros_like(nodal_loads)
    residual = nodal_loads
    precond = residual / jacobi
    direction = precond
    residual_dot = jnp.sum(residual * precond)
    for iteration in range(ITERS):
        applied = operate(direction)
        step_size = residual_dot / jnp.sum(direction * applied)
        solution = solution + step_size * direction
        residual = residual - step_size * applied
        if iteration + 1 < ITERS:
            precond = residual / jacobi
            dot_next = jnp.sum(residual * precond)
            direction = precond + dot_next / residual_dot * direction
            residual_dot = dot_next
    padded = jnp.pad(solution, ((0, 0), (1, 1), (1, 1), (0, 0)))
    energy = energy_blocks(padded, stiffness, block_width)
    sens = 3.0 * rho_phys ** 2 * (1.0 - E_MIN) * energy
    weights = cone_weights()
    weight_sum = float(weights.sum())
    spectrum = jnp.einsum('xa,yb,zc,abc->xyz', cone_cosines(jnp.arange(NX, dtype=jnp.int32), NX), cone_cosines(jnp.arange(NY, dtype=jnp.int32), NY), cone_cosines(jnp.arange(NZ, dtype=jnp.int32), NZ), jnp.asarray(weights, jnp.float32))
    convolved = jnp.real(jnp.fft.ifftn(jnp.fft.fftn(rho_phys * sens) * spectrum))
    filtered = convolved / (weight_sum * rho_phys)
    root_term = rho_phys * jnp.sqrt(filtered)
    lower = jnp.maximum(RHO_FLOOR, rho_phys - MOVE_LIMIT)
    upper = jnp.minimum(1.0, rho_phys + MOVE_LIMIT)

    def trial(log_multiplier):
        moved = jnp.clip(root_term * jnp.exp(-0.5 * log_multiplier), lower, upper)
        return jnp.where(solid_mask == 1, 1.0, jnp.where(void_mask == 1, RHO_FLOOR, moved))
    target = VOLUME_SHARE * NX * NY * NZ
    log_multiplier = jnp.zeros((), jnp.float32)
    for newton_step in range(NEWTON):
        volume = jnp.sum(trial(log_multiplier))
        log_multiplier = log_multiplier + 2.0 * jnp.log(volume / target)
    return (trial(log_multiplier), solution)
```

```python
import functools
import math

import jax
import jax.numpy as jnp
import numpy as np
from jax import lax
from jax.experimental import pallas as pl
from jax.experimental.pallas import tpu as pltpu
from jax.sharding import PartitionSpec as P

E_MIN = 0.001
RHO_FLOOR = 0.001
MOVE_LIMIT = 0.2
VOLUME_SHARE = 0.4
BASIS = 4
HALO = BASIS
REACH = 2
AXES = ("gx", "gy")
VMEM_LIMIT = 40 * 1024 * 1024

POISSON = 0.3
LAME = POISSON / ((1.0 + POISSON) * (1.0 - 2.0 * POISSON))
SHEAR = 1.0 / (2.0 * (1.0 + POISSON))
NORMAL = 2.0 * SHEAR / 16.0
TRACE = LAME / 16.0
SHEAR_FIRST = SHEAR / 16.0
BEND = (LAME + 3.0 * SHEAR) / 48.0
BEND_MIX = LAME / 48.0
TWIST = SHEAR / 48.0
THIRD = (LAME + 4.0 * SHEAR) / 144.0
DIAGONAL = NORMAL + TRACE + 2.0 * SHEAR_FIRST + 2.0 * BEND + 2.0 * TWIST + THIRD
PAIRS = (("xdds", "zsdd"), ("ydds", "zdsd"), ("xdsd", "ysdd"))
TRIPLE = ("zdds", "ydsd", "xsdd")
CLASSES = [c + y + z for c in "xyz" for y in "sd" for z in "sd"]


def physical(density, void_mask, solid_mask):
    return jnp.where(solid_mask == 1, 1.0, jnp.where(void_mask == 1, RHO_FLOOR, density))


def lane_index(shape):
    return lax.broadcasted_iota(jnp.int32, shape, len(shape) - 1)


def plane_modes(lower, upper, keep_last):
    depth = keep_last.shape[-1]
    modes = {}
    for component, low, high in zip("xyz", lower, upper):
        for name, part in (("s", low + high), ("d", high - low)):
            lifted = pltpu.roll(part, depth - 1, 1) * keep_last
            modes[component + name + "s"] = lifted + part
            modes[component + name + "d"] = lifted - part
    return modes


def element_modes(before, after):
    modes = {}
    for key in CLASSES:
        if key[1:] != "ss":
            modes[key[0] + "s" + key[1:]] = after[key] + before[key]
        modes[key[0] + "d" + key[1:]] = after[key] - before[key]
    return modes


def mode_forces(u, moduli):
    forces = {}
    normal = moduli * NORMAL
    trace = (u["xdss"] + u["ysds"] + u["zssd"]) * (TRACE / NORMAL)
    for key in ("xdss", "ysds", "zssd"):
        forces[key] = normal * (u[key] + trace)
    shear = moduli * SHEAR_FIRST
    for one, other in (("ydss", "xsds"), ("zsds", "yssd"), ("xssd", "zdss")):
        forces[one] = forces[other] = shear * (u[one] + u[other])
    bend = moduli * BEND
    for one, other in PAIRS:
        forces[one] = bend * (u[one] + (BEND_MIX / BEND) * u[other])
        forces[other] = bend * (u[other] + (BEND_MIX / BEND) * u[one])
    twist = moduli * TWIST
    total = u[TRIPLE[0]] + u[TRIPLE[1]] + u[TRIPLE[2]]
    for key in TRIPLE:
        forces[key] = twist * (total + u[key])
    third = moduli * THIRD
    for component in "xyz":
        forces[component + "ddd"] = third * u[component + "ddd"]
    return forces


def unit_energy(u):
    trace = u["xdss"] + u["ysds"] + u["zssd"]
    energy = TRACE * (trace * trace)
    energy += NORMAL * (u["xdss"] ** 2 + u["ysds"] ** 2 + u["zssd"] ** 2)
    shears = [u[a] + u[b] for a, b in (("ydss", "xsds"), ("zsds", "yssd"), ("xssd", "zdss"))]
    energy += SHEAR_FIRST * (shears[0] ** 2 + shears[1] ** 2 + shears[2] ** 2)
    squares, mixed = 0.0, 0.0
    for one, other in PAIRS:
        squares += u[one] ** 2 + u[other] ** 2
        mixed += (u[one] + u[other]) ** 2
    energy += (BEND - BEND_MIX) * squares + BEND_MIX * mixed
    total = u[TRIPLE[0]] + u[TRIPLE[1]] + u[TRIPLE[2]]
    squares = total * total
    for key in TRIPLE:
        squares += u[key] ** 2
    energy += TWIST * squares
    energy += THIRD * (u["xddd"] ** 2 + u["yddd"] ** 2 + u["zddd"] ** 2)
    return energy


def fields_kernel(shape, density, void, solid, fixed, load, traction, own, low, high):
    rows, cols, _ = shape
    rho = physical(density[...], void[...], solid[...])
    own[0] = E_MIN + rho * rho * rho * (1.0 - E_MIN)
    free = (1 - fixed[...]).astype(jnp.float32)
    own[1] = free
    loaded = free * load[...].astype(jnp.float32)
    for component in range(3):
        own[2 + component] = loaded * traction[component]
    for layer in range(HALO):
        for field in range(5):
            low[layer, field] = own[field, pl.ds(layer, rows, stride=cols), :]
            high[layer, field] = own[field, pl.ds(cols - HALO + layer, rows, stride=cols), :]


def widen_kernel(shape, own, from_low, from_high, ext, low, high):
    rows, cols, _ = shape
    wide = cols + 2 * HALO
    for field in range(5):
        for row in range(rows):
            ext[field, pl.ds(row * wide + HALO, cols), :] = own[field, pl.ds(row * cols, cols), :]
        for layer in range(HALO):
            ext[field, pl.ds(layer, rows, stride=wide), :] = from_low[layer, field]
            ext[field, pl.ds(wide - HALO + layer, rows, stride=wide), :] = from_high[layer, field]
        low[field] = ext[field, : HALO * wide, :]
        high[field] = ext[field, (rows - HALO) * wide :, :]


def basis_kernel(
    shape, ext, from_low, from_high, basis_out, sums_out, field_ref, inverse_ref, p_ref, w_ref, mode_ref, lift_ref
):
    rows, cols, depth = shape
    wide, long = cols + 2 * HALO, rows + 2 * HALO
    lanes = lane_index((wide, depth))
    keep_last = jnp.where(lanes < depth - 1, 1.0, 0.0)
    keep_first = jnp.where(lanes > 0, 1.0, 0.0)

    field_ref[:, :8, :] = jnp.zeros((long, 8, depth), jnp.float32)
    p_ref[:, :, :, wide:, :] = jnp.zeros((BASIS, 3, long, 8, depth), jnp.float32)

    def place(source, source_row, plane):
        moduli = source[0, pl.ds(source_row, wide), :]
        field_ref[plane, 8:, :] = moduli
        inverse_ref[0, plane] = source[1, pl.ds(source_row, wide), :]
        for component in range(3):
            w_ref[0, component, plane] = source[2 + component, pl.ds(source_row, wide), :]

    for layer in range(HALO):
        place(from_low, layer * wide, layer)
        place(from_high, layer * wide, long - HALO + layer)

    def place_own(row, carry):
        place(ext, pl.multiple_of(row * wide, 8), row + HALO)
        return carry

    lax.fori_loop(0, rows, place_own, 0)

    def start(plane, carry):
        around = (
            field_ref[plane, 8:, :]
            + field_ref[plane - 1, 8:, :]
            + field_ref[plane, 7 : 7 + wide, :]
            + field_ref[plane - 1, 7 : 7 + wide, :]
        )
        around = around + pltpu.roll(around, 1, 1) * keep_first
        free = inverse_ref[0, plane]
        inverse = 1.0 / (free * (DIAGONAL * around) + (1.0 - free))
        inverse_ref[1, plane] = inverse
        for component in range(3):
            p_ref[0, component, plane, :wide] = w_ref[0, component, plane] * inverse
        return carry

    lax.fori_loop(1, long, start, 0)

    def load_modes(level, plane):
        return plane_modes(
            [p_ref[level, c, plane, :wide, :] for c in range(3)],
            [p_ref[level, c, plane, 1 : wide + 1, :] for c in range(3)],
            keep_last,
        )

    for level in range(BASIS - 1):
        first, last = level + 1, long - 2 - level
        modes = load_modes(level, first)
        for index, key in enumerate(CLASSES):
            mode_ref[index] = modes[key]
            lift_ref[index] = jnp.zeros((wide, depth), jnp.float32)

        def layer_step(plane, carry):
            after = load_modes(level, plane + 1)
            before = {key: mode_ref[index] for index, key in enumerate(CLASSES)}
            forces = mode_forces(element_modes(before, after), field_ref[plane, 8:, :])
            for index, key in enumerate(CLASSES):
                mode_ref[index] = after[key]
            free = inverse_ref[0, plane]
            inverse = inverse_ref[1, plane]
            for number, component in enumerate("xyz"):
                along_y = {}
                for y in "sd":
                    along_z = {}
                    for z in "sd":
                        index = CLASSES.index(component + y + z)
                        slope = forces[component + "d" + y + z]
                        if y + z == "ss":
                            low, high = -slope, slope
                        else:
                            mean = forces[component + "s" + y + z]
                            low, high = mean - slope, mean + slope
                        along_z[z] = lift_ref[index] + low
                        lift_ref[index] = high
                    along_y[y] = (along_z["s"] - along_z["d"]) + pltpu.roll(
                        along_z["s"] + along_z["d"], 1, 1
                    ) * keep_first
                force = (along_y["s"] - along_y["d"]) + pltpu.roll(along_y["s"] + along_y["d"], 1, 0)
                residual = free * force - w_ref[level, number, plane]
                w_ref[level + 1, number, plane] = residual
                p_ref[level + 1, number, plane, :wide] = residual * inverse
            return carry

        lax.fori_loop(first, last + 1, layer_step, 0)

    keep = keep_last[:cols]

    def own_modes(plane):
        last = BASIS - 1
        return plane_modes(
            [p_ref[last, c, plane, HALO : HALO + cols, :] for c in range(3)],
            [p_ref[last, c, plane, HALO + 1 : HALO + cols + 1, :] for c in range(3)],
            keep,
        )

    pairs = [(i, j) for i in range(BASIS) for j in range(i + 1)]
    modes = own_modes(HALO)
    for index, key in enumerate(CLASSES):
        mode_ref[index, :cols] = modes[key]

    def dot_step(plane, totals):
        totals = list(totals)
        window = pl.ds(HALO, cols)
        for component in range(3):
            ps = [p_ref[level, component, plane, window, :] for level in range(BASIS)]
            ws = [w_ref[level, component, plane, window, :] for level in range(BASIS)]
            for index, (i, j) in enumerate(pairs):
                totals[index] = totals[index] + ps[i] * ws[j]
        after = own_modes(plane + 1)
        before = {key: mode_ref[index, :cols] for index, key in enumerate(CLASSES)}
        for index, key in enumerate(CLASSES):
            mode_ref[index, :cols] = after[key]
        energy = unit_energy(element_modes(before, after))
        totals[-1] = totals[-1] + field_ref[plane, 8 + HALO : 8 + HALO + cols, :] * energy
        return tuple(totals)

    zeros = jnp.zeros((cols, depth), jnp.float32)
    totals = lax.fori_loop(HALO, HALO + rows, dot_step, (zeros,) * (len(pairs) + 1))
    slots = lane_index((1, 128))
    line = jnp.zeros((1, 128), jnp.float32)
    for index, total in enumerate(totals):
        share = jnp.sum(jnp.sum(total, axis=0, keepdims=True), axis=1, keepdims=True)
        line = line + jnp.where(slots == index, share, 0.0)
    sums_out[...] = jnp.broadcast_to(line, sums_out.shape)

    def emit(row, carry):
        for level in range(BASIS):
            for component in range(3):
                basis_out[level, component, row] = p_ref[level, component, row + HALO, HALO : HALO + cols + 8, :]
        return carry

    lax.fori_loop(0, rows + 1, emit, 0)


def coefficients(shares):
    line = jnp.sum(shares, axis=0, keepdims=True)
    slots = lane_index(line.shape)

    def entry(index):
        return jnp.sum(jnp.where(slots == index, line, 0.0), axis=1, keepdims=True)

    inner = {}
    for index, (i, j) in enumerate([(i, j) for i in range(BASIS) for j in range(i + 1)]):
        inner[i, j] = inner[j, i] = entry(index)
    energy = {(BASIS - 1, BASIS - 1): entry(BASIS * (BASIS + 1) // 2)}
    for i in range(BASIS):
        for j in range(min(i + 1, BASIS - 1)):
            energy[i, j] = inner[i, j + 1] + inner[i, j]
    lower, pivot, inverse, solved = {}, {}, {}, {}
    for k in range(BASIS):
        left = energy[k, k]
        for m in range(k):
            left = left - lower[k, m] * lower[k, m] * pivot[m]
        sound = left > 1e-6 * energy[k, k]
        pivot[k] = jnp.where(sound, left, 0.0)
        inverse[k] = jnp.where(sound, 1.0 / jnp.where(sound, left, 1.0), 0.0)
        for i in range(k + 1, BASIS):
            part = energy[i, k]
            for m in range(k):
                part = part - lower[i, m] * lower[k, m] * pivot[m]
            lower[i, k] = part * inverse[k]
    for k in range(BASIS):
        part = inner[k, 0]
        for m in range(k):
            part = part - lower[k, m] * solved[m]
        solved[k] = part
    result = {}
    for k in reversed(range(BASIS)):
        part = solved[k] * inverse[k]
        for m in range(k + 1, BASIS):
            part = part - lower[m, k] * result[m]
        result[k] = part
    return [result[k] for k in range(BASIS)]


def energy_kernel(
    shape, shares, basis, density, void, solid, displacement, weighted, low, high, u_ref, mode_ref
):
    rows, cols, depth = shape
    keep_last = jnp.where(lane_index((cols, depth)) < depth - 1, 1.0, 0.0)
    parts = [jnp.broadcast_to(part, (cols + 8, depth)) for part in coefficients(shares[...])]

    def combine(row, carry):
        for component in range(3):
            total = parts[0] * basis[0, component, row]
            for level in range(1, BASIS):
                total = total + parts[level] * basis[level, component, row]
            u_ref[component, row] = total
        return carry

    lax.fori_loop(0, rows + 1, combine, 0)

    def own_modes(row):
        return plane_modes(
            [u_ref[c, row, :cols, :] for c in range(3)],
            [u_ref[c, row, 1 : cols + 1, :] for c in range(3)],
            keep_last,
        )

    modes = own_modes(0)
    for index, key in enumerate(CLASSES):
        mode_ref[index] = modes[key]

    def energy_step(row, carry):
        after = own_modes(row + 1)
        before = {key: mode_ref[index] for index, key in enumerate(CLASSES)}
        for index, key in enumerate(CLASSES):
            mode_ref[index] = after[key]
        energy = unit_energy(element_modes(before, after))
        rho = physical(density[row], void[row], solid[row])
        weighted[pl.ds(pl.multiple_of(row * cols, 8), cols), :] = rho * (
            3.0 * rho * rho * (1.0 - E_MIN) * energy
        )
        for component in range(3):
            displacement[component, row] = u_ref[component, row, :cols, :]
        return carry

    lax.fori_loop(0, rows, energy_step, 0)
    for layer in range(REACH):
        low[layer] = weighted[pl.ds(layer, rows, stride=cols), :]
        high[layer] = weighted[pl.ds(cols - REACH + layer, rows, stride=cols), :]


def stretch_kernel(shape, own, from_low, from_high, ext, low, high):
    rows, cols, _ = shape
    wide = cols + 8
    for row in range(rows):
        ext[pl.ds(row * wide + REACH, cols), :] = own[pl.ds(row * cols, cols), :]
    for layer in range(REACH):
        ext[pl.ds(layer, rows, stride=wide), :] = from_low[layer]
        ext[pl.ds(REACH + cols + layer, rows, stride=wide), :] = from_high[layer]
    for layer in range(2 * REACH, 8):
        ext[pl.ds(cols + layer, rows, stride=wide), :] = jnp.zeros_like(from_low[0])
    low[...] = ext[: REACH * wide, :]
    high[...] = ext[(rows - REACH) * wide :, :]


def cone_table():
    table, total = {}, 0.0
    for a in range(-2, 3):
        for b in range(-2, 3):
            for c in range(-2, 3):
                total += max(0.0, 3.0 - math.sqrt(a * a + b * b + c * c))
    for flat in (0, 1, 2, 4, 5, 8):
        for c in range(3):
            table[flat, c] = max(0.0, 3.0 - math.sqrt(flat + c * c))
    return table, total


def volume_row(total):
    return jnp.sum(total, axis=0, keepdims=True)


def filter_kernel(
    shape, ext, from_low, from_high, density, void, solid, root, lower, upper, volume, plane_ref
):
    rows, cols, depth = shape
    wide = cols + 8
    table, total = cone_table()
    plane_ref[: REACH * wide, :] = from_low[...]
    plane_ref[REACH * wide : (rows + REACH) * wide, :] = ext[...]
    plane_ref[(rows + REACH) * wide :, :] = from_high[...]
    volume_sum = jnp.zeros((cols, depth), jnp.float32)
    for row in range(rows):
        spread = {}
        for a in range(-REACH, REACH + 1):
            for b in range(-REACH, REACH + 1):
                key = a * a + b * b
                value = plane_ref[pl.ds((row + REACH + a) * wide + REACH + b, cols), :]
                spread[key] = value if key not in spread else spread[key] + value
        sums = []
        for c in range(3):
            part = None
            for key, value in spread.items():
                if table[key, c] > 0.0:
                    term = table[key, c] * value
                    part = term if part is None else part + term
            sums.append(part)
        convolved = sums[0]
        for c in (1, 2):
            convolved = convolved + (pltpu.roll(sums[c], c, 1) + pltpu.roll(sums[c], depth - c, 1))
        is_solid, is_void = solid[row] == 1, void[row] == 1
        rho = physical(density[row], void[row], solid[row])
        base = rho * jnp.sqrt(convolved / (total * rho))
        low = jnp.maximum(RHO_FLOOR, rho - MOVE_LIMIT)
        high = jnp.minimum(1.0, rho + MOVE_LIMIT)
        low = jnp.where(is_solid, 1.0, jnp.where(is_void, RHO_FLOOR, low))
        high = jnp.where(is_solid, 1.0, jnp.where(is_void, RHO_FLOOR, high))
        root[row] = base
        lower[row] = low
        upper[row] = high
        volume_sum = volume_sum + jnp.minimum(jnp.maximum(base, low), high)
    volume[...] = jnp.broadcast_to(volume_row(volume_sum), volume.shape)


def scale_of(target, volumes):
    scale = None
    for volume in volumes:
        whole = jnp.sum(jnp.sum(volume[...], axis=0, keepdims=True), axis=1, keepdims=True)
        ratio = target / whole
        scale = ratio if scale is None else scale * ratio
    return scale


def trial_kernel(target, steps, final, *refs):
    volumes, (root, lower, upper, out) = refs[:steps], refs[steps:]
    scale = scale_of(target, volumes)
    moved = jnp.minimum(jnp.maximum(root[...] * scale[None], lower[...]), upper[...])
    if final:
        out[...] = moved
    else:
        total = jnp.sum(moved, axis=0)
        out[...] = jnp.broadcast_to(volume_row(total), out.shape)


def call(kernel, name, out_shapes, *args, scratch=(), flops=0):
    shapes = [jax.ShapeDtypeStruct(shape, jnp.float32) for shape in out_shapes]
    moved = sum(4 * math.prod(value.shape) for value in [*args, *shapes])
    whole = pl.BlockSpec(memory_space=pltpu.VMEM)
    return pl.pallas_call(
        kernel,
        name=name,
        out_shape=shapes,
        in_specs=[whole] * len(args),
        out_specs=[whole] * len(shapes),
        scratch_shapes=[pltpu.VMEM(shape, jnp.float32) for shape in scratch],
        compiler_params=pltpu.CompilerParams(vmem_limit_bytes=VMEM_LIMIT),
        cost_estimate=pl.CostEstimate(flops=flops, bytes_accessed=moved, transcendentals=0),
    )(*args)


def exchange(low, high, axis, wrap):
    count = lax.axis_size(axis)
    ends = count if wrap else count - 1
    from_low = lax.ppermute(high, axis, [(i, (i + 1) % count) for i in range(ends)])
    from_high = lax.ppermute(low, axis, [((i + 1) % count, i) for i in range(ends)])
    return from_low, from_high


def everyone(shares):
    return lax.all_to_all(shares, AXES, 0, 0, tiled=True)


def shards(density, void_mask, solid_mask, fixed_mask, load_mask, traction):
    shape = rows, cols, depth = density.shape
    devices = lax.axis_size("gx") * lax.axis_size("gy")
    wide, long = cols + 2 * HALO, rows + 2 * HALO
    named = lambda kernel: functools.partial(kernel, shape)
    flat = lambda value: value.reshape(*value.shape[:-3], -1, depth)

    own, low, high = call(
        named(fields_kernel),
        "fields",
        [(5, rows * cols, depth), (HALO, 5, rows, depth), (HALO, 5, rows, depth)],
        *[flat(v) for v in (density, void_mask, solid_mask, fixed_mask, load_mask, traction)],
    )
    from_low, from_high = exchange(low, high, "gy", False)
    ext, low, high = call(
        named(widen_kernel),
        "widen",
        [(5, rows * wide, depth), (5, HALO * wide, depth), (5, HALO * wide, depth)],
        own,
        from_low,
        from_high,
    )
    from_low, from_high = exchange(low, high, "gx", False)
    basis, sums = call(
        named(basis_kernel),
        "basis",
        [(BASIS, 3, rows + 1, cols + 8, depth), (devices, 128)],
        ext,
        from_low,
        from_high,
        scratch=[
            (long, 8 + wide, depth),
            (2, long, wide, depth),
            (BASIS, 3, long, wide + 8, depth),
            (BASIS, 3, long, wide, depth),
            (12, wide, depth),
            (12, wide, depth),
        ],
    )
    displacement, weighted, low, high = call(
        named(energy_kernel),
        "energy",
        [(3, rows, cols, depth), (rows * cols, depth), (REACH, rows, depth), (REACH, rows, depth)],
        everyone(sums),
        basis,
        density,
        void_mask,
        solid_mask,
        scratch=[(3, rows + 1, cols + 8, depth), (12, cols, depth)],
    )
    from_low, from_high = exchange(low, high, "gy", True)
    ext, low, high = call(
        named(stretch_kernel),
        "stretch",
        [(rows * (cols + 8), depth), (REACH * (cols + 8), depth), (REACH * (cols + 8), depth)],
        weighted,
        from_low,
        from_high,
    )
    from_low, from_high = exchange(low, high, "gx", True)
    *terms, volume = call(
        named(filter_kernel),
        "filter",
        [shape, shape, shape, (devices, depth)],
        ext,
        from_low,
        from_high,
        density,
        void_mask,
        solid_mask,
        scratch=[((rows + 2 * REACH) * (cols + 8), depth)],
    )
    target = VOLUME_SHARE * rows * cols * depth * devices
    volumes = [everyone(volume)]
    for step in (1, 2):
        (volume,) = call(
            functools.partial(trial_kernel, target, step, False), "trial", [(devices, depth)], *volumes, *terms
        )
        volumes.append(everyone(volume))
    (new_density,) = call(functools.partial(trial_kernel, target, 3, True), "update", [shape], *volumes, *terms)
    return new_density, displacement


def solution(mesh):
    placed = (P("gx", "gy", None),) * 5 + (P(None, "gx", "gy", None),)
    return jax.shard_map(
        shards,
        mesh=mesh,
        in_specs=placed,
        out_specs=(P("gx", "gy", None), P(None, "gx", "gy", None)),
        check_vma=False,
    )
```

```python
import functools
import math

import jax
import jax.numpy as jnp
import numpy as np
from jax import lax
from jax.experimental import pallas as pl
from jax.experimental.pallas import tpu as pltpu
from jax.sharding import PartitionSpec as P

E_MIN = 0.001
RHO_FLOOR = 0.001
MOVE_LIMIT = 0.2
VOLUME_SHARE = 0.4
BASIS = 4
HALO = BASIS
REACH = 2
AXES = ("gx", "gy")
VMEM_LIMIT = 40 * 1024 * 1024

POISSON = 0.3
LAME = POISSON / ((1.0 + POISSON) * (1.0 - 2.0 * POISSON))
SHEAR = 1.0 / (2.0 * (1.0 + POISSON))
NORMAL = 2.0 * SHEAR / 16.0
TRACE = LAME / 16.0
SHEAR_FIRST = SHEAR / 16.0
BEND = (LAME + 3.0 * SHEAR) / 48.0
BEND_MIX = LAME / 48.0
TWIST = SHEAR / 48.0
THIRD = (LAME + 4.0 * SHEAR) / 144.0
DIAGONAL = NORMAL + TRACE + 2.0 * SHEAR_FIRST + 2.0 * BEND + 2.0 * TWIST + THIRD
PAIRS = (("xdds", "zsdd"), ("ydds", "zdsd"), ("xdsd", "ysdd"))
TRIPLE = ("zdds", "ydsd", "xsdd")
CLASSES = [c + y + z for c in "xyz" for y in "sd" for z in "sd"]


def lane_index(shape):
    return lax.broadcasted_iota(jnp.int32, shape, len(shape) - 1)


def load_modes(z_ref, plane, begin, count):
    modes = {}
    for number, component in enumerate("xyz"):
        for index, z in enumerate("sd"):
            low = z_ref[number, index, plane, begin : begin + count, :]
            high = z_ref[number, index, plane, begin + 1 : begin + 1 + count, :]
            modes[component + "s" + z] = high + low
            modes[component + "d" + z] = high - low
    return modes


def element_modes(before, after):
    modes = {}
    for key in CLASSES:
        if key[1:] != "ss":
            modes[key[0] + "s" + key[1:]] = after[key] + before[key]
        modes[key[0] + "d" + key[1:]] = after[key] - before[key]
    return modes


def mode_forces(u, moduli):
    forces = {}
    normal = moduli * NORMAL
    trace = (u["xdss"] + u["ysds"] + u["zssd"]) * (TRACE / NORMAL)
    for key in ("xdss", "ysds", "zssd"):
        forces[key] = normal * (u[key] + trace)
    shear = moduli * SHEAR_FIRST
    for one, other in (("ydss", "xsds"), ("zsds", "yssd"), ("xssd", "zdss")):
        forces[one] = forces[other] = shear * (u[one] + u[other])
    bend = moduli * BEND
    for one, other in PAIRS:
        forces[one] = bend * (u[one] + (BEND_MIX / BEND) * u[other])
        forces[other] = bend * (u[other] + (BEND_MIX / BEND) * u[one])
    twist = moduli * TWIST
    total = u[TRIPLE[0]] + u[TRIPLE[1]] + u[TRIPLE[2]]
    for key in TRIPLE:
        forces[key] = twist * (total + u[key])
    third = moduli * THIRD
    for component in "xyz":
        forces[component + "ddd"] = third * u[component + "ddd"]
    return forces


def unit_energy(u):
    trace = u["xdss"] + u["ysds"] + u["zssd"]
    energy = TRACE * (trace * trace)
    energy += NORMAL * (u["xdss"] ** 2 + u["ysds"] ** 2 + u["zssd"] ** 2)
    shears = [u[a] + u[b] for a, b in (("ydss", "xsds"), ("zsds", "yssd"), ("xssd", "zdss"))]
    energy += SHEAR_FIRST * (shears[0] ** 2 + shears[1] ** 2 + shears[2] ** 2)
    squares, mixed = 0.0, 0.0
    for one, other in PAIRS:
        squares += u[one] ** 2 + u[other] ** 2
        mixed += (u[one] + u[other]) ** 2
    energy += (BEND - BEND_MIX) * squares + BEND_MIX * mixed
    total = u[TRIPLE[0]] + u[TRIPLE[1]] + u[TRIPLE[2]]
    squares = total * total
    for key in TRIPLE:
        squares += u[key] ** 2
    energy += TWIST * squares
    energy += THIRD * (u["xddd"] ** 2 + u["yddd"] ** 2 + u["zddd"] ** 2)
    return energy


def fields_kernel(shape, *refs):
    rows, cols, _ = shape
    sources, (own, rho_out, lower, upper, low, high) = refs[:6], refs[6:12]
    *local, arrived = refs[12:]
    copies = [pltpu.make_async_copy(s, t, arrived.at[i]) for i, (s, t) in enumerate(zip(sources, local))]
    for copy in copies:
        copy.start()
    for copy in copies:
        copy.wait()
    density, void, solid, fixed, load, traction = local
    is_solid, is_void = solid[...] == 1, void[...] == 1
    rho = jnp.where(is_solid, 1.0, jnp.where(is_void, RHO_FLOOR, density[...]))
    own[0] = E_MIN + rho * rho * rho * (1.0 - E_MIN)
    free = (1 - fixed[...]).astype(jnp.float32)
    own[1] = free
    loaded = free * load[...].astype(jnp.float32)
    for component in range(3):
        own[2 + component] = loaded * traction[component]
    for layer in range(HALO):
        for field in range(5):
            low[layer, field] = own[field, pl.ds(layer, rows, stride=cols), :]
            high[layer, field] = own[field, pl.ds(cols - HALO + layer, rows, stride=cols), :]
    rho_out[...] = rho
    least = jnp.maximum(RHO_FLOOR, rho - MOVE_LIMIT)
    most = jnp.minimum(1.0, rho + MOVE_LIMIT)
    lower[...] = jnp.where(is_solid, 1.0, jnp.where(is_void, RHO_FLOOR, least))
    upper[...] = jnp.where(is_solid, 1.0, jnp.where(is_void, RHO_FLOOR, most))


def widen_kernel(shape, own, from_low, from_high, ext, low, high):
    rows, cols, _ = shape
    wide = cols + 2 * HALO
    for field in range(5):
        for row in range(rows):
            ext[field, pl.ds(row * wide + HALO, cols), :] = own[field, pl.ds(row * cols, cols), :]
        for layer in range(HALO):
            ext[field, pl.ds(layer, rows, stride=wide), :] = from_low[layer, field]
            ext[field, pl.ds(wide - HALO + layer, rows, stride=wide), :] = from_high[layer, field]
        low[field] = ext[field, : HALO * wide, :]
        high[field] = ext[field, (rows - HALO) * wide :, :]


def basis_kernel(shape, ext, from_low, from_high, p_ref, sums_out, field_ref, inverse_ref, w_ref, z_ref, mode_ref, lift_ref, pipe_ref):
    rows, cols, depth = shape
    wide, long = cols + 2 * HALO, rows + 2 * HALO
    lanes = lane_index((wide, depth))
    keep_last = jnp.where(lanes < depth - 1, 1.0, 0.0)
    keep_first = jnp.where(lanes > 0, 1.0, 0.0)

    field_ref[:, :8, :] = jnp.zeros((long, 8, depth), jnp.float32)
    z_ref[:, :, :, wide:, :] = jnp.zeros((3, 2, long + 1, 8, depth), jnp.float32)

    def place(source, source_row, plane):
        field_ref[plane, 8:, :] = source[0, pl.ds(source_row, wide), :]
        inverse_ref[plane] = source[1, pl.ds(source_row, wide), :]
        for component in range(3):
            w_ref[0, component, plane] = source[2 + component, pl.ds(source_row, wide), :]

    for layer in range(HALO):
        place(from_low, layer * wide, layer)
        place(from_high, layer * wide, long - HALO + layer)
    for row in range(rows):
        place(ext, row * wide, row + HALO)

    def produce(level, plane):
        for component in range(3):
            value = p_ref[level, component, plane + 1]
            lifted = pltpu.roll(value, depth - 1, 1) * keep_last
            z_ref[component, 0, plane + 1, :wide] = lifted + value
            z_ref[component, 1, plane + 1, :wide] = lifted - value

    for plane in range(1, long):
        around = (
            field_ref[plane, 8:, :]
            + field_ref[plane - 1, 8:, :]
            + field_ref[plane, 7 : 7 + wide, :]
            + field_ref[plane - 1, 7 : 7 + wide, :]
        )
        around = around + pltpu.roll(around, 1, 1) * keep_first
        free = inverse_ref[plane]
        inverse = free / (free * (DIAGONAL * around) + (1.0 - free))
        inverse_ref[plane] = inverse
        for component in range(3):
            p_ref[0, component, plane + 1] = w_ref[0, component, plane] * inverse
    for plane in range(1, long):
        produce(0, plane)

    def finish(level, plane):
        for component in range(3):
            shifted = pltpu.roll(pipe_ref[component, 0], 1, 1) * keep_first
            residual = (pipe_ref[component, 1] + shifted) - w_ref[level, component, plane]
            w_ref[level + 1, component, plane] = residual
            p_ref[level + 1, component, plane + 1] = residual * inverse_ref[plane]

    for level in range(BASIS - 1):
        first, last = level + 1, long - 2 - level
        modes = load_modes(z_ref, first + 1, 0, wide)
        for index, key in enumerate(CLASSES):
            mode_ref[index] = modes[key]
            lift_ref[index] = jnp.zeros((wide, depth), jnp.float32)
        pipe_ref[...] = jnp.zeros(pipe_ref.shape, jnp.float32)

        def layer_step(step, carry):
            plane = first + step
            produce(level + 1, plane - 2)
            finish(level, plane - 1)
            after = load_modes(z_ref, plane + 2, 0, wide)
            before = {key: mode_ref[index] for index, key in enumerate(CLASSES)}
            lift = {key: lift_ref[index] for index, key in enumerate(CLASSES)}
            forces = mode_forces(element_modes(before, after), field_ref[plane, 8:, :])
            for number, component in enumerate("xyz"):
                along_z = {}
                for z in "sd":
                    along_y = {}
                    for y in "sd":
                        key = component + y + z
                        slope = forces[component + "d" + y + z]
                        if y + z == "ss":
                            along_y[y] = lift[key] - slope
                            lift[key] = slope
                        else:
                            mean = forces[component + "s" + y + z]
                            along_y[y] = lift[key] + (mean - slope)
                            lift[key] = mean + slope
                    along_z[z] = (along_y["s"] - along_y["d"]) + pltpu.roll(along_y["s"] + along_y["d"], 1, 0)
                pipe_ref[number, 0] = along_z["s"] + along_z["d"]
                pipe_ref[number, 1] = along_z["s"] - along_z["d"]
            for index, key in enumerate(CLASSES):
                mode_ref[index] = after[key]
                lift_ref[index] = lift[key]
            return carry

        lax.fori_loop(0, last + 1 - first, layer_step, 0)
        finish(level, last)
        produce(level + 1, last - 1)
        produce(level + 1, last)

    pairs = [(i, j) for i in range(BASIS) for j in range(i + 1)]
    modes = load_modes(z_ref, HALO + 1, HALO, cols)
    for index, key in enumerate(CLASSES):
        mode_ref[index, :cols] = modes[key]

    def dot_step(plane, totals):
        totals = list(totals)
        window = pl.ds(HALO, cols)
        for component in range(3):
            ps = [p_ref[level, component, plane + 1, window, :] for level in range(BASIS)]
            ws = [w_ref[level, component, plane, window, :] for level in range(BASIS)]
            for index, (i, j) in enumerate(pairs):
                totals[index] = totals[index] + ps[i] * ws[j]
        after = load_modes(z_ref, plane + 2, HALO, cols)
        before = {key: mode_ref[index, :cols] for index, key in enumerate(CLASSES)}
        for index, key in enumerate(CLASSES):
            mode_ref[index, :cols] = after[key]
        energy = unit_energy(element_modes(before, after))
        totals[-1] = totals[-1] + field_ref[plane, 8 + HALO : 8 + HALO + cols, :] * energy
        return tuple(totals)

    zeros = jnp.zeros((cols, depth), jnp.float32)
    totals = lax.fori_loop(HALO, HALO + rows, dot_step, (zeros,) * (len(pairs) + 1))
    slots = lane_index((1, 128))
    line = jnp.zeros((1, 128), jnp.float32)
    for index, total in enumerate(totals):
        share = jnp.sum(jnp.sum(total, axis=0, keepdims=True), axis=1, keepdims=True)
        line = line + jnp.where(slots == index, share, 0.0)
    sums_out[...] = jnp.broadcast_to(line, sums_out.shape)


def coefficients(shares):
    line = jnp.sum(shares, axis=0, keepdims=True)
    slots = lane_index(line.shape)

    def entry(index):
        return jnp.sum(jnp.where(slots == index, line, 0.0), axis=1, keepdims=True)

    inner = {}
    for index, (i, j) in enumerate([(i, j) for i in range(BASIS) for j in range(i + 1)]):
        inner[i, j] = inner[j, i] = entry(index)
    energy = {(BASIS - 1, BASIS - 1): entry(BASIS * (BASIS + 1) // 2)}
    for i in range(BASIS):
        for j in range(min(i + 1, BASIS - 1)):
            energy[i, j] = inner[i, j + 1] + inner[i, j]
    lower, pivot, inverse, solved = {}, {}, {}, {}
    for k in range(BASIS):
        left = energy[k, k]
        for m in range(k):
            left = left - lower[k, m] * lower[k, m] * pivot[m]
        sound = left > 1e-6 * energy[k, k]
        pivot[k] = jnp.where(sound, left, 0.0)
        inverse[k] = jnp.where(sound, 1.0 / jnp.where(sound, left, 1.0), 0.0)
        for i in range(k + 1, BASIS):
            part = energy[i, k]
            for m in range(k):
                part = part - lower[i, m] * lower[k, m] * pivot[m]
            lower[i, k] = part * inverse[k]
    for k in range(BASIS):
        part = inner[k, 0]
        for m in range(k):
            part = part - lower[k, m] * solved[m]
        solved[k] = part
    result = {}
    for k in reversed(range(BASIS)):
        part = solved[k] * inverse[k]
        for m in range(k + 1, BASIS):
            part = part - lower[m, k] * result[m]
        result[k] = part
    return [result[k] for k in range(BASIS)]


def energy_kernel(shape, shares, basis, rho_ref, displacement, weighted, low, high, u_ref, z_ref):
    rows, cols, depth = shape
    wide = cols + 2 * HALO
    keep_last = jnp.where(lane_index((wide, depth)) < depth - 1, 1.0, 0.0)
    parts = [jnp.broadcast_to(part, (wide, depth)) for part in coefficients(shares[...])]
    for row in range(rows + 1):
        for component in range(3):
            total = parts[0] * basis[0, component, row + HALO + 1]
            for level in range(1, BASIS):
                total = total + parts[level] * basis[level, component, row + HALO + 1]
            u_ref[component, row] = total
            lifted = pltpu.roll(total, depth - 1, 1) * keep_last
            z_ref[component, 0, row] = lifted + total
            z_ref[component, 1, row] = lifted - total
            if row < rows:
                displacement[component, row] = u_ref[component, row, HALO : HALO + cols, :]
    before = load_modes(z_ref, 0, HALO, cols)
    for row in range(rows):
        after = load_modes(z_ref, row + 1, HALO, cols)
        energy = unit_energy(element_modes(before, after))
        before = after
        rho = rho_ref[row * cols : (row + 1) * cols, :]
        weighted[row * cols : (row + 1) * cols, :] = rho * (3.0 * rho * rho * (1.0 - E_MIN) * energy)
    for layer in range(REACH):
        low[layer] = weighted[pl.ds(layer, rows, stride=cols), :]
        high[layer] = weighted[pl.ds(cols - REACH + layer, rows, stride=cols), :]


def stretch_kernel(shape, own, from_low, from_high, ext, low, high):
    rows, cols, _ = shape
    wide = cols + 8
    for row in range(rows):
        ext[pl.ds(row * wide + REACH, cols), :] = own[pl.ds(row * cols, cols), :]
    for layer in range(REACH):
        ext[pl.ds(layer, rows, stride=wide), :] = from_low[layer]
        ext[pl.ds(REACH + cols + layer, rows, stride=wide), :] = from_high[layer]
    for layer in range(2 * REACH, 8):
        ext[pl.ds(cols + layer, rows, stride=wide), :] = jnp.zeros_like(from_low[0])
    low[...] = ext[: REACH * wide, :]
    high[...] = ext[(rows - REACH) * wide :, :]


def cone_table():
    table, total = {}, 0.0
    for a in range(-2, 3):
        for b in range(-2, 3):
            for c in range(-2, 3):
                total += max(0.0, 3.0 - math.sqrt(a * a + b * b + c * c))
    for flat in (0, 1, 2, 4, 5, 8):
        for c in range(3):
            table[flat, c] = max(0.0, 3.0 - math.sqrt(flat + c * c))
    return table, total


def volume_row(total):
    return jnp.sum(total, axis=0, keepdims=True)


def filter_kernel(shape, ext, from_low, from_high, rho_ref, lower, upper, root, volume, plane_ref):
    rows, cols, depth = shape
    wide = cols + 8
    table, total = cone_table()
    plane_ref[: REACH * wide, :] = from_low[...]
    plane_ref[REACH * wide : (rows + REACH) * wide, :] = ext[...]
    plane_ref[(rows + REACH) * wide :, :] = from_high[...]
    volume_sum = jnp.zeros((cols, depth), jnp.float32)
    for row in range(rows):
        spread = {}
        for a in range(-REACH, REACH + 1):
            for b in range(-REACH, REACH + 1):
                key = a * a + b * b
                value = plane_ref[pl.ds((row + REACH + a) * wide + REACH + b, cols), :]
                spread[key] = value if key not in spread else spread[key] + value
        sums = []
        for c in range(3):
            part = None
            for key, value in spread.items():
                if table[key, c] > 0.0:
                    term = table[key, c] * value
                    part = term if part is None else part + term
            sums.append(part)
        convolved = sums[0]
        for c in (1, 2):
            convolved = convolved + (pltpu.roll(sums[c], c, 1) + pltpu.roll(sums[c], depth - c, 1))
        window = slice(row * cols, (row + 1) * cols)
        rho = rho_ref[window, :]
        base = rho * jnp.sqrt(convolved / (total * rho))
        root[window, :] = base
        volume_sum = volume_sum + jnp.minimum(jnp.maximum(base, lower[window, :]), upper[window, :])
    volume[...] = jnp.broadcast_to(volume_row(volume_sum), volume.shape)


def scale_of(target, volumes):
    scale = None
    for volume in volumes:
        whole = jnp.sum(jnp.sum(volume[...], axis=0, keepdims=True), axis=1, keepdims=True)
        ratio = target / whole
        scale = ratio if scale is None else scale * ratio
    return scale


def trial_kernel(target, steps, final, *refs):
    volumes, (root, lower, upper, out) = refs[:steps], refs[steps:]
    scale = scale_of(target, volumes)
    moved = jnp.minimum(jnp.maximum(root[...] * scale, lower[...]), upper[...])
    if final:
        out[...] = moved
    else:
        out[...] = jnp.broadcast_to(volume_row(moved), out.shape)


def call(kernel, name, out_shapes, *args, scratch=(), flops=0, space=pltpu.VMEM):
    shapes = [jax.ShapeDtypeStruct(shape, jnp.float32) for shape in out_shapes]
    moved = sum(4 * math.prod(value.shape) for value in [*args, *shapes])
    return pl.pallas_call(
        kernel,
        name=name,
        out_shape=shapes,
        in_specs=[pl.BlockSpec(memory_space=space)] * len(args),
        out_specs=[pl.BlockSpec(memory_space=pltpu.VMEM)] * len(shapes),
        scratch_shapes=[pltpu.VMEM(item, jnp.float32) if isinstance(item, tuple) else item for item in scratch],
        compiler_params=pltpu.CompilerParams(vmem_limit_bytes=VMEM_LIMIT),
        cost_estimate=pl.CostEstimate(flops=flops, bytes_accessed=moved, transcendentals=0),
    )(*args)


def exchange(low, high, axis, wrap):
    count = lax.axis_size(axis)
    ends = count if wrap else count - 1
    from_low = lax.ppermute(high, axis, [(i, (i + 1) % count) for i in range(ends)])
    from_high = lax.ppermute(low, axis, [((i + 1) % count, i) for i in range(ends)])
    return from_low, from_high


def everyone(shares):
    return lax.all_to_all(shares, AXES, 0, 0, tiled=True)


def shards(density, void_mask, solid_mask, fixed_mask, load_mask, traction):
    shape = rows, cols, depth = density.shape
    devices = lax.axis_size("gx") * lax.axis_size("gy")
    wide, long = cols + 2 * HALO, rows + 2 * HALO
    named = lambda kernel: functools.partial(kernel, shape)
    flat = (rows * cols, depth)
    inputs = [
        value.reshape(*value.shape[:-3], *flat)
        for value in (density, void_mask, solid_mask, fixed_mask, load_mask, traction)
    ]

    own, rho, lower, upper, low, high = call(
        named(fields_kernel),
        "fields",
        [(5, *flat), flat, flat, flat, (HALO, 5, rows, depth), (HALO, 5, rows, depth)],
        *inputs,
        scratch=[pltpu.VMEM(value.shape, value.dtype) for value in inputs] + [pltpu.SemaphoreType.DMA((6,))],
        space=pltpu.HBM,
    )
    from_low, from_high = exchange(low, high, "gy", False)
    ext, low, high = call(
        named(widen_kernel),
        "widen",
        [(5, rows * wide, depth), (5, HALO * wide, depth), (5, HALO * wide, depth)],
        own,
        from_low,
        from_high,
    )
    from_low, from_high = exchange(low, high, "gx", False)
    basis, sums = call(
        named(basis_kernel),
        "basis",
        [(BASIS, 3, long + 1, wide, depth), (devices, 128)],
        ext,
        from_low,
        from_high,
        scratch=[
            (long, 8 + wide, depth),
            (long, wide, depth),
            (BASIS, 3, long, wide, depth),
            (3, 2, long + 1, wide + 8, depth),
            (12, wide, depth),
            (12, wide, depth),
            (3, 2, wide, depth),
        ],
    )
    displacement, weighted, low, high = call(
        named(energy_kernel),
        "energy",
        [(3, rows, cols, depth), flat, (REACH, rows, depth), (REACH, rows, depth)],
        everyone(sums),
        basis,
        rho,
        scratch=[(3, rows + 1, wide, depth), (3, 2, rows + 1, wide, depth)],
    )
    from_low, from_high = exchange(low, high, "gy", True)
    ext, low, high = call(
        named(stretch_kernel),
        "stretch",
        [(rows * (cols + 8), depth), (REACH * (cols + 8), depth), (REACH * (cols + 8), depth)],
        weighted,
        from_low,
        from_high,
    )
    from_low, from_high = exchange(low, high, "gx", True)
    root, volume = call(
        named(filter_kernel),
        "filter",
        [flat, (devices, depth)],
        ext,
        from_low,
        from_high,
        rho,
        lower,
        upper,
        scratch=[((rows + 2 * REACH) * (cols + 8), depth)],
    )
    target = VOLUME_SHARE * rows * cols * depth * devices
    terms, volumes = (root, lower, upper), [everyone(volume)]
    for step in (1, 2):
        (volume,) = call(
            functools.partial(trial_kernel, target, step, False), "trial", [(devices, depth)], *volumes, *terms
        )
        volumes.append(everyone(volume))
    (new_density,) = call(functools.partial(trial_kernel, target, 3, True), "update", [flat], *volumes, *terms)
    return new_density.reshape(shape), displacement


def solution(mesh):
    placed = (P("gx", "gy", None),) * 5 + (P(None, "gx", "gy", None),)
    return jax.shard_map(
        shards,
        mesh=mesh,
        in_specs=placed,
        out_specs=(P("gx", "gy", None), P(None, "gx", "gy", None)),
        check_vma=False,
    )
```

```python
import functools
import math

import jax
import jax.numpy as jnp
import numpy as np
from jax import lax
from jax.experimental import pallas as pl
from jax.experimental.pallas import tpu as pltpu
from jax.sharding import PartitionSpec as P

E_MIN = 0.001
RHO_FLOOR = 0.001
MOVE_LIMIT = 0.2
VOLUME_SHARE = 0.4
BASIS = 4
REACH = 2
HALO = BASIS
HALO_X = BASIS + REACH
AXES = ("gx", "gy")
VMEM_LIMIT = 40 * 1024 * 1024

POISSON = 0.3
LAME = POISSON / ((1.0 + POISSON) * (1.0 - 2.0 * POISSON))
SHEAR = 1.0 / (2.0 * (1.0 + POISSON))
NORMAL = 2.0 * SHEAR / 16.0
TRACE = LAME / 16.0
SHEAR_FIRST = SHEAR / 16.0
BEND = (LAME + 3.0 * SHEAR) / 48.0
BEND_MIX = LAME / 48.0
TWIST = SHEAR / 48.0
THIRD = (LAME + 4.0 * SHEAR) / 144.0
DIAGONAL = NORMAL + TRACE + 2.0 * SHEAR_FIRST + 2.0 * BEND + 2.0 * TWIST + THIRD
PAIRS = (("xdds", "zsdd"), ("ydds", "zdsd"), ("xdsd", "ysdd"))
TRIPLE = ("zdds", "ydsd", "xsdd")
CLASSES = [c + y + z for c in "xyz" for y in "sd" for z in "sd"]


def lane_index(shape):
    return lax.broadcasted_iota(jnp.int32, shape, len(shape) - 1)


def load_modes(z_ref, plane, begin, count):
    modes = {}
    for number, component in enumerate("xyz"):
        for index, z in enumerate("sd"):
            low = z_ref[number, index, plane, begin : begin + count, :]
            high = z_ref[number, index, plane, begin + 1 : begin + 1 + count, :]
            modes[component + "s" + z] = high + low
            modes[component + "d" + z] = high - low
    return modes


def element_modes(before, after):
    modes = {}
    for key in CLASSES:
        if key[1:] != "ss":
            modes[key[0] + "s" + key[1:]] = after[key] + before[key]
        modes[key[0] + "d" + key[1:]] = after[key] - before[key]
    return modes


def mode_forces(u, moduli):
    forces = {}
    normal = moduli * NORMAL
    trace = (u["xdss"] + u["ysds"] + u["zssd"]) * (TRACE / NORMAL)
    for key in ("xdss", "ysds", "zssd"):
        forces[key] = normal * (u[key] + trace)
    shear = moduli * SHEAR_FIRST
    for one, other in (("ydss", "xsds"), ("zsds", "yssd"), ("xssd", "zdss")):
        forces[one] = forces[other] = shear * (u[one] + u[other])
    bend = moduli * BEND
    for one, other in PAIRS:
        forces[one] = bend * (u[one] + (BEND_MIX / BEND) * u[other])
        forces[other] = bend * (u[other] + (BEND_MIX / BEND) * u[one])
    twist = moduli * TWIST
    total = u[TRIPLE[0]] + u[TRIPLE[1]] + u[TRIPLE[2]]
    for key in TRIPLE:
        forces[key] = twist * (total + u[key])
    third = moduli * THIRD
    for component in "xyz":
        forces[component + "ddd"] = third * u[component + "ddd"]
    return forces


def unit_energy(u):
    trace = u["xdss"] + u["ysds"] + u["zssd"]
    energy = TRACE * (trace * trace)
    energy += NORMAL * (u["xdss"] ** 2 + u["ysds"] ** 2 + u["zssd"] ** 2)
    shears = [u[a] + u[b] for a, b in (("ydss", "xsds"), ("zsds", "yssd"), ("xssd", "zdss"))]
    energy += SHEAR_FIRST * (shears[0] ** 2 + shears[1] ** 2 + shears[2] ** 2)
    squares, mixed = 0.0, 0.0
    for one, other in PAIRS:
        squares += u[one] ** 2 + u[other] ** 2
        mixed += (u[one] + u[other]) ** 2
    energy += (BEND - BEND_MIX) * squares + BEND_MIX * mixed
    total = u[TRIPLE[0]] + u[TRIPLE[1]] + u[TRIPLE[2]]
    squares = total * total
    for key in TRIPLE:
        squares += u[key] ** 2
    energy += TWIST * squares
    energy += THIRD * (u["xddd"] ** 2 + u["yddd"] ** 2 + u["zddd"] ** 2)
    return energy


def fields_kernel(shape, *refs):
    rows, cols, _ = shape
    sources, (own, lower, upper, low, high) = refs[:6], refs[6:11]
    *local, arrived = refs[11:]
    copies = [pltpu.make_async_copy(s, t, arrived.at[i]) for i, (s, t) in enumerate(zip(sources, local))]
    for copy in copies:
        copy.start()
    for copy in copies:
        copy.wait()
    density, void, solid, fixed, load, traction = local
    is_solid, is_void = solid[...] == 1, void[...] == 1
    rho = jnp.where(is_solid, 1.0, jnp.where(is_void, RHO_FLOOR, density[...]))
    own[0] = rho
    free = (1 - fixed[...]).astype(jnp.float32)
    own[1] = free
    loaded = free * load[...].astype(jnp.float32)
    for component in range(3):
        own[2 + component] = loaded * traction[component]
    for layer in range(HALO):
        for field in range(5):
            low[layer, field] = own[field, pl.ds(layer, rows, stride=cols), :]
            high[layer, field] = own[field, pl.ds(cols - HALO + layer, rows, stride=cols), :]
    least = jnp.maximum(RHO_FLOOR, rho - MOVE_LIMIT)
    most = jnp.minimum(1.0, rho + MOVE_LIMIT)
    lower[...] = jnp.where(is_solid, 1.0, jnp.where(is_void, RHO_FLOOR, least))
    upper[...] = jnp.where(is_solid, 1.0, jnp.where(is_void, RHO_FLOOR, most))


def widen_kernel(shape, own, from_low, from_high, ext, low, high):
    rows, cols, _ = shape
    wide = cols + 2 * HALO
    for field in range(5):
        for row in range(rows):
            ext[field, pl.ds(row * wide + HALO, cols), :] = own[field, pl.ds(row * cols, cols), :]
        for layer in range(HALO):
            ext[field, pl.ds(layer, rows, stride=wide), :] = from_low[layer, field]
            ext[field, pl.ds(wide - HALO + layer, rows, stride=wide), :] = from_high[layer, field]
        low[field] = ext[field, : HALO_X * wide, :]
        high[field] = ext[field, (rows - HALO_X) * wide :, :]


def grid_cuts(rows):
    place, last = lax.axis_index("gx"), lax.axis_size("gx") - 1
    return {
        HALO_X - 1: jnp.where(place == 0, 0.0, 1.0),
        HALO_X + rows - 1: jnp.where(place == last, 0.0, 1.0),
    }


def cut_off(values, keep):
    return values if keep is None else {key: value * keep for key, value in values.items()}


def basis_kernel(shape, ext, from_low, from_high, p_ref, sums_out, field_ref, inverse_ref, w_ref, z_ref, mode_ref, lift_ref, pipe_ref):
    rows, cols, depth = shape
    wide, long = cols + 2 * HALO, rows + 2 * HALO_X
    lanes = lane_index((wide, depth))
    keep_last = jnp.where(lanes < depth - 1, 1.0, 0.0)
    keep_first = jnp.where(lanes > 0, 1.0, 0.0)

    field_ref[:, :8, :] = jnp.zeros((long, 8, depth), jnp.float32)
    z_ref[:, :, :, wide:, :] = jnp.zeros((3, 2, long + 1, 8, depth), jnp.float32)

    def place(source, source_row, plane):
        rho = source[0, pl.ds(source_row, wide), :]
        field_ref[plane, 8:, :] = jnp.where(rho > 0.0, E_MIN + rho * rho * rho * (1.0 - E_MIN), 0.0)
        inverse_ref[plane] = source[1, pl.ds(source_row, wide), :]
        for component in range(3):
            w_ref[0, component, plane] = source[2 + component, pl.ds(source_row, wide), :]

    for layer in range(HALO_X):
        place(from_low, layer * wide, layer)
        place(from_high, layer * wide, long - HALO_X + layer)
    for row in range(rows):
        place(ext, row * wide, row + HALO_X)
    cuts = grid_cuts(rows)

    def produce(level, plane):
        for component in range(3):
            value = p_ref[level, component, plane + 1]
            lifted = pltpu.roll(value, depth - 1, 1) * keep_last
            z_ref[component, 0, plane + 1, :wide] = lifted + value
            z_ref[component, 1, plane + 1, :wide] = lifted - value

    for plane in range(1, long):
        around = field_ref[plane - 1, 8:, :] + field_ref[plane - 1, 7 : 7 + wide, :]
        if plane - 1 in cuts:
            around = around * cuts[plane - 1]
        around = around + (field_ref[plane, 8:, :] + field_ref[plane, 7 : 7 + wide, :])
        around = around + pltpu.roll(around, 1, 1) * keep_first
        free = inverse_ref[plane]
        inverse = free / (free * (DIAGONAL * around) + (1.0 - free))
        inverse_ref[plane] = inverse
        for component in range(3):
            p_ref[0, component, plane + 1] = w_ref[0, component, plane] * inverse
    for plane in range(1, long):
        produce(0, plane)

    def finish(level, plane):
        for component in range(3):
            shifted = pltpu.roll(pipe_ref[component, 0], 1, 1) * keep_first
            residual = (pipe_ref[component, 1] + shifted) - w_ref[level, component, plane]
            w_ref[level + 1, component, plane] = residual
            p_ref[level + 1, component, plane + 1] = residual * inverse_ref[plane]

    for level in range(BASIS - 1):
        first, last = level + 1, long - 2 - level
        modes = load_modes(z_ref, first + 1, 0, wide)
        for index, key in enumerate(CLASSES):
            mode_ref[index] = modes[key]
            lift_ref[index] = jnp.zeros((wide, depth), jnp.float32)
        pipe_ref[...] = jnp.zeros(pipe_ref.shape, jnp.float32)

        def layer_step(plane, carry, keep=None):
            produce(level + 1, plane - 2)
            finish(level, plane - 1)
            after = load_modes(z_ref, plane + 2, 0, wide)
            before = {key: mode_ref[index] for index, key in enumerate(CLASSES)}
            lift = {key: lift_ref[index] for index, key in enumerate(CLASSES)}
            forces = mode_forces(element_modes(before, cut_off(after, keep)), field_ref[plane, 8:, :])
            for number, component in enumerate("xyz"):
                along_z = {}
                for z in "sd":
                    along_y = {}
                    for y in "sd":
                        key = component + y + z
                        slope = forces[component + "d" + y + z]
                        if y + z == "ss":
                            along_y[y] = lift[key] - slope
                            lift[key] = slope
                        else:
                            mean = forces[component + "s" + y + z]
                            along_y[y] = lift[key] + (mean - slope)
                            lift[key] = mean + slope
                    along_z[z] = (along_y["s"] - along_y["d"]) + pltpu.roll(along_y["s"] + along_y["d"], 1, 0)
                pipe_ref[number, 0] = along_z["s"] + along_z["d"]
                pipe_ref[number, 1] = along_z["s"] - along_z["d"]
            lift = cut_off(lift, keep)
            for index, key in enumerate(CLASSES):
                mode_ref[index] = after[key]
                lift_ref[index] = lift[key]
            return carry

        begin = first
        for plane, keep in cuts.items():
            lax.fori_loop(begin, plane, layer_step, 0)
            layer_step(plane, 0, keep)
            begin = plane + 1
        lax.fori_loop(begin, last + 1, layer_step, 0)
        finish(level, last)
        produce(level + 1, last - 1)
        produce(level + 1, last)

    pairs = [(i, j) for i in range(BASIS) for j in range(i + 1)]
    modes = load_modes(z_ref, HALO_X + 1, HALO, cols)
    for index, key in enumerate(CLASSES):
        mode_ref[index, :cols] = modes[key]

    def dot_step(plane, totals, keep=None):
        totals = list(totals)
        window = pl.ds(HALO, cols)
        for component in range(3):
            ps = [p_ref[level, component, plane + 1, window, :] for level in range(BASIS)]
            ws = [w_ref[level, component, plane, window, :] for level in range(BASIS)]
            for index, (i, j) in enumerate(pairs):
                totals[index] = totals[index] + ps[i] * ws[j]
        after = load_modes(z_ref, plane + 2, HALO, cols)
        before = {key: mode_ref[index, :cols] for index, key in enumerate(CLASSES)}
        for index, key in enumerate(CLASSES):
            mode_ref[index, :cols] = after[key]
        energy = unit_energy(element_modes(before, cut_off(after, keep)))
        totals[-1] = totals[-1] + field_ref[plane, 8 + HALO : 8 + HALO + cols, :] * energy
        return tuple(totals)

    zeros = jnp.zeros((cols, depth), jnp.float32)
    outer = HALO_X + rows - 1
    totals = lax.fori_loop(HALO_X, outer, dot_step, (zeros,) * (len(pairs) + 1))
    totals = dot_step(outer, totals, cuts[outer])
    slots = lane_index((1, 128))
    line = jnp.zeros((1, 128), jnp.float32)
    for index, total in enumerate(totals):
        share = jnp.sum(jnp.sum(total, axis=0, keepdims=True), axis=1, keepdims=True)
        line = line + jnp.where(slots == index, share, 0.0)
    sums_out[...] = jnp.broadcast_to(line, sums_out.shape)


def coefficients(shares):
    line = jnp.sum(shares, axis=0, keepdims=True)
    slots = lane_index(line.shape)

    def entry(index):
        return jnp.sum(jnp.where(slots == index, line, 0.0), axis=1, keepdims=True)

    inner = {}
    for index, (i, j) in enumerate([(i, j) for i in range(BASIS) for j in range(i + 1)]):
        inner[i, j] = inner[j, i] = entry(index)
    energy = {(BASIS - 1, BASIS - 1): entry(BASIS * (BASIS + 1) // 2)}
    for i in range(BASIS):
        for j in range(min(i + 1, BASIS - 1)):
            energy[i, j] = inner[i, j + 1] + inner[i, j]
    lower, pivot, inverse, solved = {}, {}, {}, {}
    for k in range(BASIS):
        left = energy[k, k]
        for m in range(k):
            left = left - lower[k, m] * lower[k, m] * pivot[m]
        sound = left > 1e-6 * energy[k, k]
        pivot[k] = jnp.where(sound, left, 0.0)
        inverse[k] = jnp.where(sound, 1.0 / jnp.where(sound, left, 1.0), 0.0)
        for i in range(k + 1, BASIS):
            part = energy[i, k]
            for m in range(k):
                part = part - lower[i, m] * lower[k, m] * pivot[m]
            lower[i, k] = part * inverse[k]
    for k in range(BASIS):
        part = inner[k, 0]
        for m in range(k):
            part = part - lower[k, m] * solved[m]
        solved[k] = part
    result = {}
    for k in reversed(range(BASIS)):
        part = solved[k] * inverse[k]
        for m in range(k + 1, BASIS):
            part = part - lower[m, k] * result[m]
        result[k] = part
    return [result[k] for k in range(BASIS)]


def energy_kernel(
    shape, shares, basis, own, from_low, from_high, displacement, weighted, low, high, u_ref, z_ref
):
    rows, cols, depth = shape
    wide, planes = cols + 2 * HALO, rows + 2 * REACH
    keep_last = jnp.where(lane_index((wide, depth)) < depth - 1, 1.0, 0.0)
    parts = [jnp.broadcast_to(part, (wide, depth)) for part in coefficients(shares[...])]
    cuts = grid_cuts(rows)
    for plane in range(planes + 1):
        source = plane + HALO_X - REACH + 1
        for component in range(3):
            total = parts[0] * basis[0, component, source]
            for level in range(1, BASIS):
                total = total + parts[level] * basis[level, component, source]
            lifted = pltpu.roll(total, depth - 1, 1) * keep_last
            z_ref[component, 0, plane] = lifted + total
            z_ref[component, 1, plane] = lifted - total
            row = plane - REACH
            if 0 <= row < rows:
                u_ref[component, row] = total
                displacement[component, row] = u_ref[component, row, HALO : HALO + cols, :]
    before = load_modes(z_ref, 0, HALO, cols)
    for plane in range(planes):
        row = plane - REACH
        after = load_modes(z_ref, plane + 1, HALO, cols)
        energy = unit_energy(element_modes(before, cut_off(after, cuts.get(row + HALO_X))))
        before = after
        if row < 0:
            rho = from_low[0, (row + HALO_X) * wide + HALO : (row + HALO_X) * wide + HALO + cols, :]
        elif row < rows:
            rho = own[0, row * cols : (row + 1) * cols, :]
        else:
            rho = from_high[0, (row - rows) * wide + HALO : (row - rows) * wide + HALO + cols, :]
        weighted[plane * cols : (plane + 1) * cols, :] = rho * (3.0 * rho * rho * (1.0 - E_MIN) * energy)
    for layer in range(REACH):
        low[layer] = weighted[pl.ds(layer, planes, stride=cols), :]
        high[layer] = weighted[pl.ds(cols - REACH + layer, planes, stride=cols), :]


def cone_table():
    table, total = {}, 0.0
    for a in range(-2, 3):
        for b in range(-2, 3):
            for c in range(-2, 3):
                total += max(0.0, 3.0 - math.sqrt(a * a + b * b + c * c))
    for flat in (0, 1, 2, 4, 5, 8):
        for c in range(3):
            table[flat, c] = max(0.0, 3.0 - math.sqrt(flat + c * c))
    return table, total


def volume_row(total):
    return jnp.sum(total, axis=0, keepdims=True)


def filter_kernel(shape, weighted, from_low, from_high, own, lower, upper, root, volume, plane_ref):
    rows, cols, depth = shape
    wide, planes = cols + 8, rows + 2 * REACH
    table, total = cone_table()
    for plane in range(planes):
        plane_ref[plane * wide + REACH : plane * wide + REACH + cols, :] = weighted[plane * cols : (plane + 1) * cols, :]
    for layer in range(REACH):
        plane_ref[pl.ds(layer, planes, stride=wide), :] = from_low[layer]
        plane_ref[pl.ds(REACH + cols + layer, planes, stride=wide), :] = from_high[layer]
    volume_sum = jnp.zeros((cols, depth), jnp.float32)
    for row in range(rows):
        spread = {}
        for a in range(-REACH, REACH + 1):
            for b in range(-REACH, REACH + 1):
                key = a * a + b * b
                value = plane_ref[pl.ds((row + REACH + a) * wide + REACH + b, cols), :]
                spread[key] = value if key not in spread else spread[key] + value
        sums = []
        for c in range(3):
            part = None
            for key, value in spread.items():
                if table[key, c] > 0.0:
                    term = table[key, c] * value
                    part = term if part is None else part + term
            sums.append(part)
        convolved = sums[0]
        for c in (1, 2):
            convolved = convolved + (pltpu.roll(sums[c], c, 1) + pltpu.roll(sums[c], depth - c, 1))
        window = slice(row * cols, (row + 1) * cols)
        rho = own[0, window, :]
        base = rho * jnp.sqrt(convolved / (total * rho))
        root[window, :] = base
        volume_sum = volume_sum + jnp.minimum(jnp.maximum(base, lower[window, :]), upper[window, :])
    volume[...] = jnp.broadcast_to(volume_row(volume_sum), volume.shape)


def scale_of(target, volumes):
    scale = None
    for volume in volumes:
        whole = jnp.sum(jnp.sum(volume[...], axis=0, keepdims=True), axis=1, keepdims=True)
        ratio = target / whole
        scale = ratio if scale is None else scale * ratio
    return scale


def trial_kernel(target, steps, final, *refs):
    volumes, (root, lower, upper, out) = refs[:steps], refs[steps:]
    scale = scale_of(target, volumes)
    moved = jnp.minimum(jnp.maximum(root[...] * scale, lower[...]), upper[...])
    if final:
        out[...] = moved
    else:
        out[...] = jnp.broadcast_to(volume_row(moved), out.shape)


def call(kernel, name, out_shapes, *args, scratch=(), flops=0, space=pltpu.VMEM):
    shapes = [jax.ShapeDtypeStruct(shape, jnp.float32) for shape in out_shapes]
    moved = sum(4 * math.prod(value.shape) for value in [*args, *shapes])
    return pl.pallas_call(
        kernel,
        name=name,
        out_shape=shapes,
        in_specs=[pl.BlockSpec(memory_space=space)] * len(args),
        out_specs=[pl.BlockSpec(memory_space=pltpu.VMEM)] * len(shapes),
        scratch_shapes=[pltpu.VMEM(item, jnp.float32) if isinstance(item, tuple) else item for item in scratch],
        compiler_params=pltpu.CompilerParams(vmem_limit_bytes=VMEM_LIMIT),
        cost_estimate=pl.CostEstimate(flops=flops, bytes_accessed=moved, transcendentals=0),
    )(*args)


def exchange(low, high, axis, wrap):
    count = lax.axis_size(axis)
    ends = count if wrap else count - 1
    from_low = lax.ppermute(high, axis, [(i, (i + 1) % count) for i in range(ends)])
    from_high = lax.ppermute(low, axis, [((i + 1) % count, i) for i in range(ends)])
    return from_low, from_high


def everyone(shares):
    return lax.all_to_all(shares, AXES, 0, 0, tiled=True)


def shards(density, void_mask, solid_mask, fixed_mask, load_mask, traction):
    shape = rows, cols, depth = density.shape
    devices = lax.axis_size("gx") * lax.axis_size("gy")
    wide, long = cols + 2 * HALO, rows + 2 * HALO_X
    planes = rows + 2 * REACH
    named = lambda kernel: functools.partial(kernel, shape)
    flat = (rows * cols, depth)
    inputs = [
        pltpu.with_memory_space_constraint(value.reshape(*value.shape[:-3], *flat), pltpu.HBM)
        for value in (density, void_mask, solid_mask, fixed_mask, load_mask, traction)
    ]

    own, lower, upper, low, high = call(
        named(fields_kernel),
        "fields",
        [(5, *flat), flat, flat, (HALO, 5, rows, depth), (HALO, 5, rows, depth)],
        *inputs,
        scratch=[pltpu.VMEM(value.shape, value.dtype) for value in inputs] + [pltpu.SemaphoreType.DMA((6,))],
        space=pltpu.HBM,
    )
    from_low, from_high = exchange(low, high, "gy", False)
    ext, low, high = call(
        named(widen_kernel),
        "widen",
        [(5, rows * wide, depth), (5, HALO_X * wide, depth), (5, HALO_X * wide, depth)],
        own,
        from_low,
        from_high,
    )
    from_low, from_high = exchange(low, high, "gx", True)
    basis, sums = call(
        named(basis_kernel),
        "basis",
        [(BASIS, 3, long + 1, wide, depth), (devices, 128)],
        ext,
        from_low,
        from_high,
        scratch=[
            (long, 8 + wide, depth),
            (long, wide, depth),
            (BASIS, 3, long, wide, depth),
            (3, 2, long + 1, wide + 8, depth),
            (12, wide, depth),
            (12, wide, depth),
            (3, 2, wide, depth),
        ],
    )
    displacement, weighted, low, high = call(
        named(energy_kernel),
        "energy",
        [(3, rows, cols, depth), (planes * cols, depth), (REACH, planes, depth), (REACH, planes, depth)],
        everyone(sums),
        basis,
        own,
        from_low,
        from_high,
        scratch=[(3, rows, wide, depth), (3, 2, planes + 1, wide, depth)],
    )
    from_low, from_high = exchange(low, high, "gy", True)
    root, volume = call(
        named(filter_kernel),
        "filter",
        [flat, (devices, depth)],
        weighted,
        from_low,
        from_high,
        own,
        lower,
        upper,
        scratch=[(planes * (cols + 8), depth)],
    )
    target = VOLUME_SHARE * rows * cols * depth * devices
    terms, volumes = (root, lower, upper), [everyone(volume)]
    for step in (1, 2):
        (volume,) = call(
            functools.partial(trial_kernel, target, step, False), "trial", [(devices, depth)], *volumes, *terms
        )
        volumes.append(everyone(volume))
    (new_density,) = call(functools.partial(trial_kernel, target, 3, True), "update", [flat], *volumes, *terms)
    return new_density.reshape(shape), displacement


def solution(mesh):
    placed = (P("gx", "gy", None),) * 5 + (P(None, "gx", "gy", None),)
    return jax.shard_map(
        shards,
        mesh=mesh,
        in_specs=placed,
        out_specs=(P("gx", "gy", None), P(None, "gx", "gy", None)),
        check_vma=False,
    )
```

```python
import functools
import math

import jax
import jax.numpy as jnp
import numpy as np
from jax import lax
from jax.experimental import pallas as pl
from jax.experimental.pallas import tpu as pltpu
from jax.sharding import PartitionSpec as P

E_MIN = 0.001
RHO_FLOOR = 0.001
MOVE_LIMIT = 0.2
VOLUME_SHARE = 0.4
BASIS = 4
REACH = 2
HALO = BASIS
HALO_X = BASIS + REACH
AXES = ("gx", "gy")
VMEM_LIMIT = 40 * 1024 * 1024

POISSON = 0.3
LAME = POISSON / ((1.0 + POISSON) * (1.0 - 2.0 * POISSON))
SHEAR = 1.0 / (2.0 * (1.0 + POISSON))
NORMAL = 2.0 * SHEAR / 16.0
TRACE = LAME / 16.0
SHEAR_FIRST = SHEAR / 16.0
BEND = (LAME + 3.0 * SHEAR) / 48.0
BEND_MIX = LAME / 48.0
TWIST = SHEAR / 48.0
THIRD = (LAME + 4.0 * SHEAR) / 144.0
DIAGONAL = NORMAL + TRACE + 2.0 * SHEAR_FIRST + 2.0 * BEND + 2.0 * TWIST + THIRD
PAIRS = (("xdds", "zsdd"), ("ydds", "zdsd"), ("xdsd", "ysdd"))
TRIPLE = ("zdds", "ydsd", "xsdd")
CLASSES = [c + y + z for c in "xyz" for y in "sd" for z in "sd"]


def lane_index(shape):
    return lax.broadcasted_iota(jnp.int32, shape, len(shape) - 1)


def load_modes(z_ref, plane, begin, count):
    modes = {}
    for number, component in enumerate("xyz"):
        for index, z in enumerate("sd"):
            low = z_ref[number, index, plane, begin : begin + count, :]
            high = z_ref[number, index, plane, begin + 1 : begin + 1 + count, :]
            modes[component + "s" + z] = high + low
            modes[component + "d" + z] = high - low
    return modes


def element_modes(before, after):
    modes = {}
    for key in CLASSES:
        if key[1:] != "ss":
            modes[key[0] + "s" + key[1:]] = after[key] + before[key]
        modes[key[0] + "d" + key[1:]] = after[key] - before[key]
    return modes


def mode_forces(u, moduli):
    forces = {}
    normal = moduli * NORMAL
    trace = (u["xdss"] + u["ysds"] + u["zssd"]) * (TRACE / NORMAL)
    for key in ("xdss", "ysds", "zssd"):
        forces[key] = normal * (u[key] + trace)
    shear = moduli * SHEAR_FIRST
    for one, other in (("ydss", "xsds"), ("zsds", "yssd"), ("xssd", "zdss")):
        forces[one] = forces[other] = shear * (u[one] + u[other])
    bend = moduli * BEND
    for one, other in PAIRS:
        forces[one] = bend * (u[one] + (BEND_MIX / BEND) * u[other])
        forces[other] = bend * (u[other] + (BEND_MIX / BEND) * u[one])
    twist = moduli * TWIST
    total = u[TRIPLE[0]] + u[TRIPLE[1]] + u[TRIPLE[2]]
    for key in TRIPLE:
        forces[key] = twist * (total + u[key])
    third = moduli * THIRD
    for component in "xyz":
        forces[component + "ddd"] = third * u[component + "ddd"]
    return forces


def unit_energy(u):
    trace = u["xdss"] + u["ysds"] + u["zssd"]
    energy = TRACE * (trace * trace)
    energy += NORMAL * (u["xdss"] ** 2 + u["ysds"] ** 2 + u["zssd"] ** 2)
    shears = [u[a] + u[b] for a, b in (("ydss", "xsds"), ("zsds", "yssd"), ("xssd", "zdss"))]
    energy += SHEAR_FIRST * (shears[0] ** 2 + shears[1] ** 2 + shears[2] ** 2)
    squares, mixed = 0.0, 0.0
    for one, other in PAIRS:
        squares += u[one] ** 2 + u[other] ** 2
        mixed += (u[one] + u[other]) ** 2
    energy += (BEND - BEND_MIX) * squares + BEND_MIX * mixed
    total = u[TRIPLE[0]] + u[TRIPLE[1]] + u[TRIPLE[2]]
    squares = total * total
    for key in TRIPLE:
        squares += u[key] ** 2
    energy += TWIST * squares
    energy += THIRD * (u["xddd"] ** 2 + u["yddd"] ** 2 + u["zddd"] ** 2)
    return energy


def fields_kernel(shape, *refs):
    rows, cols, _ = shape
    sources, (own, lower, upper, low, high) = refs[:6], refs[6:11]
    *local, arrived = refs[11:]
    copies = [pltpu.make_async_copy(s, t, arrived.at[i]) for i, (s, t) in enumerate(zip(sources, local))]
    for copy in copies:
        copy.start()
    for copy in copies:
        copy.wait()
    density, void, solid, fixed, load, traction = local
    is_solid, is_void = solid[...] == 1, void[...] == 1
    rho = jnp.where(is_solid, 1.0, jnp.where(is_void, RHO_FLOOR, density[...]))
    own[0] = rho
    free = (1 - fixed[...]).astype(jnp.float32)
    own[1] = free
    loaded = free * load[...].astype(jnp.float32)
    for component in range(3):
        own[2 + component] = loaded * traction[component]
    for layer in range(HALO):
        for field in range(5):
            low[layer, field] = own[field, pl.ds(layer, rows, stride=cols), :]
            high[layer, field] = own[field, pl.ds(cols - HALO + layer, rows, stride=cols), :]
    least = jnp.maximum(RHO_FLOOR, rho - MOVE_LIMIT)
    most = jnp.minimum(1.0, rho + MOVE_LIMIT)
    lower[...] = jnp.where(is_solid, 1.0, jnp.where(is_void, RHO_FLOOR, least))
    upper[...] = jnp.where(is_solid, 1.0, jnp.where(is_void, RHO_FLOOR, most))


def widen_kernel(shape, own, from_low, from_high, ext, low, high):
    rows, cols, _ = shape
    wide = cols + 2 * HALO
    for field in range(5):
        for row in range(rows):
            ext[field, pl.ds(row * wide + HALO, cols), :] = own[field, pl.ds(row * cols, cols), :]
        for layer in range(HALO):
            ext[field, pl.ds(layer, rows, stride=wide), :] = from_low[layer, field]
            ext[field, pl.ds(wide - HALO + layer, rows, stride=wide), :] = from_high[layer, field]
        low[field] = ext[field, : HALO_X * wide, :]
        high[field] = ext[field, (rows - HALO_X) * wide :, :]


def grid_cuts(rows):
    place, last = lax.axis_index("gx"), lax.axis_size("gx") - 1
    return {
        HALO_X - 1: jnp.where(place == 0, 0.0, 1.0),
        HALO_X + rows - 1: jnp.where(place == last, 0.0, 1.0),
    }


def cut_off(values, keep):
    return values if keep is None else {key: value * keep for key, value in values.items()}


class Stages:
    def __init__(self, shape, fields, inverses, p, w, set_p, set_w, z_ref, mode_ref, lift_ref, pipe_ref):
        self.wide, self.depth = shape[1] + 2 * HALO, shape[2]
        lanes = lane_index((self.wide, self.depth))
        self.keep_last = jnp.where(lanes < self.depth - 1, 1.0, 0.0)
        self.keep_first = jnp.where(lanes > 0, 1.0, 0.0)
        self.fields, self.inverses, self.p, self.w = fields, inverses, p, w
        self.set_p, self.set_w = set_p, set_w
        self.z_ref, self.mode_ref, self.lift_ref, self.pipe_ref = z_ref, mode_ref, lift_ref, pipe_ref

    def lift_moduli(self, around):
        return around + pltpu.roll(around, 1, 1) * self.keep_first

    def produce(self, level, plane, slot):
        for component in range(3):
            value = self.p(level, component, plane)
            lifted = pltpu.roll(value, self.depth - 1, 1) * self.keep_last
            self.z_ref[component, 0, slot, : self.wide] = lifted + value
            self.z_ref[component, 1, slot, : self.wide] = lifted - value

    def begin(self, slot):
        modes = load_modes(self.z_ref, slot, 0, self.wide)
        for index, key in enumerate(CLASSES):
            self.mode_ref[index] = modes[key]
            self.lift_ref[index] = jnp.zeros((self.wide, self.depth), jnp.float32)

    def spread(self, plane, slot, keep=None):
        after = load_modes(self.z_ref, slot, 0, self.wide)
        before = {key: self.mode_ref[index] for index, key in enumerate(CLASSES)}
        lift = {key: self.lift_ref[index] for index, key in enumerate(CLASSES)}
        forces = mode_forces(element_modes(before, cut_off(after, keep)), self.fields(plane))
        for number, component in enumerate("xyz"):
            along_z = {}
            for z in "sd":
                along_y = {}
                for y in "sd":
                    key = component + y + z
                    slope = forces[component + "d" + y + z]
                    if y + z == "ss":
                        along_y[y] = lift[key] - slope
                        lift[key] = slope
                    else:
                        mean = forces[component + "s" + y + z]
                        along_y[y] = lift[key] + (mean - slope)
                        lift[key] = mean + slope
                along_z[z] = (along_y["s"] - along_y["d"]) + pltpu.roll(along_y["s"] + along_y["d"], 1, 0)
            self.pipe_ref[number, 0] = along_z["s"] + along_z["d"]
            self.pipe_ref[number, 1] = along_z["s"] - along_z["d"]
        lift = cut_off(lift, keep)
        for index, key in enumerate(CLASSES):
            self.mode_ref[index] = after[key]
            self.lift_ref[index] = lift[key]

    def finish(self, level, plane):
        for component in range(3):
            shifted = pltpu.roll(self.pipe_ref[component, 0], 1, 1) * self.keep_first
            residual = (self.pipe_ref[component, 1] + shifted) - self.w(level, component, plane)
            self.set_w(level + 1, component, plane, residual)
            self.set_p(level + 1, component, plane, residual * self.inverses(plane))


def moduli_of(rho):
    return jnp.where(rho > 0.0, E_MIN + rho * rho * rho * (1.0 - E_MIN), 0.0)


def inverse_of(free, around):
    return free / (free * (DIAGONAL * around) + (1.0 - free))


PAIR_LIST = [(i, j) for i in range(BASIS) for j in range(i + 1)]


def inner_kernel(shape, ext, p_ref, w_ref, field_ref, inverse_ref, totals_ref, z_ref, mode_ref, lift_ref, pipe_ref):
    rows, cols, depth = shape
    wide, shift = cols + 2 * HALO, HALO_X - 1
    field_ref[:, :8, :] = jnp.zeros((rows, 8, depth), jnp.float32)
    z_ref[:, :, :, wide:, :] = jnp.zeros((3, 2, z_ref.shape[2], 8, depth), jnp.float32)
    for row in range(rows):
        window = slice(row * wide, (row + 1) * wide)
        field_ref[row, 8:, :] = moduli_of(ext[0, window, :])
        for component in range(3):
            w_ref[0, component, row + 1] = ext[2 + component, window, :]

    def store(ref):
        def put(level, component, plane, value):
            ref[level, component, plane - shift] = value

        return put

    stages = Stages(
        shape,
        lambda plane: field_ref[plane - HALO_X, 8:, :],
        lambda plane: inverse_ref[plane - HALO_X],
        lambda level, component, plane: p_ref[level, component, plane - shift],
        lambda level, component, plane: w_ref[level, component, plane - shift],
        store(p_ref),
        store(w_ref),
        z_ref,
        mode_ref,
        lift_ref,
        pipe_ref,
    )
    inverse_ref[0] = jnp.zeros((wide, depth), jnp.float32)
    for row in range(1, rows):
        around = field_ref[row - 1, 8:, :] + field_ref[row - 1, 7 : 7 + wide, :]
        around = around + (field_ref[row, 8:, :] + field_ref[row, 7 : 7 + wide, :])
        inverse = inverse_of(ext[1, row * wide : (row + 1) * wide, :], stages.lift_moduli(around))
        inverse_ref[row] = inverse
        for component in range(3):
            p_ref[0, component, row + 1] = w_ref[0, component, row + 1] * inverse
    for row in range(1, rows):
        stages.produce(0, row + HALO_X, row + 1)

    for level in range(BASIS - 1):
        first, last = HALO_X + 1 + level, HALO_X + rows - 2 - level
        stages.begin(first - shift)
        pipe_ref[...] = jnp.zeros(pipe_ref.shape, jnp.float32)

        def step(plane, carry):
            stages.produce(level + 1, plane - 2, plane - 2 - shift)
            stages.finish(level, plane - 1)
            stages.spread(plane, plane + 1 - shift)
            return carry

        lax.fori_loop(first, last + 1, step, 0)
        stages.finish(level, last)
        stages.produce(level + 1, last - 1, last - 1 - shift)
        stages.produce(level + 1, last, last - shift)

    first, last = HALO_X + BASIS, HALO_X + rows - 1 - (BASIS - 1)
    modes = load_modes(z_ref, first - shift, HALO, cols)
    for index, key in enumerate(CLASSES):
        mode_ref[index, :cols] = modes[key]

    def dot_step(plane, totals):
        totals = add_dots(
            totals,
            lambda level, component: p_ref[level, component, plane - shift, HALO : HALO + cols, :],
            lambda level, component: w_ref[level, component, plane - shift, HALO : HALO + cols, :],
        )
        after = load_modes(z_ref, plane + 1 - shift, HALO, cols)
        before = {key: mode_ref[index, :cols] for index, key in enumerate(CLASSES)}
        for index, key in enumerate(CLASSES):
            mode_ref[index, :cols] = after[key]
        energy = unit_energy(element_modes(before, after))
        totals[-1] = totals[-1] + field_ref[plane - HALO_X, 8 + HALO : 8 + HALO + cols, :] * energy
        return tuple(totals)

    zeros = jnp.zeros((cols, depth), jnp.float32)
    totals = lax.fori_loop(first, last, dot_step, (zeros,) * (len(PAIR_LIST) + 1))
    totals = add_dots(
        totals,
        lambda level, component: p_ref[level, component, last - shift, HALO : HALO + cols, :],
        lambda level, component: w_ref[level, component, last - shift, HALO : HALO + cols, :],
    )
    for index, total in enumerate(totals):
        totals_ref[index] = total


def add_dots(totals, p, w):
    totals = list(totals)
    for component in range(3):
        ps = [p(level, component) for level in range(BASIS)]
        ws = [w(level, component) for level in range(BASIS)]
        for index, (i, j) in enumerate(PAIR_LIST):
            totals[index] = totals[index] + ps[i] * ws[j]
    return totals


def outer_kernel(shape, ext, from_low, from_high, p_in, w_in, field_in, inverse_in, totals_in, p_ref, sums_out, *scratch):
    rows, cols, depth = shape
    wide, long, shift = cols + 2 * HALO, rows + 2 * HALO_X, HALO_X - 1
    field_ref, inverse_ref, w_ref, z_ref, *both = scratch
    cuts = grid_cuts(rows)
    own = range(HALO_X, HALO_X + rows)
    z_ref[:, :, :, wide:, :] = jnp.zeros((3, 2, long, 8, depth), jnp.float32)
    field_ref[:, :8, :] = jnp.zeros((long, 8, depth), jnp.float32)

    def source(plane):
        if plane < HALO_X:
            return from_low, plane * wide
        if plane < HALO_X + rows:
            return ext, (plane - HALO_X) * wide
        return from_high, (plane - HALO_X - rows) * wide

    def given(field, plane):
        ref, row = source(plane)
        return ref[field, row : row + wide, :]

    def fields(plane, begin=0, count=wide):
        if plane in own:
            return field_in[plane - HALO_X, 8 + begin : 8 + begin + count, :]
        return field_ref[plane, 8 + begin : 8 + begin + count, :]

    def inverses(plane):
        return inverse_in[plane - HALO_X] if HALO_X < plane < HALO_X + rows else inverse_ref[plane]

    def is_inner(level, plane):
        return HALO_X + 1 + level <= plane <= HALO_X + rows - 1 - level

    def p(level, component, plane, begin=0, count=wide):
        if is_inner(level, plane):
            return p_in[level, component, plane - shift, begin : begin + count, :]
        return p_ref[level, component, plane, begin : begin + count, :]

    def w(level, component, plane, begin=0, count=wide):
        if is_inner(level, plane):
            return w_in[level, component, plane - shift, begin : begin + count, :]
        if level == 0:
            ref, row = source(plane)
            return ref[2 + component, row + begin : row + begin + count, :]
        return w_ref[level, component, plane, begin : begin + count, :]

    def set_p(level, component, plane, value):
        p_ref[level, component, plane] = value

    def set_w(level, component, plane, value):
        w_ref[level, component, plane] = value

    sides = [
        Stages(shape, fields, inverses, p, w, set_p, set_w, z_ref, both[0], both[1], both[2]),
        Stages(shape, fields, inverses, p, w, set_p, set_w, z_ref, both[3], both[4], both[5]),
    ]
    for plane in range(long):
        if plane not in own:
            field_ref[plane, 8:, :] = moduli_of(given(0, plane))
    edge_planes = [*range(1, HALO_X + 1), *range(HALO_X + rows, long)]
    for plane in edge_planes:
        around = fields(plane - 1) + fields(plane - 1, -1)
        if plane - 1 in cuts:
            around = around * cuts[plane - 1]
        around = around + (fields(plane) + fields(plane, -1))
        inverse = inverse_of(given(1, plane), sides[0].lift_moduli(around))
        inverse_ref[plane] = inverse
        for component in range(3):
            set_p(0, component, plane, given(2 + component, plane) * inverse)
    for plane in edge_planes:
        sides[0].produce(0, plane, plane)

    steps = HALO_X + 1
    for level in range(BASIS - 1):
        starts = 1 + level, HALO_X + rows - 2 - level
        wanted = 2 + level, HALO_X + rows - 1 - level
        for plane in (HALO_X + 1 + level, HALO_X + 2 + level, HALO_X + rows - 2 - level, HALO_X + rows - 1 - level):
            sides[0].produce(level, plane, plane)
        for side, start in zip(sides, starts):
            side.begin(start)
        for step in range(steps + 2):
            for side, start, least in zip(sides, starts, wanted):
                plane = start + step
                if least <= plane - 2 < start + steps:
                    side.produce(level + 1, plane - 2, plane - 2)
                if least <= plane - 1 < start + steps:
                    side.finish(level, plane - 1)
                if plane < start + steps:
                    side.spread(plane, plane + 1, cuts.get(plane))

    last = BASIS - 1
    for plane in (HALO_X + 1 + last, HALO_X + rows - 1 - last):
        sides[0].produce(last, plane, plane)
    totals = [totals_in[index] for index in range(len(PAIR_LIST) + 1)]
    for plane in own:
        if not is_inner(last, plane):
            totals = add_dots(
                totals,
                lambda level, component: p(level, component, plane, HALO, cols),
                lambda level, component: w(level, component, plane, HALO, cols),
            )
        if not (is_inner(last, plane) and is_inner(last, plane + 1)):
            before = load_modes(z_ref, plane, HALO, cols)
            after = cut_off(load_modes(z_ref, plane + 1, HALO, cols), cuts.get(plane))
            energy = unit_energy(element_modes(before, after))
            totals[-1] = totals[-1] + fields(plane, HALO, cols) * energy
    slots = lane_index((1, 128))
    line = jnp.zeros((1, 128), jnp.float32)
    for index, total in enumerate(totals):
        share = jnp.sum(jnp.sum(total, axis=0, keepdims=True), axis=1, keepdims=True)
        line = line + jnp.where(slots == index, share, 0.0)
    sums_out[...] = jnp.broadcast_to(line, sums_out.shape)


def coefficients(shares):
    line = jnp.sum(shares, axis=0, keepdims=True)
    slots = lane_index(line.shape)

    def entry(index):
        return jnp.sum(jnp.where(slots == index, line, 0.0), axis=1, keepdims=True)

    inner = {}
    for index, (i, j) in enumerate(PAIR_LIST):
        inner[i, j] = inner[j, i] = entry(index)
    energy = {(BASIS - 1, BASIS - 1): entry(len(PAIR_LIST))}
    for i in range(BASIS):
        for j in range(min(i + 1, BASIS - 1)):
            energy[i, j] = inner[i, j + 1] + inner[i, j]
    lower, pivot, inverse, solved = {}, {}, {}, {}
    for k in range(BASIS):
        left = energy[k, k]
        for m in range(k):
            left = left - lower[k, m] * lower[k, m] * pivot[m]
        sound = left > 1e-6 * energy[k, k]
        pivot[k] = jnp.where(sound, left, 0.0)
        inverse[k] = jnp.where(sound, 1.0 / jnp.where(sound, left, 1.0), 0.0)
        for i in range(k + 1, BASIS):
            part = energy[i, k]
            for m in range(k):
                part = part - lower[i, m] * lower[k, m] * pivot[m]
            lower[i, k] = part * inverse[k]
    for k in range(BASIS):
        part = inner[k, 0]
        for m in range(k):
            part = part - lower[k, m] * solved[m]
        solved[k] = part
    result = {}
    for k in reversed(range(BASIS)):
        part = solved[k] * inverse[k]
        for m in range(k + 1, BASIS):
            part = part - lower[m, k] * result[m]
        result[k] = part
    return [result[k] for k in range(BASIS)]


def energy_kernel(
    shape, shares, inner, outer, own, from_low, from_high, displacement, weighted, low, high, u_ref, z_ref
):
    rows, cols, depth = shape
    wide, planes = cols + 2 * HALO, rows + 2 * REACH
    keep_last = jnp.where(lane_index((wide, depth)) < depth - 1, 1.0, 0.0)
    parts = [jnp.broadcast_to(part, (wide, depth)) for part in coefficients(shares[...])]
    cuts = grid_cuts(rows)
    for plane in range(planes + 1):
        source = plane + HALO_X - REACH
        for component in range(3):
            total = None
            for level in range(BASIS):
                if HALO_X + 1 + level <= source <= HALO_X + rows - 1 - level:
                    term = parts[level] * inner[level, component, source - HALO_X + 1]
                else:
                    term = parts[level] * outer[level, component, source]
                total = term if total is None else total + term
            lifted = pltpu.roll(total, depth - 1, 1) * keep_last
            z_ref[component, 0, plane] = lifted + total
            z_ref[component, 1, plane] = lifted - total
            row = plane - REACH
            if 0 <= row < rows:
                u_ref[component, row] = total
                displacement[component, row] = u_ref[component, row, HALO : HALO + cols, :]
    before = load_modes(z_ref, 0, HALO, cols)
    for plane in range(planes):
        row = plane - REACH
        after = load_modes(z_ref, plane + 1, HALO, cols)
        energy = unit_energy(element_modes(before, cut_off(after, cuts.get(row + HALO_X))))
        before = after
        if row < 0:
            rho = from_low[0, (row + HALO_X) * wide + HALO : (row + HALO_X) * wide + HALO + cols, :]
        elif row < rows:
            rho = own[0, row * cols : (row + 1) * cols, :]
        else:
            rho = from_high[0, (row - rows) * wide + HALO : (row - rows) * wide + HALO + cols, :]
        weighted[plane * cols : (plane + 1) * cols, :] = rho * (3.0 * rho * rho * (1.0 - E_MIN) * energy)
    for layer in range(REACH):
        low[layer] = weighted[pl.ds(layer, planes, stride=cols), :]
        high[layer] = weighted[pl.ds(cols - REACH + layer, planes, stride=cols), :]


def cone_table():
    table, total = {}, 0.0
    for a in range(-2, 3):
        for b in range(-2, 3):
            for c in range(-2, 3):
                total += max(0.0, 3.0 - math.sqrt(a * a + b * b + c * c))
    for flat in (0, 1, 2, 4, 5, 8):
        for c in range(3):
            table[flat, c] = max(0.0, 3.0 - math.sqrt(flat + c * c))
    return table, total


def volume_row(total):
    return jnp.sum(total, axis=0, keepdims=True)


def filter_kernel(shape, weighted, from_low, from_high, own, lower, upper, root, volume, plane_ref):
    rows, cols, depth = shape
    wide, planes = cols + 8, rows + 2 * REACH
    table, total = cone_table()
    for plane in range(planes):
        plane_ref[plane * wide + REACH : plane * wide + REACH + cols, :] = weighted[plane * cols : (plane + 1) * cols, :]
    for layer in range(REACH):
        plane_ref[pl.ds(layer, planes, stride=wide), :] = from_low[layer]
        plane_ref[pl.ds(REACH + cols + layer, planes, stride=wide), :] = from_high[layer]
    volume_sum = jnp.zeros((cols, depth), jnp.float32)
    for row in range(rows):
        spread = {}
        for a in range(-REACH, REACH + 1):
            for b in range(-REACH, REACH + 1):
                key = a * a + b * b
                value = plane_ref[pl.ds((row + REACH + a) * wide + REACH + b, cols), :]
                spread[key] = value if key not in spread else spread[key] + value
        sums = []
        for c in range(3):
            part = None
            for key, value in spread.items():
                if table[key, c] > 0.0:
                    term = table[key, c] * value
                    part = term if part is None else part + term
            sums.append(part)
        convolved = sums[0]
        for c in (1, 2):
            convolved = convolved + (pltpu.roll(sums[c], c, 1) + pltpu.roll(sums[c], depth - c, 1))
        window = slice(row * cols, (row + 1) * cols)
        rho = own[0, window, :]
        base = rho * jnp.sqrt(convolved / (total * rho))
        root[window, :] = base
        volume_sum = volume_sum + jnp.minimum(jnp.maximum(base, lower[window, :]), upper[window, :])
    volume[...] = jnp.broadcast_to(volume_row(volume_sum), volume.shape)


def scale_of(target, volumes):
    scale = None
    for volume in volumes:
        whole = jnp.sum(jnp.sum(volume[...], axis=0, keepdims=True), axis=1, keepdims=True)
        ratio = target / whole
        scale = ratio if scale is None else scale * ratio
    return scale


def trial_kernel(target, steps, final, *refs):
    volumes, (root, lower, upper, out) = refs[:steps], refs[steps:]
    scale = scale_of(target, volumes)
    moved = jnp.minimum(jnp.maximum(root[...] * scale, lower[...]), upper[...])
    if final:
        out[...] = moved
    else:
        out[...] = jnp.broadcast_to(volume_row(moved), out.shape)


def call(kernel, name, out_shapes, *args, scratch=(), flops=0, space=pltpu.VMEM):
    shapes = [jax.ShapeDtypeStruct(shape, jnp.float32) for shape in out_shapes]
    moved = sum(4 * math.prod(value.shape) for value in [*args, *shapes])
    return pl.pallas_call(
        kernel,
        name=name,
        out_shape=shapes,
        in_specs=[pl.BlockSpec(memory_space=space)] * len(args),
        out_specs=[pl.BlockSpec(memory_space=pltpu.VMEM)] * len(shapes),
        scratch_shapes=[pltpu.VMEM(item, jnp.float32) if isinstance(item, tuple) else item for item in scratch],
        compiler_params=pltpu.CompilerParams(vmem_limit_bytes=VMEM_LIMIT),
        cost_estimate=pl.CostEstimate(flops=flops, bytes_accessed=moved, transcendentals=0),
    )(*args)


def exchange(low, high, axis, wrap):
    count = lax.axis_size(axis)
    ends = count if wrap else count - 1
    from_low = lax.ppermute(high, axis, [(i, (i + 1) % count) for i in range(ends)])
    from_high = lax.ppermute(low, axis, [((i + 1) % count, i) for i in range(ends)])
    return from_low, from_high


def everyone(shares):
    return lax.all_to_all(shares, AXES, 0, 0, tiled=True)


def shards(density, void_mask, solid_mask, fixed_mask, load_mask, traction):
    shape = rows, cols, depth = density.shape
    devices = lax.axis_size("gx") * lax.axis_size("gy")
    wide, long = cols + 2 * HALO, rows + 2 * HALO_X
    planes = rows + 2 * REACH
    named = lambda kernel: functools.partial(kernel, shape)
    flat = (rows * cols, depth)
    inputs = [
        pltpu.with_memory_space_constraint(value.reshape(*value.shape[:-3], *flat), pltpu.HBM)
        for value in (density, void_mask, solid_mask, fixed_mask, load_mask, traction)
    ]

    own, lower, upper, low, high = call(
        named(fields_kernel),
        "fields",
        [(5, *flat), flat, flat, (HALO, 5, rows, depth), (HALO, 5, rows, depth)],
        *inputs,
        scratch=[pltpu.VMEM(value.shape, value.dtype) for value in inputs] + [pltpu.SemaphoreType.DMA((6,))],
        space=pltpu.HBM,
    )
    from_low, from_high = exchange(low, high, "gy", False)
    ext, low, high = call(
        named(widen_kernel),
        "widen",
        [(5, rows * wide, depth), (5, HALO_X * wide, depth), (5, HALO_X * wide, depth)],
        own,
        from_low,
        from_high,
    )
    from_low, from_high = exchange(low, high, "gx", True)
    side = [(12, wide, depth), (12, wide, depth), (3, 2, wide, depth)]
    inner = call(
        named(inner_kernel),
        "inner",
        [
            (BASIS, 3, rows + 1, wide, depth),
            (BASIS, 3, rows + 1, wide, depth),
            (rows, 8 + wide, depth),
            (rows, wide, depth),
            (len(PAIR_LIST) + 1, cols, depth),
        ],
        ext,
        scratch=[(3, 2, rows + 1, wide + 8, depth), *side],
    )
    outer, sums = call(
        named(outer_kernel),
        "outer",
        [(BASIS, 3, long, wide, depth), (devices, 128)],
        ext,
        from_low,
        from_high,
        *inner,
        scratch=[
            (long, 8 + wide, depth),
            (long, wide, depth),
            (BASIS, 3, long, wide, depth),
            (3, 2, long, wide + 8, depth),
            *side,
            *side,
        ],
    )
    displacement, weighted, low, high = call(
        named(energy_kernel),
        "energy",
        [(3, rows, cols, depth), (planes * cols, depth), (REACH, planes, depth), (REACH, planes, depth)],
        everyone(sums),
        inner[0],
        outer,
        own,
        from_low,
        from_high,
        scratch=[(3, rows, wide, depth), (3, 2, planes + 1, wide, depth)],
    )
    from_low, from_high = exchange(low, high, "gy", True)
    root, volume = call(
        named(filter_kernel),
        "filter",
        [flat, (devices, depth)],
        weighted,
        from_low,
        from_high,
        own,
        lower,
        upper,
        scratch=[(planes * (cols + 8), depth)],
    )
    target = VOLUME_SHARE * rows * cols * depth * devices
    terms, volumes = (root, lower, upper), [everyone(volume)]
    for step in (1, 2):
        (volume,) = call(
            functools.partial(trial_kernel, target, step, False), "trial", [(devices, depth)], *volumes, *terms
        )
        volumes.append(everyone(volume))
    (new_density,) = call(functools.partial(trial_kernel, target, 3, True), "update", [flat], *volumes, *terms)
    return new_density.reshape(shape), displacement


def solution(mesh):
    placed = (P("gx", "gy", None),) * 5 + (P(None, "gx", "gy", None),)
    return jax.shard_map(
        shards,
        mesh=mesh,
        in_specs=placed,
        out_specs=(P("gx", "gy", None), P(None, "gx", "gy", None)),
        check_vma=False,
    )
```

```python
import functools
import math

import jax
import jax.numpy as jnp
import numpy as np
from jax import lax
from jax.experimental import pallas as pl
from jax.experimental.pallas import tpu as pltpu
from jax.sharding import PartitionSpec as P

E_MIN = 0.001
RHO_FLOOR = 0.001
MOVE_LIMIT = 0.2
VOLUME_SHARE = 0.4
BASIS = 4
REACH = 2
HALO = BASIS
HALO_X = BASIS + REACH
AXES = ("gx", "gy")
FIELDS = 5
LOW_HALO = [(layer, field) for layer in range(HALO) for field in range(FIELDS) if layer > 0 or field == 0]
HIGH_HALO = [(layer, field) for layer in range(HALO) for field in range(FIELDS)]
VMEM_LIMIT = 40 * 1024 * 1024

POISSON = 0.3
LAME = POISSON / ((1.0 + POISSON) * (1.0 - 2.0 * POISSON))
SHEAR = 1.0 / (2.0 * (1.0 + POISSON))
NORMAL = 2.0 * SHEAR / 16.0
TRACE = LAME / 16.0
SHEAR_FIRST = SHEAR / 16.0
BEND = (LAME + 3.0 * SHEAR) / 48.0
BEND_MIX = LAME / 48.0
TWIST = SHEAR / 48.0
THIRD = (LAME + 4.0 * SHEAR) / 144.0
DIAGONAL = NORMAL + TRACE + 2.0 * SHEAR_FIRST + 2.0 * BEND + 2.0 * TWIST + THIRD
PAIRS = (("xdds", "zsdd"), ("ydds", "zdsd"), ("xdsd", "ysdd"))
TRIPLE = ("zdds", "ydsd", "xsdd")
CLASSES = [c + y + z for c in "xyz" for y in "sd" for z in "sd"]


def lane_index(shape):
    return lax.broadcasted_iota(jnp.int32, shape, len(shape) - 1)


def load_modes(z_ref, plane, begin, count):
    modes = {}
    for number, component in enumerate("xyz"):
        for index, z in enumerate("sd"):
            low = z_ref[number, index, plane, begin : begin + count, :]
            high = z_ref[number, index, plane, begin + 1 : begin + 1 + count, :]
            modes[component + "s" + z] = high + low
            modes[component + "d" + z] = high - low
    return modes


def element_modes(before, after):
    modes = {}
    for key in CLASSES:
        if key[1:] != "ss":
            modes[key[0] + "s" + key[1:]] = after[key] + before[key]
        modes[key[0] + "d" + key[1:]] = after[key] - before[key]
    return modes


def mode_forces(u, moduli):
    forces = {}
    normal = moduli * NORMAL
    trace = (u["xdss"] + u["ysds"] + u["zssd"]) * (TRACE / NORMAL)
    for key in ("xdss", "ysds", "zssd"):
        forces[key] = normal * (u[key] + trace)
    shear = moduli * SHEAR_FIRST
    for one, other in (("ydss", "xsds"), ("zsds", "yssd"), ("xssd", "zdss")):
        forces[one] = forces[other] = shear * (u[one] + u[other])
    bend = moduli * BEND
    for one, other in PAIRS:
        forces[one] = bend * (u[one] + (BEND_MIX / BEND) * u[other])
        forces[other] = bend * (u[other] + (BEND_MIX / BEND) * u[one])
    twist = moduli * TWIST
    total = u[TRIPLE[0]] + u[TRIPLE[1]] + u[TRIPLE[2]]
    for key in TRIPLE:
        forces[key] = twist * (total + u[key])
    third = moduli * THIRD
    for component in "xyz":
        forces[component + "ddd"] = third * u[component + "ddd"]
    return forces


def unit_energy(u):
    trace = u["xdss"] + u["ysds"] + u["zssd"]
    energy = TRACE * (trace * trace)
    energy += NORMAL * (u["xdss"] ** 2 + u["ysds"] ** 2 + u["zssd"] ** 2)
    shears = [u[a] + u[b] for a, b in (("ydss", "xsds"), ("zsds", "yssd"), ("xssd", "zdss"))]
    energy += SHEAR_FIRST * (shears[0] ** 2 + shears[1] ** 2 + shears[2] ** 2)
    squares, mixed = 0.0, 0.0
    for one, other in PAIRS:
        squares += u[one] ** 2 + u[other] ** 2
        mixed += (u[one] + u[other]) ** 2
    energy += (BEND - BEND_MIX) * squares + BEND_MIX * mixed
    total = u[TRIPLE[0]] + u[TRIPLE[1]] + u[TRIPLE[2]]
    squares = total * total
    for key in TRIPLE:
        squares += u[key] ** 2
    energy += TWIST * squares
    energy += THIRD * (u["xddd"] ** 2 + u["yddd"] ** 2 + u["zddd"] ** 2)
    return energy


def fields_kernel(shape, *refs):
    rows, cols, _ = shape
    sources, (own, lower, upper, low, high, low_x, high_x) = refs[:6], refs[6:13]
    *local, arrived = refs[13:]
    copies = [pltpu.make_async_copy(s, t, arrived.at[i]) for i, (s, t) in enumerate(zip(sources, local))]
    for copy in copies:
        copy.start()
    for copy in copies:
        copy.wait()
    density, void, solid, fixed, load, traction = local
    is_solid, is_void = solid[...] == 1, void[...] == 1
    rho = jnp.where(is_solid, 1.0, jnp.where(is_void, RHO_FLOOR, density[...]))
    own[0] = rho
    free = (1 - fixed[...]).astype(jnp.float32)
    own[1] = free
    loaded = free * load[...].astype(jnp.float32)
    for component in range(3):
        own[2 + component] = loaded * traction[component]
    for index, (layer, field) in enumerate(HIGH_HALO):
        low[index] = own[field, pl.ds(layer, rows, stride=cols), :]
    for index, (layer, field) in enumerate(LOW_HALO):
        high[index] = own[field, pl.ds(cols - HALO + layer, rows, stride=cols), :]
    low_x[...] = own[:, : HALO_X * cols, :]
    high_x[...] = own[:, (rows - HALO_X) * cols :, :]
    least = jnp.maximum(RHO_FLOOR, rho - MOVE_LIMIT)
    most = jnp.minimum(1.0, rho + MOVE_LIMIT)
    lower[...] = jnp.where(is_solid, 1.0, jnp.where(is_void, RHO_FLOOR, least))
    upper[...] = jnp.where(is_solid, 1.0, jnp.where(is_void, RHO_FLOOR, most))


def widen_kernel(shape, own, from_low, from_high, ext, low, high):
    rows, cols, depth = shape
    wide = cols + 2 * HALO
    for field in range(FIELDS):
        for row in range(rows):
            ext[field, pl.ds(row * wide + HALO, cols), :] = own[field, pl.ds(row * cols, cols), :]
        for layer in range(HALO):
            for entries, source, shift in ((LOW_HALO, from_low, 0), (HIGH_HALO, from_high, HALO)):
                if (layer, field) in entries:
                    index = entries.index((layer, field))
                    whole = source[index]
                    begin, end = source[index, :HALO_X], source[index, rows - HALO_X :]
                else:
                    whole = jnp.zeros((rows, depth), jnp.float32)
                    begin = end = jnp.zeros((HALO_X, depth), jnp.float32)
                row = layer if shift == 0 else cols + HALO + layer
                ext[field, pl.ds(row, rows, stride=wide), :] = whole
                low[field, pl.ds(shift + layer, HALO_X, stride=2 * HALO), :] = begin
                high[field, pl.ds(shift + layer, HALO_X, stride=2 * HALO), :] = end


def grid_cuts(rows):
    place, last = lax.axis_index("gx"), lax.axis_size("gx") - 1
    return {
        HALO_X - 1: jnp.where(place == 0, 0.0, 1.0),
        HALO_X + rows - 1: jnp.where(place == last, 0.0, 1.0),
    }


def cut_off(values, keep):
    return values if keep is None else {key: value * keep for key, value in values.items()}


class Stages:
    def __init__(self, shape, fields, inverses, p, w, set_p, set_w, z_ref, mode_ref, lift_ref, pipe_ref):
        self.wide, self.depth = shape[1] + 2 * HALO, shape[2]
        lanes = lane_index((self.wide, self.depth))
        self.keep_last = jnp.where(lanes < self.depth - 1, 1.0, 0.0)
        self.keep_first = jnp.where(lanes > 0, 1.0, 0.0)
        self.fields, self.inverses, self.p, self.w = fields, inverses, p, w
        self.set_p, self.set_w = set_p, set_w
        self.z_ref, self.mode_ref, self.lift_ref, self.pipe_ref = z_ref, mode_ref, lift_ref, pipe_ref

    def lift_moduli(self, around):
        return around + pltpu.roll(around, 1, 1) * self.keep_first

    def produce(self, level, plane, slot):
        for component in range(3):
            value = self.p(level, component, plane)
            lifted = pltpu.roll(value, self.depth - 1, 1) * self.keep_last
            self.z_ref[component, 0, slot, : self.wide] = lifted + value
            self.z_ref[component, 1, slot, : self.wide] = lifted - value

    def begin(self, slot):
        modes = load_modes(self.z_ref, slot, 0, self.wide)
        for index, key in enumerate(CLASSES):
            self.mode_ref[index] = modes[key]
            self.lift_ref[index] = jnp.zeros((self.wide, self.depth), jnp.float32)

    def spread(self, plane, slot, keep=None):
        after = load_modes(self.z_ref, slot, 0, self.wide)
        before = {key: self.mode_ref[index] for index, key in enumerate(CLASSES)}
        lift = {key: self.lift_ref[index] for index, key in enumerate(CLASSES)}
        forces = mode_forces(element_modes(before, cut_off(after, keep)), self.fields(plane))
        for number, component in enumerate("xyz"):
            along_z = {}
            for z in "sd":
                along_y = {}
                for y in "sd":
                    key = component + y + z
                    slope = forces[component + "d" + y + z]
                    if y + z == "ss":
                        along_y[y] = lift[key] - slope
                        lift[key] = slope
                    else:
                        mean = forces[component + "s" + y + z]
                        along_y[y] = lift[key] + (mean - slope)
                        lift[key] = mean + slope
                along_z[z] = (along_y["s"] - along_y["d"]) + pltpu.roll(along_y["s"] + along_y["d"], 1, 0)
            self.pipe_ref[number, 0] = along_z["s"] + along_z["d"]
            self.pipe_ref[number, 1] = along_z["s"] - along_z["d"]
        lift = cut_off(lift, keep)
        for index, key in enumerate(CLASSES):
            self.mode_ref[index] = after[key]
            self.lift_ref[index] = lift[key]

    def finish(self, level, plane):
        for component in range(3):
            shifted = pltpu.roll(self.pipe_ref[component, 0], 1, 1) * self.keep_first
            residual = (self.pipe_ref[component, 1] + shifted) - self.w(level, component, plane)
            self.set_w(level + 1, component, plane, residual)
            self.set_p(level + 1, component, plane, residual * self.inverses(plane))


def moduli_of(rho):
    return jnp.where(rho > 0.0, E_MIN + rho * rho * rho * (1.0 - E_MIN), 0.0)


def inverse_of(free, around):
    return free / (free * (DIAGONAL * around) + (1.0 - free))


PAIR_LIST = [(i, j) for i in range(BASIS) for j in range(i + 1)]


def inner_kernel(shape, ext, p_ref, w_ref, field_ref, inverse_ref, totals_ref, z_ref, mode_ref, lift_ref, pipe_ref):
    rows, cols, depth = shape
    wide, shift = cols + 2 * HALO, HALO_X - 1
    field_ref[:, :8, :] = jnp.zeros((rows, 8, depth), jnp.float32)
    z_ref[:, :, :, wide:, :] = jnp.zeros((3, 2, z_ref.shape[2], 8, depth), jnp.float32)
    for row in range(rows):
        window = slice(row * wide, (row + 1) * wide)
        field_ref[row, 8:, :] = moduli_of(ext[0, window, :])
        for component in range(3):
            w_ref[0, component, row + 1] = ext[2 + component, window, :]

    def store(ref):
        def put(level, component, plane, value):
            ref[level, component, plane - shift] = value

        return put

    stages = Stages(
        shape,
        lambda plane: field_ref[plane - HALO_X, 8:, :],
        lambda plane: inverse_ref[plane - HALO_X],
        lambda level, component, plane: p_ref[level, component, plane - shift],
        lambda level, component, plane: w_ref[level, component, plane - shift],
        store(p_ref),
        store(w_ref),
        z_ref,
        mode_ref,
        lift_ref,
        pipe_ref,
    )
    inverse_ref[0] = jnp.zeros((wide, depth), jnp.float32)
    for row in range(1, rows):
        around = field_ref[row - 1, 8:, :] + field_ref[row - 1, 7 : 7 + wide, :]
        around = around + (field_ref[row, 8:, :] + field_ref[row, 7 : 7 + wide, :])
        inverse = inverse_of(ext[1, row * wide : (row + 1) * wide, :], stages.lift_moduli(around))
        inverse_ref[row] = inverse
        for component in range(3):
            p_ref[0, component, row + 1] = w_ref[0, component, row + 1] * inverse
    for row in range(1, rows):
        stages.produce(0, row + HALO_X, row + 1)

    for level in range(BASIS - 1):
        first, last = HALO_X + 1 + level, HALO_X + rows - 2 - level
        stages.begin(first - shift)
        pipe_ref[...] = jnp.zeros(pipe_ref.shape, jnp.float32)

        def step(plane, carry):
            stages.produce(level + 1, plane - 2, plane - 2 - shift)
            stages.finish(level, plane - 1)
            stages.spread(plane, plane + 1 - shift)
            return carry

        lax.fori_loop(first, last + 1, step, 0)
        stages.finish(level, last)
        stages.produce(level + 1, last - 1, last - 1 - shift)
        stages.produce(level + 1, last, last - shift)

    first, last = HALO_X + BASIS, HALO_X + rows - 1 - (BASIS - 1)
    modes = load_modes(z_ref, first - shift, HALO, cols)
    for index, key in enumerate(CLASSES):
        mode_ref[index, :cols] = modes[key]

    def dot_step(plane, totals):
        totals = add_dots(
            totals,
            lambda level, component: p_ref[level, component, plane - shift, HALO : HALO + cols, :],
            lambda level, component: w_ref[level, component, plane - shift, HALO : HALO + cols, :],
        )
        after = load_modes(z_ref, plane + 1 - shift, HALO, cols)
        before = {key: mode_ref[index, :cols] for index, key in enumerate(CLASSES)}
        for index, key in enumerate(CLASSES):
            mode_ref[index, :cols] = after[key]
        energy = unit_energy(element_modes(before, after))
        totals[-1] = totals[-1] + field_ref[plane - HALO_X, 8 + HALO : 8 + HALO + cols, :] * energy
        return tuple(totals)

    zeros = jnp.zeros((cols, depth), jnp.float32)
    totals = lax.fori_loop(first, last, dot_step, (zeros,) * (len(PAIR_LIST) + 1))
    totals = add_dots(
        totals,
        lambda level, component: p_ref[level, component, last - shift, HALO : HALO + cols, :],
        lambda level, component: w_ref[level, component, last - shift, HALO : HALO + cols, :],
    )
    for index, total in enumerate(totals):
        totals_ref[index] = total


def add_dots(totals, p, w):
    totals = list(totals)
    for component in range(3):
        ps = [p(level, component) for level in range(BASIS)]
        ws = [w(level, component) for level in range(BASIS)]
        for index, (i, j) in enumerate(PAIR_LIST):
            totals[index] = totals[index] + ps[i] * ws[j]
    return totals


def outer_kernel(
    shape, ext, low_x, high_x, low_xy, high_xy, p_in, w_in, field_in, inverse_in, totals_in, p_ref, sums_out, *scratch
):
    rows, cols, depth = shape
    wide, long, shift = cols + 2 * HALO, rows + 2 * HALO_X, HALO_X - 1
    halo_ref, field_ref, inverse_ref, w_ref, z_ref, *both = scratch
    cuts = grid_cuts(rows)
    own = range(HALO_X, HALO_X + rows)
    z_ref[:, :, :, wide:, :] = jnp.zeros((3, 2, long, 8, depth), jnp.float32)
    field_ref[:, :8, :] = jnp.zeros((long, 8, depth), jnp.float32)

    for side, (middle, rim) in enumerate(((low_x, low_xy), (high_x, high_xy))):
        for field in range(FIELDS):
            for layer in range(HALO_X):
                plane = side * HALO_X + layer
                halo_ref[field, plane, HALO : HALO + cols, :] = middle[field, layer * cols : (layer + 1) * cols, :]
                row = layer * 2 * HALO
                halo_ref[field, plane, :HALO, :] = rim[field, row : row + HALO, :]
                halo_ref[field, plane, HALO + cols :, :] = rim[field, row + HALO : row + 2 * HALO, :]

    def given(field, plane, begin=0, count=wide):
        if plane in own:
            row = (plane - HALO_X) * wide + begin
            return ext[field, row : row + count, :]
        return halo_ref[field, plane if plane < HALO_X else plane - rows, begin : begin + count, :]

    def fields(plane, begin=0, count=wide):
        if plane in own:
            return field_in[plane - HALO_X, 8 + begin : 8 + begin + count, :]
        return field_ref[plane, 8 + begin : 8 + begin + count, :]

    def inverses(plane):
        return inverse_in[plane - HALO_X] if HALO_X < plane < HALO_X + rows else inverse_ref[plane]

    def is_inner(level, plane):
        return HALO_X + 1 + level <= plane <= HALO_X + rows - 1 - level

    def p(level, component, plane, begin=0, count=wide):
        if is_inner(level, plane):
            return p_in[level, component, plane - shift, begin : begin + count, :]
        return p_ref[level, component, plane, begin : begin + count, :]

    def w(level, component, plane, begin=0, count=wide):
        if is_inner(level, plane):
            return w_in[level, component, plane - shift, begin : begin + count, :]
        if level == 0:
            return given(2 + component, plane, begin, count)
        return w_ref[level, component, plane, begin : begin + count, :]

    def set_p(level, component, plane, value):
        p_ref[level, component, plane] = value

    def set_w(level, component, plane, value):
        w_ref[level, component, plane] = value

    sides = [
        Stages(shape, fields, inverses, p, w, set_p, set_w, z_ref, both[0], both[1], both[2]),
        Stages(shape, fields, inverses, p, w, set_p, set_w, z_ref, both[3], both[4], both[5]),
    ]
    for plane in range(long):
        if plane not in own:
            field_ref[plane, 8:, :] = moduli_of(given(0, plane))
    edge_planes = [*range(1, HALO_X + 1), *range(HALO_X + rows, long)]
    for plane in edge_planes:
        around = fields(plane - 1) + fields(plane - 1, -1)
        if plane - 1 in cuts:
            around = around * cuts[plane - 1]
        around = around + (fields(plane) + fields(plane, -1))
        inverse = inverse_of(given(1, plane), sides[0].lift_moduli(around))
        inverse_ref[plane] = inverse
        for component in range(3):
            set_p(0, component, plane, given(2 + component, plane) * inverse)
    for plane in edge_planes:
        sides[0].produce(0, plane, plane)

    steps = HALO_X + 1
    for level in range(BASIS - 1):
        starts = 1 + level, HALO_X + rows - 2 - level
        wanted = 2 + level, HALO_X + rows - 1 - level
        for plane in (HALO_X + 1 + level, HALO_X + 2 + level, HALO_X + rows - 2 - level, HALO_X + rows - 1 - level):
            sides[0].produce(level, plane, plane)
        for side, start in zip(sides, starts):
            side.begin(start)
        for step in range(steps + 2):
            for side, start, least in zip(sides, starts, wanted):
                plane = start + step
                if least <= plane - 2 < start + steps:
                    side.produce(level + 1, plane - 2, plane - 2)
                if least <= plane - 1 < start + steps:
                    side.finish(level, plane - 1)
                if plane < start + steps:
                    side.spread(plane, plane + 1, cuts.get(plane))

    last = BASIS - 1
    for plane in (HALO_X + 1 + last, HALO_X + rows - 1 - last):
        sides[0].produce(last, plane, plane)
    totals = [totals_in[index] for index in range(len(PAIR_LIST) + 1)]
    for plane in own:
        if not is_inner(last, plane):
            totals = add_dots(
                totals,
                lambda level, component: p(level, component, plane, HALO, cols),
                lambda level, component: w(level, component, plane, HALO, cols),
            )
        if not (is_inner(last, plane) and is_inner(last, plane + 1)):
            before = load_modes(z_ref, plane, HALO, cols)
            after = cut_off(load_modes(z_ref, plane + 1, HALO, cols), cuts.get(plane))
            energy = unit_energy(element_modes(before, after))
            totals[-1] = totals[-1] + fields(plane, HALO, cols) * energy
    slots = lane_index((1, 128))
    line = jnp.zeros((1, 128), jnp.float32)
    for index, total in enumerate(totals):
        share = jnp.sum(jnp.sum(total, axis=0, keepdims=True), axis=1, keepdims=True)
        line = line + jnp.where(slots == index, share, 0.0)
    sums_out[...] = jnp.broadcast_to(line, sums_out.shape)


def coefficients(shares):
    line = jnp.sum(shares, axis=0, keepdims=True)
    slots = lane_index(line.shape)

    def entry(index):
        return jnp.sum(jnp.where(slots == index, line, 0.0), axis=1, keepdims=True)

    inner = {}
    for index, (i, j) in enumerate(PAIR_LIST):
        inner[i, j] = inner[j, i] = entry(index)
    energy = {(BASIS - 1, BASIS - 1): entry(len(PAIR_LIST))}
    for i in range(BASIS):
        for j in range(min(i + 1, BASIS - 1)):
            energy[i, j] = inner[i, j + 1] + inner[i, j]
    lower, pivot, inverse, solved = {}, {}, {}, {}
    for k in range(BASIS):
        left = energy[k, k]
        for m in range(k):
            left = left - lower[k, m] * lower[k, m] * pivot[m]
        sound = left > 1e-6 * energy[k, k]
        pivot[k] = jnp.where(sound, left, 0.0)
        inverse[k] = jnp.where(sound, 1.0 / jnp.where(sound, left, 1.0), 0.0)
        for i in range(k + 1, BASIS):
            part = energy[i, k]
            for m in range(k):
                part = part - lower[i, m] * lower[k, m] * pivot[m]
            lower[i, k] = part * inverse[k]
    for k in range(BASIS):
        part = inner[k, 0]
        for m in range(k):
            part = part - lower[k, m] * solved[m]
        solved[k] = part
    result = {}
    for k in reversed(range(BASIS)):
        part = solved[k] * inverse[k]
        for m in range(k + 1, BASIS):
            part = part - lower[m, k] * result[m]
        result[k] = part
    return [result[k] for k in range(BASIS)]


def energy_kernel(
    shape, shares, inner, outer, own, low_x, high_x, displacement, weighted, low, high, u_ref, own_ref, z_ref, sent
):
    rows, cols, depth = shape
    wide, planes = cols + 2 * HALO, rows + 2 * REACH
    keep_last = jnp.where(lane_index((wide, depth)) < depth - 1, 1.0, 0.0)
    parts = [jnp.broadcast_to(part, (wide, depth)) for part in coefficients(shares[...])]
    cuts = grid_cuts(rows)
    for plane in range(planes + 1):
        source = plane + HALO_X - REACH
        for component in range(3):
            total = None
            for level in range(BASIS):
                if HALO_X + 1 + level <= source <= HALO_X + rows - 1 - level:
                    term = parts[level] * inner[level, component, source - HALO_X + 1]
                else:
                    term = parts[level] * outer[level, component, source]
                total = term if total is None else total + term
            lifted = pltpu.roll(total, depth - 1, 1) * keep_last
            z_ref[component, 0, plane] = lifted + total
            z_ref[component, 1, plane] = lifted - total
            row = plane - REACH
            if 0 <= row < rows:
                u_ref[component, row] = total
                own_ref[component, row] = u_ref[component, row, HALO : HALO + cols, :]
    copy = pltpu.make_async_copy(own_ref, displacement, sent.at[0])
    copy.start()
    before = load_modes(z_ref, 0, HALO, cols)
    for plane in range(planes):
        row = plane - REACH
        after = load_modes(z_ref, plane + 1, HALO, cols)
        energy = unit_energy(element_modes(before, cut_off(after, cuts.get(row + HALO_X))))
        before = after
        if row < 0:
            rho = low_x[0, (row + HALO_X) * cols : (row + HALO_X + 1) * cols, :]
        elif row < rows:
            rho = own[0, row * cols : (row + 1) * cols, :]
        else:
            rho = high_x[0, (row - rows) * cols : (row - rows + 1) * cols, :]
        weighted[plane * cols : (plane + 1) * cols, :] = rho * (3.0 * rho * rho * (1.0 - E_MIN) * energy)
    for layer in range(REACH):
        low[layer] = weighted[pl.ds(layer, planes, stride=cols), :]
        high[layer] = weighted[pl.ds(cols - REACH + layer, planes, stride=cols), :]
    copy.wait()


def cone_table():
    table, total = {}, 0.0
    for a in range(-2, 3):
        for b in range(-2, 3):
            for c in range(-2, 3):
                total += max(0.0, 3.0 - math.sqrt(a * a + b * b + c * c))
    for flat in (0, 1, 2, 4, 5, 8):
        for c in range(3):
            table[flat, c] = max(0.0, 3.0 - math.sqrt(flat + c * c))
    return table, total


def volume_row(total):
    return jnp.sum(total, axis=0, keepdims=True)


def filter_kernel(shape, weighted, from_low, from_high, own, lower, upper, root, volume, plane_ref):
    rows, cols, depth = shape
    wide, planes = cols + 8, rows + 2 * REACH
    table, total = cone_table()
    for plane in range(planes):
        plane_ref[plane * wide + REACH : plane * wide + REACH + cols, :] = weighted[plane * cols : (plane + 1) * cols, :]
    for layer in range(REACH):
        plane_ref[pl.ds(layer, planes, stride=wide), :] = from_low[layer]
        plane_ref[pl.ds(REACH + cols + layer, planes, stride=wide), :] = from_high[layer]
    volume_sum = jnp.zeros((cols, depth), jnp.float32)
    for row in range(rows):
        spread = {}
        for a in range(-REACH, REACH + 1):
            for b in range(-REACH, REACH + 1):
                key = a * a + b * b
                value = plane_ref[pl.ds((row + REACH + a) * wide + REACH + b, cols), :]
                spread[key] = value if key not in spread else spread[key] + value
        sums = []
        for c in range(3):
            part = None
            for key, value in spread.items():
                if table[key, c] > 0.0:
                    term = table[key, c] * value
                    part = term if part is None else part + term
            sums.append(part)
        convolved = sums[0]
        for c in (1, 2):
            convolved = convolved + (pltpu.roll(sums[c], c, 1) + pltpu.roll(sums[c], depth - c, 1))
        window = slice(row * cols, (row + 1) * cols)
        rho = own[0, window, :]
        base = rho * jnp.sqrt(convolved / (total * rho))
        root[window, :] = base
        volume_sum = volume_sum + jnp.minimum(jnp.maximum(base, lower[window, :]), upper[window, :])
    volume[...] = jnp.broadcast_to(volume_row(volume_sum), volume.shape)


def scale_of(target, volumes):
    scale = None
    for volume in volumes:
        whole = jnp.sum(jnp.sum(volume[...], axis=0, keepdims=True), axis=1, keepdims=True)
        ratio = target / whole
        scale = ratio if scale is None else scale * ratio
    return scale


def trial_kernel(target, steps, final, *refs):
    volumes, (root, lower, upper, out) = refs[:steps], refs[steps:]
    scale = scale_of(target, volumes)
    moved = jnp.minimum(jnp.maximum(root[...] * scale, lower[...]), upper[...])
    if final:
        out[...] = moved
    else:
        out[...] = jnp.broadcast_to(volume_row(moved), out.shape)


def call(kernel, name, out_shapes, *args, scratch=(), flops=0, space=pltpu.VMEM, far=()):
    shapes = [jax.ShapeDtypeStruct(shape, jnp.float32) for shape in out_shapes]
    moved = sum(4 * math.prod(value.shape) for value in [*args, *shapes])
    return pl.pallas_call(
        kernel,
        name=name,
        out_shape=shapes,
        in_specs=[pl.BlockSpec(memory_space=space)] * len(args),
        out_specs=[pl.BlockSpec(memory_space=pltpu.HBM if i in far else pltpu.VMEM) for i in range(len(shapes))],
        scratch_shapes=[pltpu.VMEM(item, jnp.float32) if isinstance(item, tuple) else item for item in scratch],
        compiler_params=pltpu.CompilerParams(vmem_limit_bytes=VMEM_LIMIT),
        cost_estimate=pl.CostEstimate(flops=flops, bytes_accessed=moved, transcendentals=0),
    )(*args)


def exchange(low, high, axis, wrap):
    count = lax.axis_size(axis)
    ends = count if wrap else count - 1
    from_low = lax.ppermute(high, axis, [(i, (i + 1) % count) for i in range(ends)])
    from_high = lax.ppermute(low, axis, [((i + 1) % count, i) for i in range(ends)])
    return from_low, from_high


def everyone(shares):
    return lax.all_to_all(shares, AXES, 0, 0, tiled=True)


def shards(density, void_mask, solid_mask, fixed_mask, load_mask, traction):
    shape = rows, cols, depth = density.shape
    devices = lax.axis_size("gx") * lax.axis_size("gy")
    wide, long = cols + 2 * HALO, rows + 2 * HALO_X
    planes = rows + 2 * REACH
    named = lambda kernel: functools.partial(kernel, shape)
    flat = (rows * cols, depth)
    inputs = [
        pltpu.with_memory_space_constraint(value.reshape(*value.shape[:-3], *flat), pltpu.HBM)
        for value in (density, void_mask, solid_mask, fixed_mask, load_mask, traction)
    ]

    own, lower, upper, low, high, low_x, high_x = call(
        named(fields_kernel),
        "fields",
        [
            (FIELDS, *flat),
            flat,
            flat,
            (len(HIGH_HALO), rows, depth),
            (len(LOW_HALO), rows, depth),
            (FIELDS, HALO_X * cols, depth),
            (FIELDS, HALO_X * cols, depth),
        ],
        *inputs,
        scratch=[pltpu.VMEM(value.shape, value.dtype) for value in inputs] + [pltpu.SemaphoreType.DMA((6,))],
        space=pltpu.HBM,
    )
    from_low, from_high = exchange(low, high, "gy", False)
    low_x, high_x = exchange(low_x, high_x, "gx", True)
    ext, low, high = call(
        named(widen_kernel),
        "widen",
        [(FIELDS, rows * wide, depth)] + [(FIELDS, HALO_X * 2 * HALO, depth)] * 2,
        own,
        from_low,
        from_high,
    )
    low_xy, high_xy = exchange(low, high, "gx", True)
    side = [(12, wide, depth), (12, wide, depth), (3, 2, wide, depth)]
    inner = call(
        named(inner_kernel),
        "inner",
        [
            (BASIS, 3, rows + 1, wide, depth),
            (BASIS, 3, rows + 1, wide, depth),
            (rows, 8 + wide, depth),
            (rows, wide, depth),
            (len(PAIR_LIST) + 1, cols, depth),
        ],
        ext,
        scratch=[(3, 2, rows + 1, wide + 8, depth), *side],
    )
    outer, sums = call(
        named(outer_kernel),
        "outer",
        [(BASIS, 3, long, wide, depth), (devices, 128)],
        ext,
        low_x,
        high_x,
        low_xy,
        high_xy,
        *inner,
        scratch=[
            (FIELDS, 2 * HALO_X, wide, depth),
            (long, 8 + wide, depth),
            (long, wide, depth),
            (BASIS, 3, long, wide, depth),
            (3, 2, long, wide + 8, depth),
            *side,
            *side,
        ],
    )
    displacement, weighted, low, high = call(
        named(energy_kernel),
        "energy",
        [(3, rows, cols, depth), (planes * cols, depth), (REACH, planes, depth), (REACH, planes, depth)],
        everyone(sums),
        inner[0],
        outer,
        own,
        low_x,
        high_x,
        scratch=[
            (3, rows, wide, depth),
            (3, rows, cols, depth),
            (3, 2, planes + 1, wide, depth),
            pltpu.SemaphoreType.DMA((1,)),
        ],
        far=(0,),
    )
    from_low, from_high = exchange(low, high, "gy", True)
    root, volume = call(
        named(filter_kernel),
        "filter",
        [flat, (devices, depth)],
        weighted,
        from_low,
        from_high,
        own,
        lower,
        upper,
        scratch=[(planes * (cols + 8), depth)],
    )
    target = VOLUME_SHARE * rows * cols * depth * devices
    terms, volumes = (root, lower, upper), [everyone(volume)]
    for step in (1, 2):
        (volume,) = call(
            functools.partial(trial_kernel, target, step, False), "trial", [(devices, depth)], *volumes, *terms
        )
        volumes.append(everyone(volume))
    (new_density,) = call(functools.partial(trial_kernel, target, 3, True), "update", [flat], *volumes, *terms)
    return new_density.reshape(shape), displacement


def solution(mesh):
    placed = (P("gx", "gy", None),) * 5 + (P(None, "gx", "gy", None),)
    return jax.shard_map(
        shards,
        mesh=mesh,
        in_specs=placed,
        out_specs=(P("gx", "gy", None), P(None, "gx", "gy", None)),
        check_vma=False,
    )
```

```python
import functools
import math

import jax
import jax.numpy as jnp
import numpy as np
from jax import lax
from jax.experimental import pallas as pl
from jax.experimental.pallas import tpu as pltpu
from jax.sharding import PartitionSpec as P

E_MIN = 0.001
RHO_FLOOR = 0.001
MOVE_LIMIT = 0.2
VOLUME_SHARE = 0.4
BASIS = 4
REACH = 2
HALO = BASIS
HALO_X = BASIS + REACH
AXES = ("gx", "gy")
FIELDS = 5
LOW_HALO = [(layer, field) for layer in range(HALO) for field in range(FIELDS) if layer > 0 or field == 0]
HIGH_HALO = [(layer, field) for layer in range(HALO) for field in range(FIELDS)]
VMEM_LIMIT = 40 * 1024 * 1024

POISSON = 0.3
LAME = POISSON / ((1.0 + POISSON) * (1.0 - 2.0 * POISSON))
SHEAR = 1.0 / (2.0 * (1.0 + POISSON))
NORMAL = 2.0 * SHEAR / 16.0
TRACE = LAME / 16.0
SHEAR_FIRST = SHEAR / 16.0
BEND = (LAME + 3.0 * SHEAR) / 48.0
BEND_MIX = LAME / 48.0
TWIST = SHEAR / 48.0
THIRD = (LAME + 4.0 * SHEAR) / 144.0
DIAGONAL = NORMAL + TRACE + 2.0 * SHEAR_FIRST + 2.0 * BEND + 2.0 * TWIST + THIRD
PAIRS = (("xdds", "zsdd"), ("ydds", "zdsd"), ("xdsd", "ysdd"))
TRIPLE = ("zdds", "ydsd", "xsdd")
CLASSES = [c + y + z for c in "xyz" for y in "sd" for z in "sd"]


def lane_index(shape):
    return lax.broadcasted_iota(jnp.int32, shape, len(shape) - 1)


def load_modes(z_ref, plane, begin, count):
    modes = {}
    for number, component in enumerate("xyz"):
        for index, z in enumerate("sd"):
            low = z_ref[number, index, plane, begin : begin + count, :]
            high = z_ref[number, index, plane, begin + 1 : begin + 1 + count, :]
            modes[component + "s" + z] = high + low
            modes[component + "d" + z] = high - low
    return modes


def element_modes(before, after):
    modes = {}
    for key in CLASSES:
        if key[1:] != "ss":
            modes[key[0] + "s" + key[1:]] = after[key] + before[key]
        modes[key[0] + "d" + key[1:]] = after[key] - before[key]
    return modes


def mode_forces(u, moduli):
    forces = {}
    normal = moduli * NORMAL
    trace = (u["xdss"] + u["ysds"] + u["zssd"]) * (TRACE / NORMAL)
    for key in ("xdss", "ysds", "zssd"):
        forces[key] = normal * (u[key] + trace)
    shear = moduli * SHEAR_FIRST
    for one, other in (("ydss", "xsds"), ("zsds", "yssd"), ("xssd", "zdss")):
        forces[one] = forces[other] = shear * (u[one] + u[other])
    bend = moduli * BEND
    for one, other in PAIRS:
        forces[one] = bend * (u[one] + (BEND_MIX / BEND) * u[other])
        forces[other] = bend * (u[other] + (BEND_MIX / BEND) * u[one])
    twist = moduli * TWIST
    total = u[TRIPLE[0]] + u[TRIPLE[1]] + u[TRIPLE[2]]
    for key in TRIPLE:
        forces[key] = twist * (total + u[key])
    third = moduli * THIRD
    for component in "xyz":
        forces[component + "ddd"] = third * u[component + "ddd"]
    return forces


def unit_energy(u):
    trace = u["xdss"] + u["ysds"] + u["zssd"]
    energy = TRACE * (trace * trace)
    energy += NORMAL * (u["xdss"] ** 2 + u["ysds"] ** 2 + u["zssd"] ** 2)
    shears = [u[a] + u[b] for a, b in (("ydss", "xsds"), ("zsds", "yssd"), ("xssd", "zdss"))]
    energy += SHEAR_FIRST * (shears[0] ** 2 + shears[1] ** 2 + shears[2] ** 2)
    squares, mixed = 0.0, 0.0
    for one, other in PAIRS:
        squares += u[one] ** 2 + u[other] ** 2
        mixed += (u[one] + u[other]) ** 2
    energy += (BEND - BEND_MIX) * squares + BEND_MIX * mixed
    total = u[TRIPLE[0]] + u[TRIPLE[1]] + u[TRIPLE[2]]
    squares = total * total
    for key in TRIPLE:
        squares += u[key] ** 2
    energy += TWIST * squares
    energy += THIRD * (u["xddd"] ** 2 + u["yddd"] ** 2 + u["zddd"] ** 2)
    return energy


def fields_kernel(shape, *refs):
    rows, cols, _ = shape
    sources, (own, lower, upper, low, high, low_x, high_x) = refs[:6], refs[6:13]
    *local, arrived = refs[13:]
    pieces = [(source, target) for source, target in zip(sources[:5], local)]
    pieces += [(sources[5].at[component], local[5].at[component]) for component in range(3)]
    copies = [pltpu.make_async_copy(s, t, arrived.at[i]) for i, (s, t) in enumerate(pieces)]
    for copy in copies:
        copy.start()
    for copy in copies:
        copy.wait()
    density, void, solid, fixed, load, traction = local
    is_solid, is_void = solid[...] == 1, void[...] == 1
    rho = jnp.where(is_solid, 1.0, jnp.where(is_void, RHO_FLOOR, density[...]))
    own[0] = rho
    free = (1 - fixed[...]).astype(jnp.float32)
    own[1] = free
    loaded = free * load[...].astype(jnp.float32)
    for component in range(3):
        own[2 + component] = loaded * traction[component]
    for index, (layer, field) in enumerate(HIGH_HALO):
        low[index] = own[field, pl.ds(layer, rows, stride=cols), :]
    for index, (layer, field) in enumerate(LOW_HALO):
        high[index] = own[field, pl.ds(cols - HALO + layer, rows, stride=cols), :]
    low_x[...] = own[:, : HALO_X * cols, :]
    high_x[...] = own[:, (rows - HALO_X) * cols :, :]
    least = jnp.maximum(RHO_FLOOR, rho - MOVE_LIMIT)
    most = jnp.minimum(1.0, rho + MOVE_LIMIT)
    lower[...] = jnp.where(is_solid, 1.0, jnp.where(is_void, RHO_FLOOR, least))
    upper[...] = jnp.where(is_solid, 1.0, jnp.where(is_void, RHO_FLOOR, most))


def widen_kernel(shape, own, from_low, from_high, ext, low, high):
    rows, cols, depth = shape
    wide = cols + 2 * HALO
    for field in range(FIELDS):
        for row in range(rows):
            ext[field, pl.ds(row * wide + HALO, cols), :] = own[field, pl.ds(row * cols, cols), :]
        for layer in range(HALO):
            for entries, source, shift in ((LOW_HALO, from_low, 0), (HIGH_HALO, from_high, HALO)):
                if (layer, field) in entries:
                    index = entries.index((layer, field))
                    whole = source[index]
                    begin, end = source[index, :HALO_X], source[index, rows - HALO_X :]
                else:
                    whole = jnp.zeros((rows, depth), jnp.float32)
                    begin = end = jnp.zeros((HALO_X, depth), jnp.float32)
                row = layer if shift == 0 else cols + HALO + layer
                ext[field, pl.ds(row, rows, stride=wide), :] = whole
                low[field, pl.ds(shift + layer, HALO_X, stride=2 * HALO), :] = begin
                high[field, pl.ds(shift + layer, HALO_X, stride=2 * HALO), :] = end


def grid_cuts(rows):
    place, last = lax.axis_index("gx"), lax.axis_size("gx") - 1
    return {
        HALO_X - 1: jnp.where(place == 0, 0.0, 1.0),
        HALO_X + rows - 1: jnp.where(place == last, 0.0, 1.0),
    }


def cut_off(values, keep):
    return values if keep is None else {key: value * keep for key, value in values.items()}


class Stages:
    def __init__(self, shape, fields, inverses, p, w, set_p, set_w, z_ref, mode_ref, lift_ref, pipe_ref):
        self.wide, self.depth = shape[1] + 2 * HALO, shape[2]
        lanes = lane_index((self.wide, self.depth))
        self.keep_last = jnp.where(lanes < self.depth - 1, 1.0, 0.0)
        self.keep_first = jnp.where(lanes > 0, 1.0, 0.0)
        self.fields, self.inverses, self.p, self.w = fields, inverses, p, w
        self.set_p, self.set_w = set_p, set_w
        self.z_ref, self.mode_ref, self.lift_ref, self.pipe_ref = z_ref, mode_ref, lift_ref, pipe_ref

    def lift_moduli(self, around):
        return around + pltpu.roll(around, 1, 1) * self.keep_first

    def produce(self, level, plane, slot):
        for component in range(3):
            value = self.p(level, component, plane)
            lifted = pltpu.roll(value, self.depth - 1, 1) * self.keep_last
            self.z_ref[component, 0, slot, : self.wide] = lifted + value
            self.z_ref[component, 1, slot, : self.wide] = lifted - value

    def begin(self, slot):
        modes = load_modes(self.z_ref, slot, 0, self.wide)
        for index, key in enumerate(CLASSES):
            self.mode_ref[index] = modes[key]
            self.lift_ref[index] = jnp.zeros((self.wide, self.depth), jnp.float32)

    def spread(self, plane, slot, keep=None):
        after = load_modes(self.z_ref, slot, 0, self.wide)
        before = {key: self.mode_ref[index] for index, key in enumerate(CLASSES)}
        lift = {key: self.lift_ref[index] for index, key in enumerate(CLASSES)}
        forces = mode_forces(element_modes(before, cut_off(after, keep)), self.fields(plane))
        for number, component in enumerate("xyz"):
            along_z = {}
            for z in "sd":
                along_y = {}
                for y in "sd":
                    key = component + y + z
                    slope = forces[component + "d" + y + z]
                    if y + z == "ss":
                        along_y[y] = lift[key] - slope
                        lift[key] = slope
                    else:
                        mean = forces[component + "s" + y + z]
                        along_y[y] = lift[key] + (mean - slope)
                        lift[key] = mean + slope
                along_z[z] = (along_y["s"] - along_y["d"]) + pltpu.roll(along_y["s"] + along_y["d"], 1, 0)
            self.pipe_ref[number, 0] = along_z["s"] + along_z["d"]
            self.pipe_ref[number, 1] = along_z["s"] - along_z["d"]
        lift = cut_off(lift, keep)
        for index, key in enumerate(CLASSES):
            self.mode_ref[index] = after[key]
            self.lift_ref[index] = lift[key]

    def finish(self, level, plane):
        for component in range(3):
            shifted = pltpu.roll(self.pipe_ref[component, 0], 1, 1) * self.keep_first
            residual = (self.pipe_ref[component, 1] + shifted) - self.w(level, component, plane)
            self.set_w(level + 1, component, plane, residual)
            self.set_p(level + 1, component, plane, residual * self.inverses(plane))


def sweep(level, sides, cuts, shift):
    for side, start, count, wanted in sides:
        side.begin(start - shift)
    for step in range(max(count for _, _, count, _ in sides) + 2):
        for side, start, count, wanted in sides:
            plane, end = start + step, start + count
            if wanted <= plane - 2 < end:
                side.produce(level + 1, plane - 2, plane - 2 - shift)
            if wanted <= plane - 1 < end:
                side.finish(level, plane - 1)
            if plane < end:
                side.spread(plane, plane + 1 - shift, cuts.get(plane))


def moduli_of(rho):
    return jnp.where(rho > 0.0, E_MIN + rho * rho * rho * (1.0 - E_MIN), 0.0)


def inverse_of(free, around):
    return free / (free * (DIAGONAL * around) + (1.0 - free))


PAIR_LIST = [(i, j) for i in range(BASIS) for j in range(i + 1)]


def inner_kernel(shape, ext, p_ref, w_ref, field_ref, inverse_ref, totals_ref, z_ref, mode_ref, lift_ref, pipe_ref):
    rows, cols, depth = shape
    wide, shift = cols + 2 * HALO, HALO_X - 1
    field_ref[:, :8, :] = jnp.zeros((rows, 8, depth), jnp.float32)
    z_ref[:, :, :, wide:, :] = jnp.zeros((3, 2, z_ref.shape[2], 8, depth), jnp.float32)
    for row in range(rows):
        window = slice(row * wide, (row + 1) * wide)
        field_ref[row, 8:, :] = moduli_of(ext[0, window, :])
        for component in range(3):
            w_ref[0, component, row + 1] = ext[2 + component, window, :]

    def store(ref):
        def put(level, component, plane, value):
            ref[level, component, plane - shift] = value

        return put

    stages = Stages(
        shape,
        lambda plane: field_ref[plane - HALO_X, 8:, :],
        lambda plane: inverse_ref[plane - HALO_X],
        lambda level, component, plane: p_ref[level, component, plane - shift],
        lambda level, component, plane: w_ref[level, component, plane - shift],
        store(p_ref),
        store(w_ref),
        z_ref,
        mode_ref,
        lift_ref,
        pipe_ref,
    )
    inverse_ref[0] = jnp.zeros((wide, depth), jnp.float32)
    for row in range(1, rows):
        around = field_ref[row - 1, 8:, :] + field_ref[row - 1, 7 : 7 + wide, :]
        around = around + (field_ref[row, 8:, :] + field_ref[row, 7 : 7 + wide, :])
        inverse = inverse_of(ext[1, row * wide : (row + 1) * wide, :], stages.lift_moduli(around))
        inverse_ref[row] = inverse
        for component in range(3):
            p_ref[0, component, row + 1] = w_ref[0, component, row + 1] * inverse
    for row in range(1, rows):
        stages.produce(0, row + HALO_X, row + 1)

    for level in range(BASIS - 1):
        start, count = HALO_X + 1 + level, rows - 2 - 2 * level
        sweep(level, [(stages, start, count, start + 1)], {}, shift)

    first, last = HALO_X + BASIS, HALO_X + rows - 1 - (BASIS - 1)
    totals = [jnp.zeros((cols, depth), jnp.float32)] * (len(PAIR_LIST) + 1)
    before = load_modes(z_ref, first - shift, HALO, cols)
    for plane in range(first, last + 1):
        totals = add_dots(
            totals,
            lambda level, component: p_ref[level, component, plane - shift, HALO : HALO + cols, :],
            lambda level, component: w_ref[level, component, plane - shift, HALO : HALO + cols, :],
        )
        if plane < last:
            after = load_modes(z_ref, plane + 1 - shift, HALO, cols)
            energy = unit_energy(element_modes(before, after))
            totals[-1] = totals[-1] + field_ref[plane - HALO_X, 8 + HALO : 8 + HALO + cols, :] * energy
            before = after
    for index, total in enumerate(totals):
        totals_ref[index] = total


def add_dots(totals, p, w):
    totals = list(totals)
    for component in range(3):
        ps = [p(level, component) for level in range(BASIS)]
        ws = [w(level, component) for level in range(BASIS)]
        for index, (i, j) in enumerate(PAIR_LIST):
            totals[index] = totals[index] + ps[i] * ws[j]
    return totals


def outer_kernel(
    shape, ext, low_x, high_x, low_xy, high_xy, p_in, w_in, field_in, inverse_in, totals_in, p_ref, sums_out, *scratch
):
    rows, cols, depth = shape
    wide, long, shift = cols + 2 * HALO, rows + 2 * HALO_X, HALO_X - 1
    halo_ref, field_ref, inverse_ref, w_ref, z_ref, *both = scratch
    cuts = grid_cuts(rows)
    own = range(HALO_X, HALO_X + rows)
    z_ref[:, :, :, wide:, :] = jnp.zeros((3, 2, long, 8, depth), jnp.float32)
    field_ref[:, :8, :] = jnp.zeros((long, 8, depth), jnp.float32)

    for side, (middle, rim) in enumerate(((low_x, low_xy), (high_x, high_xy))):
        for field in range(FIELDS):
            for layer in range(HALO_X):
                plane = side * HALO_X + layer
                halo_ref[field, plane, HALO : HALO + cols, :] = middle[field, layer * cols : (layer + 1) * cols, :]
                row = layer * 2 * HALO
                halo_ref[field, plane, :HALO, :] = rim[field, row : row + HALO, :]
                halo_ref[field, plane, HALO + cols :, :] = rim[field, row + HALO : row + 2 * HALO, :]

    def given(field, plane, begin=0, count=wide):
        if plane in own:
            row = (plane - HALO_X) * wide + begin
            return ext[field, row : row + count, :]
        return halo_ref[field, plane if plane < HALO_X else plane - rows, begin : begin + count, :]

    def fields(plane, begin=0, count=wide):
        if plane in own:
            return field_in[plane - HALO_X, 8 + begin : 8 + begin + count, :]
        return field_ref[plane, 8 + begin : 8 + begin + count, :]

    def inverses(plane):
        return inverse_in[plane - HALO_X] if HALO_X < plane < HALO_X + rows else inverse_ref[plane]

    def is_inner(level, plane):
        return HALO_X + 1 + level <= plane <= HALO_X + rows - 1 - level

    def p(level, component, plane, begin=0, count=wide):
        if is_inner(level, plane):
            return p_in[level, component, plane - shift, begin : begin + count, :]
        return p_ref[level, component, plane, begin : begin + count, :]

    def w(level, component, plane, begin=0, count=wide):
        if is_inner(level, plane):
            return w_in[level, component, plane - shift, begin : begin + count, :]
        if level == 0:
            return given(2 + component, plane, begin, count)
        return w_ref[level, component, plane, begin : begin + count, :]

    def set_p(level, component, plane, value):
        p_ref[level, component, plane] = value

    def set_w(level, component, plane, value):
        w_ref[level, component, plane] = value

    sides = [
        Stages(shape, fields, inverses, p, w, set_p, set_w, z_ref, both[0], both[1], both[2]),
        Stages(shape, fields, inverses, p, w, set_p, set_w, z_ref, both[3], both[4], both[5]),
    ]
    for plane in range(long):
        if plane not in own:
            field_ref[plane, 8:, :] = moduli_of(given(0, plane))
    edge_planes = [*range(1, HALO_X + 1), *range(HALO_X + rows, long)]
    for plane in edge_planes:
        around = fields(plane - 1) + fields(plane - 1, -1)
        if plane - 1 in cuts:
            around = around * cuts[plane - 1]
        around = around + (fields(plane) + fields(plane, -1))
        inverse = inverse_of(given(1, plane), sides[0].lift_moduli(around))
        inverse_ref[plane] = inverse
        for component in range(3):
            set_p(0, component, plane, given(2 + component, plane) * inverse)
    for plane in edge_planes:
        sides[0].produce(0, plane, plane)

    count = HALO_X + 1
    for level in range(BASIS - 1):
        for plane in (HALO_X + 1 + level, HALO_X + 2 + level, HALO_X + rows - 2 - level, HALO_X + rows - 1 - level):
            sides[0].produce(level, plane, plane)
        left, right = 1 + level, HALO_X + rows - 2 - level
        sweep(level, [(sides[0], left, count, left + 1), (sides[1], right, count, right + 1)], cuts, 0)

    last = BASIS - 1
    for plane in (HALO_X + 1 + last, HALO_X + rows - 1 - last):
        sides[0].produce(last, plane, plane)
    totals = [totals_in[index] for index in range(len(PAIR_LIST) + 1)]
    for plane in own:
        if not is_inner(last, plane):
            totals = add_dots(
                totals,
                lambda level, component: p(level, component, plane, HALO, cols),
                lambda level, component: w(level, component, plane, HALO, cols),
            )
        if not (is_inner(last, plane) and is_inner(last, plane + 1)):
            before = load_modes(z_ref, plane, HALO, cols)
            after = cut_off(load_modes(z_ref, plane + 1, HALO, cols), cuts.get(plane))
            energy = unit_energy(element_modes(before, after))
            totals[-1] = totals[-1] + fields(plane, HALO, cols) * energy
    slots = lane_index((1, 128))
    line = jnp.zeros((1, 128), jnp.float32)
    for index, total in enumerate(totals):
        share = jnp.sum(jnp.sum(total, axis=0, keepdims=True), axis=1, keepdims=True)
        line = line + jnp.where(slots == index, share, 0.0)
    sums_out[...] = jnp.broadcast_to(line, sums_out.shape)


def coefficients(shares):
    line = jnp.sum(shares, axis=0, keepdims=True)
    slots = lane_index(line.shape)

    def entry(index):
        return jnp.sum(jnp.where(slots == index, line, 0.0), axis=1, keepdims=True)

    inner = {}
    for index, (i, j) in enumerate(PAIR_LIST):
        inner[i, j] = inner[j, i] = entry(index)
    energy = {(BASIS - 1, BASIS - 1): entry(len(PAIR_LIST))}
    for i in range(BASIS):
        for j in range(min(i + 1, BASIS - 1)):
            energy[i, j] = inner[i, j + 1] + inner[i, j]
    lower, pivot, inverse, solved = {}, {}, {}, {}
    for k in range(BASIS):
        left = energy[k, k]
        for m in range(k):
            left = left - lower[k, m] * lower[k, m] * pivot[m]
        sound = left > 1e-6 * energy[k, k]
        pivot[k] = jnp.where(sound, left, 0.0)
        inverse[k] = jnp.where(sound, 1.0 / jnp.where(sound, left, 1.0), 0.0)
        for i in range(k + 1, BASIS):
            part = energy[i, k]
            for m in range(k):
                part = part - lower[i, m] * lower[k, m] * pivot[m]
            lower[i, k] = part * inverse[k]
    for k in range(BASIS):
        part = inner[k, 0]
        for m in range(k):
            part = part - lower[k, m] * solved[m]
        solved[k] = part
    result = {}
    for k in reversed(range(BASIS)):
        part = solved[k] * inverse[k]
        for m in range(k + 1, BASIS):
            part = part - lower[m, k] * result[m]
        result[k] = part
    return [result[k] for k in range(BASIS)]


def energy_kernel(
    shape, shares, inner, outer, own, low_x, high_x, displacement, weighted, low, high, u_ref, own_ref, z_ref, sent
):
    rows, cols, depth = shape
    wide, planes = cols + 2 * HALO, rows + 2 * REACH
    keep_last = jnp.where(lane_index((wide, depth)) < depth - 1, 1.0, 0.0)
    parts = [jnp.broadcast_to(part, (wide, depth)) for part in coefficients(shares[...])]
    cuts = grid_cuts(rows)
    for plane in range(planes + 1):
        source = plane + HALO_X - REACH
        for component in range(3):
            total = None
            for level in range(BASIS):
                if HALO_X + 1 + level <= source <= HALO_X + rows - 1 - level:
                    term = parts[level] * inner[level, component, source - HALO_X + 1]
                else:
                    term = parts[level] * outer[level, component, source]
                total = term if total is None else total + term
            lifted = pltpu.roll(total, depth - 1, 1) * keep_last
            z_ref[component, 0, plane] = lifted + total
            z_ref[component, 1, plane] = lifted - total
            row = plane - REACH
            if 0 <= row < rows:
                u_ref[component, row] = total
                own_ref[component, row] = u_ref[component, row, HALO : HALO + cols, :]
    copy = pltpu.make_async_copy(own_ref, displacement, sent.at[0])
    copy.start()
    before = load_modes(z_ref, 0, HALO, cols)
    for plane in range(planes):
        row = plane - REACH
        after = load_modes(z_ref, plane + 1, HALO, cols)
        energy = unit_energy(element_modes(before, cut_off(after, cuts.get(row + HALO_X))))
        before = after
        if row < 0:
            rho = low_x[0, (row + HALO_X) * cols : (row + HALO_X + 1) * cols, :]
        elif row < rows:
            rho = own[0, row * cols : (row + 1) * cols, :]
        else:
            rho = high_x[0, (row - rows) * cols : (row - rows + 1) * cols, :]
        weighted[plane * cols : (plane + 1) * cols, :] = rho * (3.0 * rho * rho * (1.0 - E_MIN) * energy)
    for layer in range(REACH):
        low[layer] = weighted[pl.ds(layer, planes, stride=cols), :]
        high[layer] = weighted[pl.ds(cols - REACH + layer, planes, stride=cols), :]
    copy.wait()


def cone_table():
    table, total = {}, 0.0
    for a in range(-2, 3):
        for b in range(-2, 3):
            for c in range(-2, 3):
                total += max(0.0, 3.0 - math.sqrt(a * a + b * b + c * c))
    for flat in (0, 1, 2, 4, 5, 8):
        for c in range(3):
            table[flat, c] = max(0.0, 3.0 - math.sqrt(flat + c * c))
    return table, total


def volume_row(total):
    return jnp.sum(total, axis=0, keepdims=True)


def filter_kernel(shape, weighted, from_low, from_high, own, lower, upper, root, volume, plane_ref):
    rows, cols, depth = shape
    wide, planes = cols + 8, rows + 2 * REACH
    table, total = cone_table()
    for plane in range(planes):
        plane_ref[plane * wide + REACH : plane * wide + REACH + cols, :] = weighted[plane * cols : (plane + 1) * cols, :]
    for layer in range(REACH):
        plane_ref[pl.ds(layer, planes, stride=wide), :] = from_low[layer]
        plane_ref[pl.ds(REACH + cols + layer, planes, stride=wide), :] = from_high[layer]
    volume_sum = jnp.zeros((cols, depth), jnp.float32)
    for row in range(rows):
        spread = {}
        for a in range(-REACH, REACH + 1):
            for b in range(-REACH, REACH + 1):
                key = a * a + b * b
                value = plane_ref[pl.ds((row + REACH + a) * wide + REACH + b, cols), :]
                spread[key] = value if key not in spread else spread[key] + value
        sums = []
        for c in range(3):
            part = None
            for key, value in spread.items():
                if table[key, c] > 0.0:
                    term = table[key, c] * value
                    part = term if part is None else part + term
            sums.append(part)
        convolved = sums[0]
        for c in (1, 2):
            convolved = convolved + (pltpu.roll(sums[c], c, 1) + pltpu.roll(sums[c], depth - c, 1))
        window = slice(row * cols, (row + 1) * cols)
        rho = own[0, window, :]
        base = rho * jnp.sqrt(convolved / (total * rho))
        root[window, :] = base
        volume_sum = volume_sum + jnp.minimum(jnp.maximum(base, lower[window, :]), upper[window, :])
    volume[...] = jnp.broadcast_to(volume_row(volume_sum), volume.shape)


def scale_of(target, volumes):
    scale = None
    for volume in volumes:
        whole = jnp.sum(jnp.sum(volume[...], axis=0, keepdims=True), axis=1, keepdims=True)
        ratio = target / whole
        scale = ratio if scale is None else scale * ratio
    return scale


def trial_kernel(target, steps, final, *refs):
    volumes, (root, lower, upper, out) = refs[:steps], refs[steps:]
    scale = scale_of(target, volumes)
    moved = jnp.minimum(jnp.maximum(root[...] * scale, lower[...]), upper[...])
    if final:
        out[...] = moved
    else:
        out[...] = jnp.broadcast_to(volume_row(moved), out.shape)


def call(kernel, name, out_shapes, *args, scratch=(), flops=0, space=pltpu.VMEM, far=()):
    shapes = [jax.ShapeDtypeStruct(shape, jnp.float32) for shape in out_shapes]
    moved = sum(4 * math.prod(value.shape) for value in [*args, *shapes])
    return pl.pallas_call(
        kernel,
        name=name,
        out_shape=shapes,
        in_specs=[pl.BlockSpec(memory_space=space)] * len(args),
        out_specs=[pl.BlockSpec(memory_space=pltpu.HBM if i in far else pltpu.VMEM) for i in range(len(shapes))],
        scratch_shapes=[pltpu.VMEM(item, jnp.float32) if isinstance(item, tuple) else item for item in scratch],
        compiler_params=pltpu.CompilerParams(vmem_limit_bytes=VMEM_LIMIT),
        cost_estimate=pl.CostEstimate(flops=flops, bytes_accessed=moved, transcendentals=0),
    )(*args)


def exchange(low, high, axis, wrap):
    count = lax.axis_size(axis)
    ends = count if wrap else count - 1
    from_low = lax.ppermute(high, axis, [(i, (i + 1) % count) for i in range(ends)])
    from_high = lax.ppermute(low, axis, [((i + 1) % count, i) for i in range(ends)])
    return from_low, from_high


def everyone(shares):
    return lax.all_to_all(shares, AXES, 0, 0, tiled=True)


def shards(density, void_mask, solid_mask, fixed_mask, load_mask, traction):
    shape = rows, cols, depth = density.shape
    devices = lax.axis_size("gx") * lax.axis_size("gy")
    wide, long = cols + 2 * HALO, rows + 2 * HALO_X
    planes = rows + 2 * REACH
    named = lambda kernel: functools.partial(kernel, shape)
    flat = (rows * cols, depth)
    inputs = [
        pltpu.with_memory_space_constraint(value.reshape(*value.shape[:-3], *flat), pltpu.HBM)
        for value in (density, void_mask, solid_mask, fixed_mask, load_mask, traction)
    ]

    own, lower, upper, low, high, low_x, high_x = call(
        named(fields_kernel),
        "fields",
        [
            (FIELDS, *flat),
            flat,
            flat,
            (len(HIGH_HALO), rows, depth),
            (len(LOW_HALO), rows, depth),
            (FIELDS, HALO_X * cols, depth),
            (FIELDS, HALO_X * cols, depth),
        ],
        *inputs,
        scratch=[pltpu.VMEM(value.shape, value.dtype) for value in inputs] + [pltpu.SemaphoreType.DMA((8,))],
        space=pltpu.HBM,
    )
    from_low, from_high = exchange(low, high, "gy", False)
    low_x, high_x = exchange(low_x, high_x, "gx", True)
    ext, low, high = call(
        named(widen_kernel),
        "widen",
        [(FIELDS, rows * wide, depth)] + [(FIELDS, HALO_X * 2 * HALO, depth)] * 2,
        own,
        from_low,
        from_high,
    )
    low_xy, high_xy = exchange(low, high, "gx", True)
    side = [(12, wide, depth), (12, wide, depth), (3, 2, wide, depth)]
    inner = call(
        named(inner_kernel),
        "inner",
        [
            (BASIS, 3, rows + 1, wide, depth),
            (BASIS, 3, rows + 1, wide, depth),
            (rows, 8 + wide, depth),
            (rows, wide, depth),
            (len(PAIR_LIST) + 1, cols, depth),
        ],
        ext,
        scratch=[(3, 2, rows + 1, wide + 8, depth), *side],
    )
    outer, sums = call(
        named(outer_kernel),
        "outer",
        [(BASIS, 3, long, wide, depth), (devices, 128)],
        ext,
        low_x,
        high_x,
        low_xy,
        high_xy,
        *inner,
        scratch=[
            (FIELDS, 2 * HALO_X, wide, depth),
            (long, 8 + wide, depth),
            (long, wide, depth),
            (BASIS, 3, long, wide, depth),
            (3, 2, long, wide + 8, depth),
            *side,
            *side,
        ],
    )
    displacement, weighted, low, high = call(
        named(energy_kernel),
        "energy",
        [(3, rows, cols, depth), (planes * cols, depth), (REACH, planes, depth), (REACH, planes, depth)],
        everyone(sums),
        inner[0],
        outer,
        own,
        low_x,
        high_x,
        scratch=[
            (3, rows, wide, depth),
            (3, rows, cols, depth),
            (3, 2, planes + 1, wide, depth),
            pltpu.SemaphoreType.DMA((1,)),
        ],
        far=(0,),
    )
    from_low, from_high = exchange(low, high, "gy", True)
    root, volume = call(
        named(filter_kernel),
        "filter",
        [flat, (devices, depth)],
        weighted,
        from_low,
        from_high,
        own,
        lower,
        upper,
        scratch=[(planes * (cols + 8), depth)],
    )
    target = VOLUME_SHARE * rows * cols * depth * devices
    terms, volumes = (root, lower, upper), [everyone(volume)]
    for step in (1, 2):
        (volume,) = call(
            functools.partial(trial_kernel, target, step, False), "trial", [(devices, depth)], *volumes, *terms
        )
        volumes.append(everyone(volume))
    (new_density,) = call(functools.partial(trial_kernel, target, 3, True), "update", [flat], *volumes, *terms)
    return new_density.reshape(shape), displacement


def solution(mesh):
    placed = (P("gx", "gy", None),) * 5 + (P(None, "gx", "gy", None),)
    return jax.shard_map(
        shards,
        mesh=mesh,
        in_specs=placed,
        out_specs=(P("gx", "gy", None), P(None, "gx", "gy", None)),
        check_vma=False,
    )
```

```python
import functools
import math

import jax
import jax.numpy as jnp
import numpy as np
from jax import lax
from jax.experimental import pallas as pl
from jax.experimental.pallas import tpu as pltpu
from jax.sharding import PartitionSpec as P

E_MIN = 0.001
RHO_FLOOR = 0.001
MOVE_LIMIT = 0.2
VOLUME_SHARE = 0.4
BASIS = 4
REACH = 2
HALO = BASIS
HALO_X = BASIS + REACH
AXES = ("gx", "gy")
FIELDS = 5
VMEM_LIMIT = 40 * 1024 * 1024

POISSON = 0.3
LAME = POISSON / ((1.0 + POISSON) * (1.0 - 2.0 * POISSON))
SHEAR = 1.0 / (2.0 * (1.0 + POISSON))
NORMAL = 2.0 * SHEAR / 16.0
TRACE = LAME / 16.0
SHEAR_FIRST = SHEAR / 16.0
BEND = (LAME + 3.0 * SHEAR) / 48.0
BEND_MIX = LAME / 48.0
TWIST = SHEAR / 48.0
THIRD = (LAME + 4.0 * SHEAR) / 144.0
DIAGONAL = NORMAL + TRACE + 2.0 * SHEAR_FIRST + 2.0 * BEND + 2.0 * TWIST + THIRD
PAIRS = (("xdds", "zsdd"), ("ydds", "zdsd"), ("xdsd", "ysdd"))
TRIPLE = ("zdds", "ydsd", "xsdd")
CLASSES = [c + y + z for c in "xyz" for y in "sd" for z in "sd"]


def by_parity(axis, first, second, body):
    even = lax.rem(lax.axis_index(axis), 2) == 0
    pl.when(even)(lambda: body(second, first))
    pl.when(jnp.logical_not(even))(lambda: body(first, second))


def lane_index(shape):
    return lax.broadcasted_iota(jnp.int32, shape, len(shape) - 1)


def load_modes(z_ref, plane, begin, count):
    modes = {}
    for number, component in enumerate("xyz"):
        for index, z in enumerate("sd"):
            low = z_ref[number, index, plane, begin : begin + count, :]
            high = z_ref[number, index, plane, begin + 1 : begin + 1 + count, :]
            modes[component + "s" + z] = high + low
            modes[component + "d" + z] = high - low
    return modes


def element_modes(before, after):
    modes = {}
    for key in CLASSES:
        if key[1:] != "ss":
            modes[key[0] + "s" + key[1:]] = after[key] + before[key]
        modes[key[0] + "d" + key[1:]] = after[key] - before[key]
    return modes


def mode_forces(u, moduli):
    forces = {}
    normal = moduli * NORMAL
    trace = (u["xdss"] + u["ysds"] + u["zssd"]) * (TRACE / NORMAL)
    for key in ("xdss", "ysds", "zssd"):
        forces[key] = normal * (u[key] + trace)
    shear = moduli * SHEAR_FIRST
    for one, other in (("ydss", "xsds"), ("zsds", "yssd"), ("xssd", "zdss")):
        forces[one] = forces[other] = shear * (u[one] + u[other])
    bend = moduli * BEND
    for one, other in PAIRS:
        forces[one] = bend * (u[one] + (BEND_MIX / BEND) * u[other])
        forces[other] = bend * (u[other] + (BEND_MIX / BEND) * u[one])
    twist = moduli * TWIST
    total = u[TRIPLE[0]] + u[TRIPLE[1]] + u[TRIPLE[2]]
    for key in TRIPLE:
        forces[key] = twist * (total + u[key])
    third = moduli * THIRD
    for component in "xyz":
        forces[component + "ddd"] = third * u[component + "ddd"]
    return forces


def unit_energy(u):
    trace = u["xdss"] + u["ysds"] + u["zssd"]
    energy = TRACE * (trace * trace)
    energy += NORMAL * (u["xdss"] ** 2 + u["ysds"] ** 2 + u["zssd"] ** 2)
    shears = [u[a] + u[b] for a, b in (("ydss", "xsds"), ("zsds", "yssd"), ("xssd", "zdss"))]
    energy += SHEAR_FIRST * (shears[0] ** 2 + shears[1] ** 2 + shears[2] ** 2)
    squares, mixed = 0.0, 0.0
    for one, other in PAIRS:
        squares += u[one] ** 2 + u[other] ** 2
        mixed += (u[one] + u[other]) ** 2
    energy += (BEND - BEND_MIX) * squares + BEND_MIX * mixed
    total = u[TRIPLE[0]] + u[TRIPLE[1]] + u[TRIPLE[2]]
    squares = total * total
    for key in TRIPLE:
        squares += u[key] ** 2
    energy += TWIST * squares
    energy += THIRD * (u["xddd"] ** 2 + u["yddd"] ** 2 + u["zddd"] ** 2)
    return energy


def fields_kernel(shape, *refs):
    rows, cols, _ = shape
    sources, (own, lower, upper, first, second, low_x, high_x) = refs[:6], refs[6:13]
    *local, arrived = refs[13:]
    pieces = [(source, target) for source, target in zip(sources[:5], local)]
    pieces += [(sources[5].at[component], local[5].at[component]) for component in range(3)]
    copies = [pltpu.make_async_copy(s, t, arrived.at[i]) for i, (s, t) in enumerate(pieces)]
    for copy in copies:
        copy.start()
    for copy in copies:
        copy.wait()
    density, void, solid, fixed, load, traction = local
    is_solid, is_void = solid[...] == 1, void[...] == 1
    rho = jnp.where(is_solid, 1.0, jnp.where(is_void, RHO_FLOOR, density[...]))
    own[0] = rho
    free = (1 - fixed[...]).astype(jnp.float32)
    own[1] = free
    loaded = free * load[...].astype(jnp.float32)
    for component in range(3):
        own[2 + component] = loaded * traction[component]

    def outer_rows(low, high):
        for layer in range(HALO):
            for field in range(FIELDS):
                low[layer, field] = own[field, pl.ds(layer, rows, stride=cols), :]
                high[layer, field] = own[field, pl.ds(cols - HALO + layer, rows, stride=cols), :]

    by_parity("gy", first, second, outer_rows)
    low_x[...] = own[:, : HALO_X * cols, :]
    high_x[...] = own[:, (rows - HALO_X) * cols :, :]
    least = jnp.maximum(RHO_FLOOR, rho - MOVE_LIMIT)
    most = jnp.minimum(1.0, rho + MOVE_LIMIT)
    lower[...] = jnp.where(is_solid, 1.0, jnp.where(is_void, RHO_FLOOR, least))
    upper[...] = jnp.where(is_solid, 1.0, jnp.where(is_void, RHO_FLOOR, most))


def widen_kernel(shape, own, from_first, from_second, ext, first, second):
    rows, cols, _ = shape
    wide = cols + 2 * HALO

    def neighbour_rows(from_low, from_high):
        for field in range(FIELDS):
            for layer in range(HALO):
                ext[field, pl.ds(layer, rows, stride=wide), :] = from_low[layer, field]
                ext[field, pl.ds(cols + HALO + layer, rows, stride=wide), :] = from_high[layer, field]

    by_parity("gy", from_first, from_second, neighbour_rows)
    for field in range(FIELDS):
        for row in range(rows):
            ext[field, pl.ds(row * wide + HALO, cols), :] = own[field, pl.ds(row * cols, cols), :]

    def corners(low, high):
        for target, begin in ((low, 0), (high, rows - HALO_X)):
            for field in range(FIELDS):
                for layer in range(HALO_X):
                    row, source = layer * 2 * HALO, (begin + layer) * wide
                    target[field, row : row + HALO, :] = ext[field, source : source + HALO, :]
                    source += cols + HALO
                    target[field, row + HALO : row + 2 * HALO, :] = ext[field, source : source + HALO, :]

    by_parity("gx", first, second, corners)


def grid_cuts(rows):
    place, last = lax.axis_index("gx"), lax.axis_size("gx") - 1
    return {
        HALO_X - 1: jnp.where(place == 0, 0.0, 1.0),
        HALO_X + rows - 1: jnp.where(place == last, 0.0, 1.0),
    }


def cut_off(values, keep):
    return values if keep is None else {key: value * keep for key, value in values.items()}


class Stages:
    def __init__(self, shape, fields, inverses, p, w, set_p, set_w, z_ref, mode_ref, lift_ref, pipe_ref):
        self.wide, self.depth = shape[1] + 2 * HALO, shape[2]
        lanes = lane_index((self.wide, self.depth))
        self.keep_last = jnp.where(lanes < self.depth - 1, 1.0, 0.0)
        self.keep_first = jnp.where(lanes > 0, 1.0, 0.0)
        self.fields, self.inverses, self.p, self.w = fields, inverses, p, w
        self.set_p, self.set_w = set_p, set_w
        self.z_ref, self.mode_ref, self.lift_ref, self.pipe_ref = z_ref, mode_ref, lift_ref, pipe_ref

    def lift_moduli(self, around):
        return around + pltpu.roll(around, 1, 1) * self.keep_first

    def produce(self, level, plane, slot):
        for component in range(3):
            value = self.p(level, component, plane)
            lifted = pltpu.roll(value, self.depth - 1, 1) * self.keep_last
            self.z_ref[component, 0, slot, : self.wide] = lifted + value
            self.z_ref[component, 1, slot, : self.wide] = lifted - value

    def begin(self, slot):
        modes = load_modes(self.z_ref, slot, 0, self.wide)
        for index, key in enumerate(CLASSES):
            self.mode_ref[index] = modes[key]
            self.lift_ref[index] = jnp.zeros((self.wide, self.depth), jnp.float32)

    def spread(self, plane, slot, keep=None):
        after = load_modes(self.z_ref, slot, 0, self.wide)
        before = {key: self.mode_ref[index] for index, key in enumerate(CLASSES)}
        lift = {key: self.lift_ref[index] for index, key in enumerate(CLASSES)}
        forces = mode_forces(element_modes(before, cut_off(after, keep)), self.fields(plane))
        for number, component in enumerate("xyz"):
            along_z = {}
            for z in "sd":
                along_y = {}
                for y in "sd":
                    key = component + y + z
                    slope = forces[component + "d" + y + z]
                    if y + z == "ss":
                        along_y[y] = lift[key] - slope
                        lift[key] = slope
                    else:
                        mean = forces[component + "s" + y + z]
                        along_y[y] = lift[key] + (mean - slope)
                        lift[key] = mean + slope
                along_z[z] = (along_y["s"] - along_y["d"]) + pltpu.roll(along_y["s"] + along_y["d"], 1, 0)
            self.pipe_ref[number, 0] = along_z["s"] + along_z["d"]
            self.pipe_ref[number, 1] = along_z["s"] - along_z["d"]
        lift = cut_off(lift, keep)
        for index, key in enumerate(CLASSES):
            self.mode_ref[index] = after[key]
            self.lift_ref[index] = lift[key]

    def finish(self, level, plane):
        for component in range(3):
            shifted = pltpu.roll(self.pipe_ref[component, 0], 1, 1) * self.keep_first
            residual = (self.pipe_ref[component, 1] + shifted) - self.w(level, component, plane)
            self.set_w(level + 1, component, plane, residual)
            self.set_p(level + 1, component, plane, residual * self.inverses(plane))


def sweep(level, sides, cuts, shift):
    for side, start, count, wanted in sides:
        side.begin(start - shift)
    for step in range(max(count for _, _, count, _ in sides) + 2):
        for side, start, count, wanted in sides:
            plane, end = start + step, start + count
            if wanted <= plane - 2 < end:
                side.produce(level + 1, plane - 2, plane - 2 - shift)
            if wanted <= plane - 1 < end:
                side.finish(level, plane - 1)
            if plane < end:
                side.spread(plane, plane + 1 - shift, cuts.get(plane))


def moduli_of(rho):
    return jnp.where(rho > 0.0, E_MIN + rho * rho * rho * (1.0 - E_MIN), 0.0)


def inverse_of(free, around):
    return free / (free * (DIAGONAL * around) + (1.0 - free))


PAIR_LIST = [(i, j) for i in range(BASIS) for j in range(i + 1)]


def inner_kernel(shape, ext, p_ref, w_ref, field_ref, inverse_ref, totals_ref, z_ref, mode_ref, lift_ref, pipe_ref):
    rows, cols, depth = shape
    wide, shift = cols + 2 * HALO, HALO_X - 1
    field_ref[:, :8, :] = jnp.zeros((rows, 8, depth), jnp.float32)
    z_ref[:, :, :, wide:, :] = jnp.zeros((3, 2, z_ref.shape[2], 8, depth), jnp.float32)
    for row in range(rows):
        window = slice(row * wide, (row + 1) * wide)
        field_ref[row, 8:, :] = moduli_of(ext[0, window, :])
        for component in range(3):
            w_ref[0, component, row + 1] = ext[2 + component, window, :]

    def store(ref):
        def put(level, component, plane, value):
            ref[level, component, plane - shift] = value

        return put

    stages = Stages(
        shape,
        lambda plane: field_ref[plane - HALO_X, 8:, :],
        lambda plane: inverse_ref[plane - HALO_X],
        lambda level, component, plane: p_ref[level, component, plane - shift],
        lambda level, component, plane: w_ref[level, component, plane - shift],
        store(p_ref),
        store(w_ref),
        z_ref,
        mode_ref,
        lift_ref,
        pipe_ref,
    )
    inverse_ref[0] = jnp.zeros((wide, depth), jnp.float32)
    for row in range(1, rows):
        around = field_ref[row - 1, 8:, :] + field_ref[row - 1, 7 : 7 + wide, :]
        around = around + (field_ref[row, 8:, :] + field_ref[row, 7 : 7 + wide, :])
        inverse = inverse_of(ext[1, row * wide : (row + 1) * wide, :], stages.lift_moduli(around))
        inverse_ref[row] = inverse
        for component in range(3):
            p_ref[0, component, row + 1] = w_ref[0, component, row + 1] * inverse
    for row in range(1, rows):
        stages.produce(0, row + HALO_X, row + 1)

    for level in range(BASIS - 1):
        start, count = HALO_X + 1 + level, rows - 2 - 2 * level
        sweep(level, [(stages, start, count, start + 1)], {}, shift)

    first, last = HALO_X + BASIS, HALO_X + rows - 1 - (BASIS - 1)
    totals = [jnp.zeros((cols, depth), jnp.float32)] * (len(PAIR_LIST) + 1)
    before = load_modes(z_ref, first - shift, HALO, cols)
    for plane in range(first, last + 1):
        totals = add_dots(
            totals,
            lambda level, component: p_ref[level, component, plane - shift, HALO : HALO + cols, :],
            lambda level, component: w_ref[level, component, plane - shift, HALO : HALO + cols, :],
        )
        if plane < last:
            after = load_modes(z_ref, plane + 1 - shift, HALO, cols)
            energy = unit_energy(element_modes(before, after))
            totals[-1] = totals[-1] + field_ref[plane - HALO_X, 8 + HALO : 8 + HALO + cols, :] * energy
            before = after
    for index, total in enumerate(totals):
        totals_ref[index] = total


def add_dots(totals, p, w):
    totals = list(totals)
    for component in range(3):
        ps = [p(level, component) for level in range(BASIS)]
        ws = [w(level, component) for level in range(BASIS)]
        for index, (i, j) in enumerate(PAIR_LIST):
            totals[index] = totals[index] + ps[i] * ws[j]
    return totals


def outer_kernel(
    shape, ext, low_x, high_x, first, second, p_in, w_in, field_in, inverse_in, totals_in, p_ref, sums_out, *scratch
):
    rows, cols, depth = shape
    wide, long, shift = cols + 2 * HALO, rows + 2 * HALO_X, HALO_X - 1
    halo_ref, field_ref, inverse_ref, w_ref, z_ref, *both = scratch
    cuts = grid_cuts(rows)
    own = range(HALO_X, HALO_X + rows)
    z_ref[:, :, :, wide:, :] = jnp.zeros((3, 2, long, 8, depth), jnp.float32)
    field_ref[:, :8, :] = jnp.zeros((long, 8, depth), jnp.float32)

    def rims(low, high):
        for rim, begin in ((low, 0), (high, HALO_X)):
            for field in range(FIELDS):
                for layer in range(HALO_X):
                    row = layer * 2 * HALO
                    halo_ref[field, begin + layer, :HALO, :] = rim[field, row : row + HALO, :]
                    halo_ref[field, begin + layer, HALO + cols :, :] = rim[field, row + HALO : row + 2 * HALO, :]

    by_parity("gx", first, second, rims)
    for middle, begin in ((low_x, 0), (high_x, HALO_X)):
        for field in range(FIELDS):
            for layer in range(HALO_X):
                window = slice(layer * cols, (layer + 1) * cols)
                halo_ref[field, begin + layer, HALO : HALO + cols, :] = middle[field, window, :]

    def given(field, plane, begin=0, count=wide):
        if plane in own:
            row = (plane - HALO_X) * wide + begin
            return ext[field, row : row + count, :]
        return halo_ref[field, plane if plane < HALO_X else plane - rows, begin : begin + count, :]

    def fields(plane, begin=0, count=wide):
        if plane in own:
            return field_in[plane - HALO_X, 8 + begin : 8 + begin + count, :]
        return field_ref[plane, 8 + begin : 8 + begin + count, :]

    def inverses(plane):
        return inverse_in[plane - HALO_X] if HALO_X < plane < HALO_X + rows else inverse_ref[plane]

    def is_inner(level, plane):
        return HALO_X + 1 + level <= plane <= HALO_X + rows - 1 - level

    def p(level, component, plane, begin=0, count=wide):
        if is_inner(level, plane):
            return p_in[level, component, plane - shift, begin : begin + count, :]
        return p_ref[level, component, plane, begin : begin + count, :]

    def w(level, component, plane, begin=0, count=wide):
        if is_inner(level, plane):
            return w_in[level, component, plane - shift, begin : begin + count, :]
        if level == 0:
            return given(2 + component, plane, begin, count)
        return w_ref[level, component, plane, begin : begin + count, :]

    def set_p(level, component, plane, value):
        p_ref[level, component, plane] = value

    def set_w(level, component, plane, value):
        w_ref[level, component, plane] = value

    sides = [
        Stages(shape, fields, inverses, p, w, set_p, set_w, z_ref, both[0], both[1], both[2]),
        Stages(shape, fields, inverses, p, w, set_p, set_w, z_ref, both[3], both[4], both[5]),
    ]
    for plane in range(long):
        if plane not in own:
            field_ref[plane, 8:, :] = moduli_of(given(0, plane))
    edge_planes = [*range(1, HALO_X + 1), *range(HALO_X + rows, long)]
    for plane in edge_planes:
        around = fields(plane - 1) + fields(plane - 1, -1)
        if plane - 1 in cuts:
            around = around * cuts[plane - 1]
        around = around + (fields(plane) + fields(plane, -1))
        inverse = inverse_of(given(1, plane), sides[0].lift_moduli(around))
        inverse_ref[plane] = inverse
        for component in range(3):
            set_p(0, component, plane, given(2 + component, plane) * inverse)
    for plane in edge_planes:
        sides[0].produce(0, plane, plane)

    count = HALO_X + 1
    for level in range(BASIS - 1):
        for plane in (HALO_X + 1 + level, HALO_X + 2 + level, HALO_X + rows - 2 - level, HALO_X + rows - 1 - level):
            sides[0].produce(level, plane, plane)
        left, right = 1 + level, HALO_X + rows - 2 - level
        sweep(level, [(sides[0], left, count, left + 1), (sides[1], right, count, right + 1)], cuts, 0)

    last = BASIS - 1
    for plane in (HALO_X + 1 + last, HALO_X + rows - 1 - last):
        sides[0].produce(last, plane, plane)
    totals = [totals_in[index] for index in range(len(PAIR_LIST) + 1)]
    for plane in own:
        if not is_inner(last, plane):
            totals = add_dots(
                totals,
                lambda level, component: p(level, component, plane, HALO, cols),
                lambda level, component: w(level, component, plane, HALO, cols),
            )
        if not (is_inner(last, plane) and is_inner(last, plane + 1)):
            before = load_modes(z_ref, plane, HALO, cols)
            after = cut_off(load_modes(z_ref, plane + 1, HALO, cols), cuts.get(plane))
            energy = unit_energy(element_modes(before, after))
            totals[-1] = totals[-1] + fields(plane, HALO, cols) * energy
    slots = lane_index((1, 128))
    line = jnp.zeros((1, 128), jnp.float32)
    for index, total in enumerate(totals):
        share = jnp.sum(jnp.sum(total, axis=0, keepdims=True), axis=1, keepdims=True)
        line = line + jnp.where(slots == index, share, 0.0)
    sums_out[...] = jnp.broadcast_to(line, sums_out.shape)


def coefficients(shares):
    line = jnp.sum(shares, axis=0, keepdims=True)
    slots = lane_index(line.shape)

    def entry(index):
        return jnp.sum(jnp.where(slots == index, line, 0.0), axis=1, keepdims=True)

    inner = {}
    for index, (i, j) in enumerate(PAIR_LIST):
        inner[i, j] = inner[j, i] = entry(index)
    energy = {(BASIS - 1, BASIS - 1): entry(len(PAIR_LIST))}
    for i in range(BASIS):
        for j in range(min(i + 1, BASIS - 1)):
            energy[i, j] = inner[i, j + 1] + inner[i, j]
    lower, pivot, inverse, solved = {}, {}, {}, {}
    for k in range(BASIS):
        left = energy[k, k]
        for m in range(k):
            left = left - lower[k, m] * lower[k, m] * pivot[m]
        sound = left > 1e-6 * energy[k, k]
        pivot[k] = jnp.where(sound, left, 0.0)
        inverse[k] = jnp.where(sound, 1.0 / jnp.where(sound, left, 1.0), 0.0)
        for i in range(k + 1, BASIS):
            part = energy[i, k]
            for m in range(k):
                part = part - lower[i, m] * lower[k, m] * pivot[m]
            lower[i, k] = part * inverse[k]
    for k in range(BASIS):
        part = inner[k, 0]
        for m in range(k):
            part = part - lower[k, m] * solved[m]
        solved[k] = part
    result = {}
    for k in reversed(range(BASIS)):
        part = solved[k] * inverse[k]
        for m in range(k + 1, BASIS):
            part = part - lower[m, k] * result[m]
        result[k] = part
    return [result[k] for k in range(BASIS)]


def energy_kernel(
    shape, shares, inner, outer, own, low_x, high_x, displacement, weighted, first, second, u_ref, own_ref, z_ref, sent
):
    rows, cols, depth = shape
    wide, planes = cols + 2 * HALO, rows + 2 * REACH
    keep_last = jnp.where(lane_index((wide, depth)) < depth - 1, 1.0, 0.0)
    parts = [jnp.broadcast_to(part, (wide, depth)) for part in coefficients(shares[...])]
    cuts = grid_cuts(rows)
    for plane in range(planes + 1):
        source = plane + HALO_X - REACH
        for component in range(3):
            total = None
            for level in range(BASIS):
                if HALO_X + 1 + level <= source <= HALO_X + rows - 1 - level:
                    term = parts[level] * inner[level, component, source - HALO_X + 1]
                else:
                    term = parts[level] * outer[level, component, source]
                total = term if total is None else total + term
            lifted = pltpu.roll(total, depth - 1, 1) * keep_last
            z_ref[component, 0, plane] = lifted + total
            z_ref[component, 1, plane] = lifted - total
            row = plane - REACH
            if 0 <= row < rows:
                u_ref[component, row] = total
                own_ref[component, row] = u_ref[component, row, HALO : HALO + cols, :]
    copy = pltpu.make_async_copy(own_ref, displacement, sent.at[0])
    copy.start()
    before = load_modes(z_ref, 0, HALO, cols)
    for plane in range(planes):
        row = plane - REACH
        after = load_modes(z_ref, plane + 1, HALO, cols)
        energy = unit_energy(element_modes(before, cut_off(after, cuts.get(row + HALO_X))))
        before = after
        if row < 0:
            rho = low_x[0, (row + HALO_X) * cols : (row + HALO_X + 1) * cols, :]
        elif row < rows:
            rho = own[0, row * cols : (row + 1) * cols, :]
        else:
            rho = high_x[0, (row - rows) * cols : (row - rows + 1) * cols, :]
        weighted[plane * cols : (plane + 1) * cols, :] = rho * (3.0 * rho * rho * (1.0 - E_MIN) * energy)

    def outer_rows(low, high):
        for layer in range(REACH):
            low[layer] = weighted[pl.ds(layer, planes, stride=cols), :]
            high[layer] = weighted[pl.ds(cols - REACH + layer, planes, stride=cols), :]

    by_parity("gy", first, second, outer_rows)
    copy.wait()


def cone_table():
    table, total = {}, 0.0
    for a in range(-2, 3):
        for b in range(-2, 3):
            for c in range(-2, 3):
                total += max(0.0, 3.0 - math.sqrt(a * a + b * b + c * c))
    for flat in (0, 1, 2, 4, 5, 8):
        for c in range(3):
            table[flat, c] = max(0.0, 3.0 - math.sqrt(flat + c * c))
    return table, total


def volume_row(total):
    return jnp.sum(total, axis=0, keepdims=True)


def filter_kernel(shape, weighted, from_first, from_second, own, lower, upper, root, volume, plane_ref):
    rows, cols, depth = shape
    wide, planes = cols + 8, rows + 2 * REACH
    table, total = cone_table()
    for plane in range(planes):
        plane_ref[plane * wide + REACH : plane * wide + REACH + cols, :] = weighted[plane * cols : (plane + 1) * cols, :]

    def neighbour_rows(from_low, from_high):
        for layer in range(REACH):
            plane_ref[pl.ds(layer, planes, stride=wide), :] = from_low[layer]
            plane_ref[pl.ds(REACH + cols + layer, planes, stride=wide), :] = from_high[layer]

    by_parity("gy", from_first, from_second, neighbour_rows)
    volume_sum = jnp.zeros((cols, depth), jnp.float32)
    for row in range(rows):
        spread = {}
        for a in range(-REACH, REACH + 1):
            for b in range(-REACH, REACH + 1):
                key = a * a + b * b
                value = plane_ref[pl.ds((row + REACH + a) * wide + REACH + b, cols), :]
                spread[key] = value if key not in spread else spread[key] + value
        sums = []
        for c in range(3):
            part = None
            for key, value in spread.items():
                if table[key, c] > 0.0:
                    term = table[key, c] * value
                    part = term if part is None else part + term
            sums.append(part)
        convolved = sums[0]
        for c in (1, 2):
            convolved = convolved + (pltpu.roll(sums[c], c, 1) + pltpu.roll(sums[c], depth - c, 1))
        window = slice(row * cols, (row + 1) * cols)
        rho = own[0, window, :]
        base = rho * jnp.sqrt(convolved / (total * rho))
        root[window, :] = base
        volume_sum = volume_sum + jnp.minimum(jnp.maximum(base, lower[window, :]), upper[window, :])
    volume[...] = jnp.broadcast_to(volume_row(volume_sum), volume.shape)


def scale_of(target, volumes):
    scale = None
    for volume in volumes:
        whole = jnp.sum(jnp.sum(volume[...], axis=0, keepdims=True), axis=1, keepdims=True)
        ratio = target / whole
        scale = ratio if scale is None else scale * ratio
    return scale


def trial_kernel(target, steps, final, *refs):
    volumes, (root, lower, upper, out) = refs[:steps], refs[steps:]
    scale = scale_of(target, volumes)
    moved = jnp.minimum(jnp.maximum(root[...] * scale, lower[...]), upper[...])
    if final:
        out[...] = moved
    else:
        out[...] = jnp.broadcast_to(volume_row(moved), out.shape)


def call(kernel, name, out_shapes, *args, scratch=(), flops=0, space=pltpu.VMEM, far=()):
    shapes = [jax.ShapeDtypeStruct(shape, jnp.float32) for shape in out_shapes]
    moved = sum(4 * math.prod(value.shape) for value in [*args, *shapes])
    return pl.pallas_call(
        kernel,
        name=name,
        out_shape=shapes,
        in_specs=[pl.BlockSpec(memory_space=space)] * len(args),
        out_specs=[pl.BlockSpec(memory_space=pltpu.HBM if i in far else pltpu.VMEM) for i in range(len(shapes))],
        scratch_shapes=[pltpu.VMEM(item, jnp.float32) if isinstance(item, tuple) else item for item in scratch],
        compiler_params=pltpu.CompilerParams(vmem_limit_bytes=VMEM_LIMIT),
        cost_estimate=pl.CostEstimate(flops=flops, bytes_accessed=moved, transcendentals=0),
    )(*args)


def exchange(low, high, axis):
    count = lax.axis_size(axis)
    from_low = lax.ppermute(high, axis, [(i, (i + 1) % count) for i in range(count)])
    from_high = lax.ppermute(low, axis, [((i + 1) % count, i) for i in range(count)])
    return from_low, from_high


def swap(first, second, axis, wrap):
    count = lax.axis_size(axis)
    assert count % 2 == 0
    ends = [(i, i + 1) for i in range(1, count - 1, 2)] + ([(count - 1, 0)] if wrap else [])
    pairs = [(i, i + 1) for i in range(0, count, 2)]
    both = lambda links: links + [(j, i) for i, j in links]
    return lax.ppermute(first, axis, both(pairs)), lax.ppermute(second, axis, both(ends))


def everyone(shares):
    return lax.all_to_all(shares, AXES, 0, 0, tiled=True)


def shards(density, void_mask, solid_mask, fixed_mask, load_mask, traction):
    shape = rows, cols, depth = density.shape
    devices = lax.axis_size("gx") * lax.axis_size("gy")
    wide, long = cols + 2 * HALO, rows + 2 * HALO_X
    planes = rows + 2 * REACH
    named = lambda kernel: functools.partial(kernel, shape)
    flat = (rows * cols, depth)
    inputs = [
        pltpu.with_memory_space_constraint(value.reshape(*value.shape[:-3], *flat), pltpu.HBM)
        for value in (density, void_mask, solid_mask, fixed_mask, load_mask, traction)
    ]

    own, lower, upper, first, second, low_x, high_x = call(
        named(fields_kernel),
        "fields",
        [
            (FIELDS, *flat),
            flat,
            flat,
            (HALO, FIELDS, rows, depth),
            (HALO, FIELDS, rows, depth),
            (FIELDS, HALO_X * cols, depth),
            (FIELDS, HALO_X * cols, depth),
        ],
        *inputs,
        scratch=[pltpu.VMEM(value.shape, value.dtype) for value in inputs] + [pltpu.SemaphoreType.DMA((8,))],
        space=pltpu.HBM,
    )
    from_first, from_second = swap(first, second, "gy", False)
    low_x, high_x = exchange(low_x, high_x, "gx")
    ext, first, second = call(
        named(widen_kernel),
        "widen",
        [(FIELDS, rows * wide, depth)] + [(FIELDS, HALO_X * 2 * HALO, depth)] * 2,
        own,
        from_first,
        from_second,
    )
    first_xy, second_xy = swap(first, second, "gx", True)
    side = [(12, wide, depth), (12, wide, depth), (3, 2, wide, depth)]
    inner = call(
        named(inner_kernel),
        "inner",
        [
            (BASIS, 3, rows + 1, wide, depth),
            (BASIS, 3, rows + 1, wide, depth),
            (rows, 8 + wide, depth),
            (rows, wide, depth),
            (len(PAIR_LIST) + 1, cols, depth),
        ],
        ext,
        scratch=[(3, 2, rows + 1, wide + 8, depth), *side],
    )
    outer, sums = call(
        named(outer_kernel),
        "outer",
        [(BASIS, 3, long, wide, depth), (devices, 128)],
        ext,
        low_x,
        high_x,
        first_xy,
        second_xy,
        *inner,
        scratch=[
            (FIELDS, 2 * HALO_X, wide, depth),
            (long, 8 + wide, depth),
            (long, wide, depth),
            (BASIS, 3, long, wide, depth),
            (3, 2, long, wide + 8, depth),
            *side,
            *side,
        ],
    )
    displacement, weighted, first, second = call(
        named(energy_kernel),
        "energy",
        [(3, rows, cols, depth), (planes * cols, depth), (REACH, planes, depth), (REACH, planes, depth)],
        everyone(sums),
        inner[0],
        outer,
        own,
        low_x,
        high_x,
        scratch=[
            (3, rows, wide, depth),
            (3, rows, cols, depth),
            (3, 2, planes + 1, wide, depth),
            pltpu.SemaphoreType.DMA((1,)),
        ],
        far=(0,),
    )
    from_first, from_second = swap(first, second, "gy", True)
    root, volume = call(
        named(filter_kernel),
        "filter",
        [flat, (devices, depth)],
        weighted,
        from_first,
        from_second,
        own,
        lower,
        upper,
        scratch=[(planes * (cols + 8), depth)],
    )
    target = VOLUME_SHARE * rows * cols * depth * devices
    terms, volumes = (root, lower, upper), [everyone(volume)]
    for step in (1, 2):
        (volume,) = call(
            functools.partial(trial_kernel, target, step, False), "trial", [(devices, depth)], *volumes, *terms
        )
        volumes.append(everyone(volume))
    (new_density,) = call(functools.partial(trial_kernel, target, 3, True), "update", [flat], *volumes, *terms)
    return new_density.reshape(shape), displacement


def solution(mesh):
    placed = (P("gx", "gy", None),) * 5 + (P(None, "gx", "gy", None),)
    return jax.shard_map(
        shards,
        mesh=mesh,
        in_specs=placed,
        out_specs=(P("gx", "gy", None), P(None, "gx", "gy", None)),
        check_vma=False,
    )
```

```python
import functools
import math

import jax
import jax.numpy as jnp
import numpy as np
from jax import lax
from jax.experimental import pallas as pl
from jax.experimental.pallas import tpu as pltpu
from jax.sharding import PartitionSpec as P

E_MIN = 0.001
RHO_FLOOR = 0.001
MOVE_LIMIT = 0.2
VOLUME_SHARE = 0.4
BASIS = 4
REACH = 2
HALO = BASIS
HALO_X = BASIS + REACH
AXES = ("gx", "gy")
FIELDS = 5
VMEM_LIMIT = 40 * 1024 * 1024

POISSON = 0.3
LAME = POISSON / ((1.0 + POISSON) * (1.0 - 2.0 * POISSON))
SHEAR = 1.0 / (2.0 * (1.0 + POISSON))
NORMAL = 2.0 * SHEAR / 16.0
TRACE = LAME / 16.0
SHEAR_FIRST = SHEAR / 16.0
BEND = (LAME + 3.0 * SHEAR) / 48.0
BEND_MIX = LAME / 48.0
TWIST = SHEAR / 48.0
THIRD = (LAME + 4.0 * SHEAR) / 144.0
DIAGONAL = NORMAL + TRACE + 2.0 * SHEAR_FIRST + 2.0 * BEND + 2.0 * TWIST + THIRD
PAIRS = (("xdds", "zsdd"), ("ydds", "zdsd"), ("xdsd", "ysdd"))
TRIPLE = ("zdds", "ydsd", "xsdd")
CLASSES = [c + y + z for c in "xyz" for y in "sd" for z in "sd"]


def by_parity(axis, first, second, body):
    even = lax.rem(lax.axis_index(axis), 2) == 0
    pl.when(even)(lambda: body(second, first))
    pl.when(jnp.logical_not(even))(lambda: body(first, second))


def lane_index(shape):
    return lax.broadcasted_iota(jnp.int32, shape, len(shape) - 1)


def load_modes(z_ref, plane, begin, count):
    modes = {}
    for number, component in enumerate("xyz"):
        for index, z in enumerate("sd"):
            low = z_ref[number, index, plane, begin : begin + count, :]
            high = z_ref[number, index, plane, begin + 1 : begin + 1 + count, :]
            modes[component + "s" + z] = high + low
            modes[component + "d" + z] = high - low
    return modes


def element_modes(before, after):
    modes = {}
    for key in CLASSES:
        if key[1:] != "ss":
            modes[key[0] + "s" + key[1:]] = after[key] + before[key]
        modes[key[0] + "d" + key[1:]] = after[key] - before[key]
    return modes


def mode_forces(u, moduli):
    forces = {}
    normal = moduli * NORMAL
    trace = (u["xdss"] + u["ysds"] + u["zssd"]) * (TRACE / NORMAL)
    for key in ("xdss", "ysds", "zssd"):
        forces[key] = normal * (u[key] + trace)
    shear = moduli * SHEAR_FIRST
    for one, other in (("ydss", "xsds"), ("zsds", "yssd"), ("xssd", "zdss")):
        forces[one] = forces[other] = shear * (u[one] + u[other])
    bend = moduli * BEND
    for one, other in PAIRS:
        forces[one] = bend * (u[one] + (BEND_MIX / BEND) * u[other])
        forces[other] = bend * (u[other] + (BEND_MIX / BEND) * u[one])
    twist = moduli * TWIST
    total = u[TRIPLE[0]] + u[TRIPLE[1]] + u[TRIPLE[2]]
    for key in TRIPLE:
        forces[key] = twist * (total + u[key])
    third = moduli * THIRD
    for component in "xyz":
        forces[component + "ddd"] = third * u[component + "ddd"]
    return forces


def unit_energy(u):
    trace = u["xdss"] + u["ysds"] + u["zssd"]
    energy = TRACE * (trace * trace)
    energy += NORMAL * (u["xdss"] ** 2 + u["ysds"] ** 2 + u["zssd"] ** 2)
    shears = [u[a] + u[b] for a, b in (("ydss", "xsds"), ("zsds", "yssd"), ("xssd", "zdss"))]
    energy += SHEAR_FIRST * (shears[0] ** 2 + shears[1] ** 2 + shears[2] ** 2)
    squares, mixed = 0.0, 0.0
    for one, other in PAIRS:
        squares += u[one] ** 2 + u[other] ** 2
        mixed += (u[one] + u[other]) ** 2
    energy += (BEND - BEND_MIX) * squares + BEND_MIX * mixed
    total = u[TRIPLE[0]] + u[TRIPLE[1]] + u[TRIPLE[2]]
    squares = total * total
    for key in TRIPLE:
        squares += u[key] ** 2
    energy += TWIST * squares
    energy += THIRD * (u["xddd"] ** 2 + u["yddd"] ** 2 + u["zddd"] ** 2)
    return energy


def fields_kernel(shape, *refs):
    rows, cols, _ = shape
    (density_in, void_in, solid_in, fixed_in, load_in, traction_in) = refs[:6]
    (own, lower, upper, first, second, low_x, high_x) = refs[6:13]
    density, void, solid, fixed, load, traction, arrived = refs[13:]
    pieces = [(fixed_in, fixed), (load_in, load)]
    pieces += [(traction_in.at[component], traction.at[component]) for component in range(3)]
    pieces += [(density_in, density), (void_in, void), (solid_in, solid)]
    copies = [pltpu.make_async_copy(s, t, arrived.at[i]) for i, (s, t) in enumerate(pieces)]
    for copy in copies:
        copy.start()

    def send(field):
        low_x[field] = own[field, : HALO_X * cols, :]
        high_x[field] = own[field, (rows - HALO_X) * cols :, :]

        def outer_rows(low, high):
            for layer in range(HALO):
                low[layer, field] = own[field, pl.ds(layer, rows, stride=cols), :]
                high[layer, field] = own[field, pl.ds(cols - HALO + layer, rows, stride=cols), :]

        by_parity("gy", first, second, outer_rows)

    copies[0].wait()
    copies[1].wait()
    free = (1 - fixed[...]).astype(jnp.float32)
    own[1] = free
    send(1)
    for component in range(3):
        copies[2 + component].wait()
        own[2 + component] = own[1] * load[...].astype(jnp.float32) * traction[component]
        send(2 + component)
    for copy in copies[5:]:
        copy.wait()
    is_solid, is_void = solid[...] == 1, void[...] == 1
    rho = jnp.where(is_solid, 1.0, jnp.where(is_void, RHO_FLOOR, density[...]))
    own[0] = rho
    send(0)
    least = jnp.maximum(RHO_FLOOR, rho - MOVE_LIMIT)
    most = jnp.minimum(1.0, rho + MOVE_LIMIT)
    lower[...] = jnp.where(is_solid, 1.0, jnp.where(is_void, RHO_FLOOR, least))
    upper[...] = jnp.where(is_solid, 1.0, jnp.where(is_void, RHO_FLOOR, most))


def widen_kernel(shape, own, from_first, from_second, ext, first, second):
    rows, cols, _ = shape
    wide = cols + 2 * HALO

    def neighbour_rows(from_low, from_high):
        for field in range(FIELDS):
            for layer in range(HALO):
                ext[field, pl.ds(layer, rows, stride=wide), :] = from_low[layer, field]
                ext[field, pl.ds(cols + HALO + layer, rows, stride=wide), :] = from_high[layer, field]

    by_parity("gy", from_first, from_second, neighbour_rows)
    for field in range(FIELDS):
        for row in range(rows):
            ext[field, pl.ds(row * wide + HALO, cols), :] = own[field, pl.ds(row * cols, cols), :]

    def corners(low, high):
        for target, begin in ((low, 0), (high, rows - HALO_X)):
            for field in range(FIELDS):
                for layer in range(HALO_X):
                    row, source = layer * 2 * HALO, (begin + layer) * wide
                    target[field, row : row + HALO, :] = ext[field, source : source + HALO, :]
                    source += cols + HALO
                    target[field, row + HALO : row + 2 * HALO, :] = ext[field, source : source + HALO, :]

    by_parity("gx", first, second, corners)


def grid_cuts(rows):
    place, last = lax.axis_index("gx"), lax.axis_size("gx") - 1
    return {
        HALO_X - 1: jnp.where(place == 0, 0.0, 1.0),
        HALO_X + rows - 1: jnp.where(place == last, 0.0, 1.0),
    }


def cut_off(values, keep):
    return values if keep is None else {key: value * keep for key, value in values.items()}


class Stages:
    def __init__(self, shape, fields, inverses, p, w, set_p, set_w, z_ref, mode_ref, lift_ref, pipe_ref):
        self.wide, self.depth = shape[1] + 2 * HALO, shape[2]
        lanes = lane_index((self.wide, self.depth))
        self.keep_last = jnp.where(lanes < self.depth - 1, 1.0, 0.0)
        self.keep_first = jnp.where(lanes > 0, 1.0, 0.0)
        self.fields, self.inverses, self.p, self.w = fields, inverses, p, w
        self.set_p, self.set_w = set_p, set_w
        self.z_ref, self.mode_ref, self.lift_ref, self.pipe_ref = z_ref, mode_ref, lift_ref, pipe_ref

    def lift_moduli(self, around):
        return around + pltpu.roll(around, 1, 1) * self.keep_first

    def produce(self, level, plane, slot):
        for component in range(3):
            value = self.p(level, component, plane)
            lifted = pltpu.roll(value, self.depth - 1, 1) * self.keep_last
            self.z_ref[component, 0, slot, : self.wide] = lifted + value
            self.z_ref[component, 1, slot, : self.wide] = lifted - value

    def begin(self, slot):
        modes = load_modes(self.z_ref, slot, 0, self.wide)
        for index, key in enumerate(CLASSES):
            self.mode_ref[index] = modes[key]
            self.lift_ref[index] = jnp.zeros((self.wide, self.depth), jnp.float32)

    def spread(self, plane, slot, keep=None):
        after = load_modes(self.z_ref, slot, 0, self.wide)
        before = {key: self.mode_ref[index] for index, key in enumerate(CLASSES)}
        lift = {key: self.lift_ref[index] for index, key in enumerate(CLASSES)}
        forces = mode_forces(element_modes(before, cut_off(after, keep)), self.fields(plane))
        for number, component in enumerate("xyz"):
            along_z = {}
            for z in "sd":
                along_y = {}
                for y in "sd":
                    key = component + y + z
                    slope = forces[component + "d" + y + z]
                    if y + z == "ss":
                        along_y[y] = lift[key] - slope
                        lift[key] = slope
                    else:
                        mean = forces[component + "s" + y + z]
                        along_y[y] = lift[key] + (mean - slope)
                        lift[key] = mean + slope
                along_z[z] = (along_y["s"] - along_y["d"]) + pltpu.roll(along_y["s"] + along_y["d"], 1, 0)
            self.pipe_ref[number, 0] = along_z["s"] + along_z["d"]
            self.pipe_ref[number, 1] = along_z["s"] - along_z["d"]
        lift = cut_off(lift, keep)
        for index, key in enumerate(CLASSES):
            self.mode_ref[index] = after[key]
            self.lift_ref[index] = lift[key]

    def finish(self, level, plane):
        for component in range(3):
            shifted = pltpu.roll(self.pipe_ref[component, 0], 1, 1) * self.keep_first
            residual = (self.pipe_ref[component, 1] + shifted) - self.w(level, component, plane)
            self.set_w(level + 1, component, plane, residual)
            self.set_p(level + 1, component, plane, residual * self.inverses(plane))


def sweep(level, sides, cuts, shift):
    for side, start, count, wanted in sides:
        side.begin(start - shift)
    for step in range(max(count for _, _, count, _ in sides) + 2):
        for side, start, count, wanted in sides:
            plane, end = start + step, start + count
            if wanted <= plane - 2 < end:
                side.produce(level + 1, plane - 2, plane - 2 - shift)
            if wanted <= plane - 1 < end:
                side.finish(level, plane - 1)
            if plane < end:
                side.spread(plane, plane + 1 - shift, cuts.get(plane))


def moduli_of(rho):
    return jnp.where(rho > 0.0, E_MIN + rho * rho * rho * (1.0 - E_MIN), 0.0)


def inverse_of(free, around):
    return free / (free * (DIAGONAL * around) + (1.0 - free))


PAIR_LIST = [(i, j) for i in range(BASIS) for j in range(i + 1)]


def inner_kernel(shape, ext, p_ref, w_ref, field_ref, inverse_ref, totals_ref, z_ref, mode_ref, lift_ref, pipe_ref):
    rows, cols, depth = shape
    wide, shift = cols + 2 * HALO, HALO_X - 1
    field_ref[:, :8, :] = jnp.zeros((rows, 8, depth), jnp.float32)
    z_ref[:, :, :, wide:, :] = jnp.zeros((3, 2, z_ref.shape[2], 8, depth), jnp.float32)
    for row in range(rows):
        window = slice(row * wide, (row + 1) * wide)
        field_ref[row, 8:, :] = moduli_of(ext[0, window, :])
        for component in range(3):
            w_ref[0, component, row + 1] = ext[2 + component, window, :]

    def store(ref):
        def put(level, component, plane, value):
            ref[level, component, plane - shift] = value

        return put

    stages = Stages(
        shape,
        lambda plane: field_ref[plane - HALO_X, 8:, :],
        lambda plane: inverse_ref[plane - HALO_X],
        lambda level, component, plane: p_ref[level, component, plane - shift],
        lambda level, component, plane: w_ref[level, component, plane - shift],
        store(p_ref),
        store(w_ref),
        z_ref,
        mode_ref,
        lift_ref,
        pipe_ref,
    )
    inverse_ref[0] = jnp.zeros((wide, depth), jnp.float32)
    for row in range(1, rows):
        around = field_ref[row - 1, 8:, :] + field_ref[row - 1, 7 : 7 + wide, :]
        around = around + (field_ref[row, 8:, :] + field_ref[row, 7 : 7 + wide, :])
        inverse = inverse_of(ext[1, row * wide : (row + 1) * wide, :], stages.lift_moduli(around))
        inverse_ref[row] = inverse
        for component in range(3):
            p_ref[0, component, row + 1] = w_ref[0, component, row + 1] * inverse
    for row in range(1, rows):
        stages.produce(0, row + HALO_X, row + 1)

    for level in range(BASIS - 1):
        start, count = HALO_X + 1 + level, rows - 2 - 2 * level
        sweep(level, [(stages, start, count, start + 1)], {}, shift)

    first, last = HALO_X + BASIS, HALO_X + rows - 1 - (BASIS - 1)
    totals = [jnp.zeros((cols, depth), jnp.float32)] * (len(PAIR_LIST) + 1)
    before = load_modes(z_ref, first - shift, HALO, cols)
    for plane in range(first, last + 1):
        totals = add_dots(
            totals,
            lambda level, component: p_ref[level, component, plane - shift, HALO : HALO + cols, :],
            lambda level, component: w_ref[level, component, plane - shift, HALO : HALO + cols, :],
        )
        if plane < last:
            after = load_modes(z_ref, plane + 1 - shift, HALO, cols)
            energy = unit_energy(element_modes(before, after))
            totals[-1] = totals[-1] + field_ref[plane - HALO_X, 8 + HALO : 8 + HALO + cols, :] * energy
            before = after
    for index, total in enumerate(totals):
        totals_ref[index] = total


def add_dots(totals, p, w):
    totals = list(totals)
    for component in range(3):
        ps = [p(level, component) for level in range(BASIS)]
        ws = [w(level, component) for level in range(BASIS)]
        for index, (i, j) in enumerate(PAIR_LIST):
            totals[index] = totals[index] + ps[i] * ws[j]
    return totals


def outer_kernel(
    shape, ext, low_x, high_x, first, second, p_in, w_in, field_in, inverse_in, totals_in, p_ref, sums_out, *scratch
):
    rows, cols, depth = shape
    wide, long, shift = cols + 2 * HALO, rows + 2 * HALO_X, HALO_X - 1
    halo_ref, field_ref, inverse_ref, w_ref, z_ref, *both = scratch
    cuts = grid_cuts(rows)
    own = range(HALO_X, HALO_X + rows)
    z_ref[:, :, :, wide:, :] = jnp.zeros((3, 2, long, 8, depth), jnp.float32)
    field_ref[:, :8, :] = jnp.zeros((long, 8, depth), jnp.float32)

    def rims(low, high):
        for rim, begin in ((low, 0), (high, HALO_X)):
            for field in range(FIELDS):
                for layer in range(HALO_X):
                    row = layer * 2 * HALO
                    halo_ref[field, begin + layer, :HALO, :] = rim[field, row : row + HALO, :]
                    halo_ref[field, begin + layer, HALO + cols :, :] = rim[field, row + HALO : row + 2 * HALO, :]

    by_parity("gx", first, second, rims)
    for middle, begin in ((low_x, 0), (high_x, HALO_X)):
        for field in range(FIELDS):
            for layer in range(HALO_X):
                window = slice(layer * cols, (layer + 1) * cols)
                halo_ref[field, begin + layer, HALO : HALO + cols, :] = middle[field, window, :]

    def given(field, plane, begin=0, count=wide):
        if plane in own:
            row = (plane - HALO_X) * wide + begin
            return ext[field, row : row + count, :]
        return halo_ref[field, plane if plane < HALO_X else plane - rows, begin : begin + count, :]

    def fields(plane, begin=0, count=wide):
        if plane in own:
            return field_in[plane - HALO_X, 8 + begin : 8 + begin + count, :]
        return field_ref[plane, 8 + begin : 8 + begin + count, :]

    def inverses(plane):
        return inverse_in[plane - HALO_X] if HALO_X < plane < HALO_X + rows else inverse_ref[plane]

    def is_inner(level, plane):
        return HALO_X + 1 + level <= plane <= HALO_X + rows - 1 - level

    def p(level, component, plane, begin=0, count=wide):
        if is_inner(level, plane):
            return p_in[level, component, plane - shift, begin : begin + count, :]
        return p_ref[level, component, plane, begin : begin + count, :]

    def w(level, component, plane, begin=0, count=wide):
        if is_inner(level, plane):
            return w_in[level, component, plane - shift, begin : begin + count, :]
        if level == 0:
            return given(2 + component, plane, begin, count)
        return w_ref[level, component, plane, begin : begin + count, :]

    def set_p(level, component, plane, value):
        p_ref[level, component, plane] = value

    def set_w(level, component, plane, value):
        w_ref[level, component, plane] = value

    sides = [
        Stages(shape, fields, inverses, p, w, set_p, set_w, z_ref, both[0], both[1], both[2]),
        Stages(shape, fields, inverses, p, w, set_p, set_w, z_ref, both[3], both[4], both[5]),
    ]
    for plane in range(long):
        if plane not in own:
            field_ref[plane, 8:, :] = moduli_of(given(0, plane))
    edge_planes = [*range(1, HALO_X + 1), *range(HALO_X + rows, long)]
    for plane in edge_planes:
        around = fields(plane - 1) + fields(plane - 1, -1)
        if plane - 1 in cuts:
            around = around * cuts[plane - 1]
        around = around + (fields(plane) + fields(plane, -1))
        inverse = inverse_of(given(1, plane), sides[0].lift_moduli(around))
        inverse_ref[plane] = inverse
        for component in range(3):
            set_p(0, component, plane, given(2 + component, plane) * inverse)
    for plane in edge_planes:
        sides[0].produce(0, plane, plane)

    count = HALO_X + 1
    for level in range(BASIS - 1):
        for plane in (HALO_X + 1 + level, HALO_X + 2 + level, HALO_X + rows - 2 - level, HALO_X + rows - 1 - level):
            sides[0].produce(level, plane, plane)
        left, right = 1 + level, HALO_X + rows - 2 - level
        sweep(level, [(sides[0], left, count, left + 1), (sides[1], right, count, right + 1)], cuts, 0)

    last = BASIS - 1
    for plane in (HALO_X + 1 + last, HALO_X + rows - 1 - last):
        sides[0].produce(last, plane, plane)
    totals = [totals_in[index] for index in range(len(PAIR_LIST) + 1)]
    for plane in own:
        if not is_inner(last, plane):
            totals = add_dots(
                totals,
                lambda level, component: p(level, component, plane, HALO, cols),
                lambda level, component: w(level, component, plane, HALO, cols),
            )
        if not (is_inner(last, plane) and is_inner(last, plane + 1)):
            before = load_modes(z_ref, plane, HALO, cols)
            after = cut_off(load_modes(z_ref, plane + 1, HALO, cols), cuts.get(plane))
            energy = unit_energy(element_modes(before, after))
            totals[-1] = totals[-1] + fields(plane, HALO, cols) * energy
    slots = lane_index((1, 128))
    line = jnp.zeros((1, 128), jnp.float32)
    for index, total in enumerate(totals):
        share = jnp.sum(jnp.sum(total, axis=0, keepdims=True), axis=1, keepdims=True)
        line = line + jnp.where(slots == index, share, 0.0)
    sums_out[...] = jnp.broadcast_to(line, sums_out.shape)


def coefficients(shares):
    line = jnp.sum(shares, axis=0, keepdims=True)
    slots = lane_index(line.shape)

    def entry(index):
        return jnp.sum(jnp.where(slots == index, line, 0.0), axis=1, keepdims=True)

    inner = {}
    for index, (i, j) in enumerate(PAIR_LIST):
        inner[i, j] = inner[j, i] = entry(index)
    energy = {(BASIS - 1, BASIS - 1): entry(len(PAIR_LIST))}
    for i in range(BASIS):
        for j in range(min(i + 1, BASIS - 1)):
            energy[i, j] = inner[i, j + 1] + inner[i, j]
    lower, pivot, inverse, solved = {}, {}, {}, {}
    for k in range(BASIS):
        left = energy[k, k]
        for m in range(k):
            left = left - lower[k, m] * lower[k, m] * pivot[m]
        sound = left > 1e-6 * energy[k, k]
        pivot[k] = jnp.where(sound, left, 0.0)
        inverse[k] = jnp.where(sound, 1.0 / jnp.where(sound, left, 1.0), 0.0)
        for i in range(k + 1, BASIS):
            part = energy[i, k]
            for m in range(k):
                part = part - lower[i, m] * lower[k, m] * pivot[m]
            lower[i, k] = part * inverse[k]
    for k in range(BASIS):
        part = inner[k, 0]
        for m in range(k):
            part = part - lower[k, m] * solved[m]
        solved[k] = part
    result = {}
    for k in reversed(range(BASIS)):
        part = solved[k] * inverse[k]
        for m in range(k + 1, BASIS):
            part = part - lower[m, k] * result[m]
        result[k] = part
    return [result[k] for k in range(BASIS)]


def energy_kernel(
    shape, shares, inner, outer, own, low_x, high_x, u_out, weighted, first, second, u_ref, z_ref
):
    rows, cols, depth = shape
    wide, planes = cols + 2 * HALO, rows + 2 * REACH
    keep_last = jnp.where(lane_index((wide, depth)) < depth - 1, 1.0, 0.0)
    parts = [jnp.broadcast_to(part, (wide, depth)) for part in coefficients(shares[...])]
    cuts = grid_cuts(rows)
    for plane in range(planes + 1):
        source = plane + HALO_X - REACH
        for component in range(3):
            total = None
            for level in range(BASIS):
                if HALO_X + 1 + level <= source <= HALO_X + rows - 1 - level:
                    term = parts[level] * inner[level, component, source - HALO_X + 1]
                else:
                    term = parts[level] * outer[level, component, source]
                total = term if total is None else total + term
            lifted = pltpu.roll(total, depth - 1, 1) * keep_last
            z_ref[component, 0, plane] = lifted + total
            z_ref[component, 1, plane] = lifted - total
            row = plane - REACH
            if 0 <= row < rows:
                u_ref[component, row] = total
                u_out[component, row] = u_ref[component, row, HALO : HALO + cols, :]
    before = load_modes(z_ref, 0, HALO, cols)
    for plane in range(planes):
        row = plane - REACH
        after = load_modes(z_ref, plane + 1, HALO, cols)
        energy = unit_energy(element_modes(before, cut_off(after, cuts.get(row + HALO_X))))
        before = after
        if row < 0:
            rho = low_x[0, (row + HALO_X) * cols : (row + HALO_X + 1) * cols, :]
        elif row < rows:
            rho = own[0, row * cols : (row + 1) * cols, :]
        else:
            rho = high_x[0, (row - rows) * cols : (row - rows + 1) * cols, :]
        weighted[plane * cols : (plane + 1) * cols, :] = rho * (3.0 * rho * rho * (1.0 - E_MIN) * energy)

    def outer_rows(low, high):
        for layer in range(REACH):
            low[layer] = weighted[pl.ds(layer, planes, stride=cols), :]
            high[layer] = weighted[pl.ds(cols - REACH + layer, planes, stride=cols), :]

    by_parity("gy", first, second, outer_rows)


def cone_table():
    table, total = {}, 0.0
    for a in range(-2, 3):
        for b in range(-2, 3):
            for c in range(-2, 3):
                total += max(0.0, 3.0 - math.sqrt(a * a + b * b + c * c))
    for flat in (0, 1, 2, 4, 5, 8):
        for c in range(3):
            table[flat, c] = max(0.0, 3.0 - math.sqrt(flat + c * c))
    return table, total


def volume_row(total):
    return jnp.sum(total, axis=0, keepdims=True)


def filter_kernel(shape, weighted, from_first, from_second, own, lower, upper, root, volume, plane_ref):
    rows, cols, depth = shape
    wide, planes = cols + 8, rows + 2 * REACH
    table, total = cone_table()
    for plane in range(planes):
        plane_ref[plane * wide + REACH : plane * wide + REACH + cols, :] = weighted[plane * cols : (plane + 1) * cols, :]

    def neighbour_rows(from_low, from_high):
        for layer in range(REACH):
            plane_ref[pl.ds(layer, planes, stride=wide), :] = from_low[layer]
            plane_ref[pl.ds(REACH + cols + layer, planes, stride=wide), :] = from_high[layer]

    by_parity("gy", from_first, from_second, neighbour_rows)
    volume_sum = jnp.zeros((cols, depth), jnp.float32)
    for row in range(rows):
        spread = {}
        for a in range(-REACH, REACH + 1):
            for b in range(-REACH, REACH + 1):
                key = a * a + b * b
                value = plane_ref[pl.ds((row + REACH + a) * wide + REACH + b, cols), :]
                spread[key] = value if key not in spread else spread[key] + value
        sums = []
        for c in range(3):
            part = None
            for key, value in spread.items():
                if table[key, c] > 0.0:
                    term = table[key, c] * value
                    part = term if part is None else part + term
            sums.append(part)
        convolved = sums[0]
        for c in (1, 2):
            convolved = convolved + (pltpu.roll(sums[c], c, 1) + pltpu.roll(sums[c], depth - c, 1))
        window = slice(row * cols, (row + 1) * cols)
        rho = own[0, window, :]
        base = rho * jnp.sqrt(convolved / (total * rho))
        root[window, :] = base
        volume_sum = volume_sum + jnp.minimum(jnp.maximum(base, lower[window, :]), upper[window, :])
    volume[...] = jnp.broadcast_to(volume_row(volume_sum), volume.shape)


def scale_of(target, volumes):
    scale = None
    for volume in volumes:
        whole = jnp.sum(jnp.sum(volume[...], axis=0, keepdims=True), axis=1, keepdims=True)
        ratio = target / whole
        scale = ratio if scale is None else scale * ratio
    return scale


def trial_of(target, volumes, terms):
    root, lower, upper = terms
    return jnp.minimum(jnp.maximum(root[...] * scale_of(target, volumes), lower[...]), upper[...])


def trial_kernel(target, *refs):
    *volumes, root, lower, upper, out = refs
    out[...] = jnp.broadcast_to(volume_row(trial_of(target, volumes, (root, lower, upper))), out.shape)


def update_kernel(target, u, *refs):
    *volumes, root, lower, upper, new_density, displacement, made, sent = refs
    copies = [
        pltpu.make_async_copy(u, displacement, sent.at[0]),
        pltpu.make_async_copy(made, new_density, sent.at[1]),
    ]
    copies[0].start()
    made[...] = trial_of(target, volumes, (root, lower, upper))
    copies[1].start()
    for copy in copies:
        copy.wait()


def call(kernel, name, out_shapes, *args, scratch=(), flops=0, space=pltpu.VMEM, far=()):
    shapes = [jax.ShapeDtypeStruct(shape, jnp.float32) for shape in out_shapes]
    moved = sum(4 * math.prod(value.shape) for value in [*args, *shapes])
    return pl.pallas_call(
        kernel,
        name=name,
        out_shape=shapes,
        in_specs=[pl.BlockSpec(memory_space=space)] * len(args),
        out_specs=[pl.BlockSpec(memory_space=pltpu.HBM if i in far else pltpu.VMEM) for i in range(len(shapes))],
        scratch_shapes=[pltpu.VMEM(item, jnp.float32) if isinstance(item, tuple) else item for item in scratch],
        compiler_params=pltpu.CompilerParams(vmem_limit_bytes=VMEM_LIMIT),
        cost_estimate=pl.CostEstimate(flops=flops, bytes_accessed=moved, transcendentals=0),
    )(*args)


def exchange(low, high, axis):
    count = lax.axis_size(axis)
    from_low = lax.ppermute(high, axis, [(i, (i + 1) % count) for i in range(count)])
    from_high = lax.ppermute(low, axis, [((i + 1) % count, i) for i in range(count)])
    return from_low, from_high


def swap(first, second, axis, wrap):
    count = lax.axis_size(axis)
    assert count % 2 == 0
    ends = [(i, i + 1) for i in range(1, count - 1, 2)] + ([(count - 1, 0)] if wrap else [])
    pairs = [(i, i + 1) for i in range(0, count, 2)]
    both = lambda links: links + [(j, i) for i, j in links]
    return lax.ppermute(first, axis, both(pairs)), lax.ppermute(second, axis, both(ends))


def everyone(shares):
    return lax.all_to_all(shares, AXES, 0, 0, tiled=True)


def shards(density, void_mask, solid_mask, fixed_mask, load_mask, traction):
    shape = rows, cols, depth = density.shape
    devices = lax.axis_size("gx") * lax.axis_size("gy")
    wide, long = cols + 2 * HALO, rows + 2 * HALO_X
    planes = rows + 2 * REACH
    named = lambda kernel: functools.partial(kernel, shape)
    flat = (rows * cols, depth)
    inputs = [
        pltpu.with_memory_space_constraint(value.reshape(*value.shape[:-3], *flat), pltpu.HBM)
        for value in (density, void_mask, solid_mask, fixed_mask, load_mask, traction)
    ]

    own, lower, upper, first, second, low_x, high_x = call(
        named(fields_kernel),
        "fields",
        [
            (FIELDS, *flat),
            flat,
            flat,
            (HALO, FIELDS, rows, depth),
            (HALO, FIELDS, rows, depth),
            (FIELDS, HALO_X * cols, depth),
            (FIELDS, HALO_X * cols, depth),
        ],
        *inputs,
        scratch=[pltpu.VMEM(value.shape, value.dtype) for value in inputs] + [pltpu.SemaphoreType.DMA((8,))],
        space=pltpu.HBM,
    )
    from_first, from_second = swap(first, second, "gy", False)
    low_x, high_x = exchange(low_x, high_x, "gx")
    ext, first, second = call(
        named(widen_kernel),
        "widen",
        [(FIELDS, rows * wide, depth)] + [(FIELDS, HALO_X * 2 * HALO, depth)] * 2,
        own,
        from_first,
        from_second,
    )
    first_xy, second_xy = swap(first, second, "gx", True)
    side = [(12, wide, depth), (12, wide, depth), (3, 2, wide, depth)]
    inner = call(
        named(inner_kernel),
        "inner",
        [
            (BASIS, 3, rows + 1, wide, depth),
            (BASIS, 3, rows + 1, wide, depth),
            (rows, 8 + wide, depth),
            (rows, wide, depth),
            (len(PAIR_LIST) + 1, cols, depth),
        ],
        ext,
        scratch=[(3, 2, rows + 1, wide + 8, depth), *side],
    )
    outer, sums = call(
        named(outer_kernel),
        "outer",
        [(BASIS, 3, long, wide, depth), (devices, 128)],
        ext,
        low_x,
        high_x,
        first_xy,
        second_xy,
        *inner,
        scratch=[
            (FIELDS, 2 * HALO_X, wide, depth),
            (long, 8 + wide, depth),
            (long, wide, depth),
            (BASIS, 3, long, wide, depth),
            (3, 2, long, wide + 8, depth),
            *side,
            *side,
        ],
    )
    u, weighted, first, second = call(
        named(energy_kernel),
        "energy",
        [(3, rows, cols, depth), (planes * cols, depth), (REACH, planes, depth), (REACH, planes, depth)],
        everyone(sums),
        inner[0],
        outer,
        own,
        low_x,
        high_x,
        scratch=[
            (3, rows, wide, depth),
            (3, 2, planes + 1, wide, depth),
        ],
    )
    from_first, from_second = swap(first, second, "gy", True)
    root, volume = call(
        named(filter_kernel),
        "filter",
        [flat, (devices, depth)],
        weighted,
        from_first,
        from_second,
        own,
        lower,
        upper,
        scratch=[(planes * (cols + 8), depth)],
    )
    target = VOLUME_SHARE * rows * cols * depth * devices
    terms, volumes = (root, lower, upper), [everyone(volume)]
    for _ in range(2):
        (volume,) = call(functools.partial(trial_kernel, target), "trial", [(devices, depth)], *volumes, *terms)
        volumes.append(everyone(volume))
    new_density, displacement = call(
        functools.partial(update_kernel, target),
        "update",
        [flat, u.shape],
        u,
        *volumes,
        *terms,
        scratch=[flat, pltpu.SemaphoreType.DMA((2,))],
        far=(0, 1),
    )
    return new_density.reshape(shape), displacement


def solution(mesh):
    placed = (P("gx", "gy", None),) * 5 + (P(None, "gx", "gy", None),)
    return jax.shard_map(
        shards,
        mesh=mesh,
        in_specs=placed,
        out_specs=(P("gx", "gy", None), P(None, "gx", "gy", None)),
        check_vma=False,
    )
```

```python
import functools
import math

import jax
import jax.numpy as jnp
import numpy as np
from jax import lax
from jax.experimental import pallas as pl
from jax.experimental.pallas import tpu as pltpu
from jax.sharding import PartitionSpec as P

E_MIN = 0.001
RHO_FLOOR = 0.001
MOVE_LIMIT = 0.2
VOLUME_SHARE = 0.4
BASIS = 4
REACH = 2
HALO = BASIS
HALO_X = BASIS + REACH
AXES = ("gx", "gy")
FIELDS = 5
VMEM_LIMIT = 40 * 1024 * 1024

POISSON = 0.3
LAME = POISSON / ((1.0 + POISSON) * (1.0 - 2.0 * POISSON))
SHEAR = 1.0 / (2.0 * (1.0 + POISSON))
NORMAL = 2.0 * SHEAR / 16.0
TRACE = LAME / 16.0
SHEAR_FIRST = SHEAR / 16.0
BEND = (LAME + 3.0 * SHEAR) / 48.0
BEND_MIX = LAME / 48.0
TWIST = SHEAR / 48.0
THIRD = (LAME + 4.0 * SHEAR) / 144.0
DIAGONAL = NORMAL + TRACE + 2.0 * SHEAR_FIRST + 2.0 * BEND + 2.0 * TWIST + THIRD
PAIRS = (("xdds", "zsdd"), ("ydds", "zdsd"), ("xdsd", "ysdd"))
TRIPLE = ("zdds", "ydsd", "xsdd")
CLASSES = [c + y + z for c in "xyz" for y in "sd" for z in "sd"]


def by_parity(axis, first, second, body):
    even = lax.rem(lax.axis_index(axis), 2) == 0
    pl.when(even)(lambda: body(first, second))
    pl.when(jnp.logical_not(even))(lambda: body(second, first))


def lane_index(shape):
    return lax.broadcasted_iota(jnp.int32, shape, len(shape) - 1)


def load_modes(z_ref, plane, begin, count):
    modes = {}
    for number, component in enumerate("xyz"):
        for index, z in enumerate("sd"):
            low = z_ref[number, index, plane, begin : begin + count, :]
            high = z_ref[number, index, plane, begin + 1 : begin + 1 + count, :]
            modes[component + "s" + z] = high + low
            modes[component + "d" + z] = high - low
    return modes


def element_modes(before, after):
    modes = {}
    for key in CLASSES:
        if key[1:] != "ss":
            modes[key[0] + "s" + key[1:]] = after[key] + before[key]
        modes[key[0] + "d" + key[1:]] = after[key] - before[key]
    return modes


def mode_forces(u, moduli):
    forces = {}
    normal = moduli * NORMAL
    trace = (u["xdss"] + u["ysds"] + u["zssd"]) * (TRACE / NORMAL)
    for key in ("xdss", "ysds", "zssd"):
        forces[key] = normal * (u[key] + trace)
    shear = moduli * SHEAR_FIRST
    for one, other in (("ydss", "xsds"), ("zsds", "yssd"), ("xssd", "zdss")):
        forces[one] = forces[other] = shear * (u[one] + u[other])
    bend = moduli * BEND
    for one, other in PAIRS:
        forces[one] = bend * (u[one] + (BEND_MIX / BEND) * u[other])
        forces[other] = bend * (u[other] + (BEND_MIX / BEND) * u[one])
    twist = moduli * TWIST
    total = u[TRIPLE[0]] + u[TRIPLE[1]] + u[TRIPLE[2]]
    for key in TRIPLE:
        forces[key] = twist * (total + u[key])
    third = moduli * THIRD
    for component in "xyz":
        forces[component + "ddd"] = third * u[component + "ddd"]
    return forces


def unit_energy(u):
    trace = u["xdss"] + u["ysds"] + u["zssd"]
    energy = TRACE * (trace * trace)
    energy += NORMAL * (u["xdss"] ** 2 + u["ysds"] ** 2 + u["zssd"] ** 2)
    shears = [u[a] + u[b] for a, b in (("ydss", "xsds"), ("zsds", "yssd"), ("xssd", "zdss"))]
    energy += SHEAR_FIRST * (shears[0] ** 2 + shears[1] ** 2 + shears[2] ** 2)
    squares, mixed = 0.0, 0.0
    for one, other in PAIRS:
        squares += u[one] ** 2 + u[other] ** 2
        mixed += (u[one] + u[other]) ** 2
    energy += (BEND - BEND_MIX) * squares + BEND_MIX * mixed
    total = u[TRIPLE[0]] + u[TRIPLE[1]] + u[TRIPLE[2]]
    squares = total * total
    for key in TRIPLE:
        squares += u[key] ** 2
    energy += TWIST * squares
    energy += THIRD * (u["xddd"] ** 2 + u["yddd"] ** 2 + u["zddd"] ** 2)
    return energy


def fields_kernel(shape, *refs):
    rows, cols, _ = shape
    (density_in, void_in, solid_in, fixed_in, load_in, traction_in) = refs[:6]
    (own, lower, upper, first, second, low_x, high_x) = refs[6:13]
    density, void, solid, fixed, load, traction, arrived = refs[13:]
    pieces = [(fixed_in, fixed), (load_in, load)]
    pieces += [(traction_in.at[component], traction.at[component]) for component in range(3)]
    pieces += [(density_in, density), (void_in, void), (solid_in, solid)]
    copies = [pltpu.make_async_copy(s, t, arrived.at[i]) for i, (s, t) in enumerate(pieces)]
    for copy in copies:
        copy.start()

    def send(field):
        low_x[field] = own[field, : HALO_X * cols, :]
        high_x[field] = own[field, (rows - HALO_X) * cols :, :]

        def outer_rows(low, high):
            for layer in range(HALO):
                low[layer, field] = own[field, pl.ds(layer, rows, stride=cols), :]
                high[layer, field] = own[field, pl.ds(cols - HALO + layer, rows, stride=cols), :]

        by_parity("gy", first, second, outer_rows)

    copies[0].wait()
    copies[1].wait()
    free = (1 - fixed[...]).astype(jnp.float32)
    own[1] = free
    send(1)
    for component in range(3):
        copies[2 + component].wait()
        own[2 + component] = own[1] * load[...].astype(jnp.float32) * traction[component]
        send(2 + component)
    for copy in copies[5:]:
        copy.wait()
    is_solid, is_void = solid[...] == 1, void[...] == 1
    rho = jnp.where(is_solid, 1.0, jnp.where(is_void, RHO_FLOOR, density[...]))
    own[0] = rho
    send(0)
    least = jnp.maximum(RHO_FLOOR, rho - MOVE_LIMIT)
    most = jnp.minimum(1.0, rho + MOVE_LIMIT)
    lower[...] = jnp.where(is_solid, 1.0, jnp.where(is_void, RHO_FLOOR, least))
    upper[...] = jnp.where(is_solid, 1.0, jnp.where(is_void, RHO_FLOOR, most))


def widen_kernel(shape, own, from_first, from_second, ext, first, second):
    rows, cols, _ = shape
    wide = cols + 2 * HALO

    def neighbour_rows(from_low, from_high):
        for field in range(FIELDS):
            for layer in range(HALO):
                ext[field, pl.ds(layer, rows, stride=wide), :] = from_low[layer, field]
                ext[field, pl.ds(cols + HALO + layer, rows, stride=wide), :] = from_high[layer, field]

    by_parity("gy", from_first, from_second, neighbour_rows)
    for field in range(FIELDS):
        for row in range(rows):
            ext[field, pl.ds(row * wide + HALO, cols), :] = own[field, pl.ds(row * cols, cols), :]

    def corners(low, high):
        for target, begin in ((low, 0), (high, rows - HALO_X)):
            for field in range(FIELDS):
                for layer in range(HALO_X):
                    row, source = layer * 2 * HALO, (begin + layer) * wide
                    target[field, row : row + HALO, :] = ext[field, source : source + HALO, :]
                    source += cols + HALO
                    target[field, row + HALO : row + 2 * HALO, :] = ext[field, source : source + HALO, :]

    by_parity("gx", first, second, corners)


def grid_cuts(rows):
    place, last = lax.axis_index("gx"), lax.axis_size("gx") - 1
    return {
        HALO_X - 1: jnp.where(place == 0, 0.0, 1.0),
        HALO_X + rows - 1: jnp.where(place == last, 0.0, 1.0),
    }


def cut_off(values, keep):
    return values if keep is None else {key: value * keep for key, value in values.items()}


class Stages:
    def __init__(self, shape, fields, inverses, p, w, set_p, set_w, z_ref, mode_ref, lift_ref, pipe_ref):
        self.wide, self.depth = shape[1] + 2 * HALO, shape[2]
        lanes = lane_index((self.wide, self.depth))
        self.keep_last = jnp.where(lanes < self.depth - 1, 1.0, 0.0)
        self.keep_first = jnp.where(lanes > 0, 1.0, 0.0)
        self.fields, self.inverses, self.p, self.w = fields, inverses, p, w
        self.set_p, self.set_w = set_p, set_w
        self.z_ref, self.mode_ref, self.lift_ref, self.pipe_ref = z_ref, mode_ref, lift_ref, pipe_ref

    def lift_moduli(self, around):
        return around + pltpu.roll(around, 1, 1) * self.keep_first

    def produce(self, level, plane, slot):
        for component in range(3):
            value = self.p(level, component, plane)
            lifted = pltpu.roll(value, self.depth - 1, 1) * self.keep_last
            self.z_ref[component, 0, slot, : self.wide] = lifted + value
            self.z_ref[component, 1, slot, : self.wide] = lifted - value

    def begin(self, slot):
        modes = load_modes(self.z_ref, slot, 0, self.wide)
        for index, key in enumerate(CLASSES):
            self.mode_ref[index] = modes[key]
            self.lift_ref[index] = jnp.zeros((self.wide, self.depth), jnp.float32)

    def spread(self, plane, slot, keep=None):
        after = load_modes(self.z_ref, slot, 0, self.wide)
        before = {key: self.mode_ref[index] for index, key in enumerate(CLASSES)}
        lift = {key: self.lift_ref[index] for index, key in enumerate(CLASSES)}
        forces = mode_forces(element_modes(before, cut_off(after, keep)), self.fields(plane))
        for number, component in enumerate("xyz"):
            along_z = {}
            for z in "sd":
                along_y = {}
                for y in "sd":
                    key = component + y + z
                    slope = forces[component + "d" + y + z]
                    if y + z == "ss":
                        along_y[y] = lift[key] - slope
                        lift[key] = slope
                    else:
                        mean = forces[component + "s" + y + z]
                        along_y[y] = lift[key] + (mean - slope)
                        lift[key] = mean + slope
                along_z[z] = (along_y["s"] - along_y["d"]) + pltpu.roll(along_y["s"] + along_y["d"], 1, 0)
            self.pipe_ref[number, 0] = along_z["s"] + along_z["d"]
            self.pipe_ref[number, 1] = along_z["s"] - along_z["d"]
        lift = cut_off(lift, keep)
        for index, key in enumerate(CLASSES):
            self.mode_ref[index] = after[key]
            self.lift_ref[index] = lift[key]

    def finish(self, level, plane):
        for component in range(3):
            shifted = pltpu.roll(self.pipe_ref[component, 0], 1, 1) * self.keep_first
            residual = (self.pipe_ref[component, 1] + shifted) - self.w(level, component, plane)
            self.set_w(level + 1, component, plane, residual)
            self.set_p(level + 1, component, plane, residual * self.inverses(plane))


def sweep(level, sides, cuts, shift):
    for side, start, count, wanted in sides:
        side.begin(start - shift)
    for step in range(max(count for _, _, count, _ in sides) + 2):
        for side, start, count, wanted in sides:
            plane, end = start + step, start + count
            if wanted <= plane - 2 < end:
                side.produce(level + 1, plane - 2, plane - 2 - shift)
            if wanted <= plane - 1 < end:
                side.finish(level, plane - 1)
            if plane < end:
                side.spread(plane, plane + 1 - shift, cuts.get(plane))


def moduli_of(rho):
    return jnp.where(rho > 0.0, E_MIN + rho * rho * rho * (1.0 - E_MIN), 0.0)


def inverse_of(free, around):
    return free / (free * (DIAGONAL * around) + (1.0 - free))


PAIR_LIST = [(i, j) for i in range(BASIS) for j in range(i + 1)]


def inner_kernel(shape, ext, p_ref, w_ref, field_ref, inverse_ref, totals_ref, z_ref, mode_ref, lift_ref, pipe_ref):
    rows, cols, depth = shape
    wide, shift = cols + 2 * HALO, HALO_X - 1
    field_ref[:, :8, :] = jnp.zeros((rows, 8, depth), jnp.float32)
    z_ref[:, :, :, wide:, :] = jnp.zeros((3, 2, z_ref.shape[2], 8, depth), jnp.float32)
    for row in range(rows):
        window = slice(row * wide, (row + 1) * wide)
        field_ref[row, 8:, :] = moduli_of(ext[0, window, :])
        for component in range(3):
            w_ref[0, component, row + 1] = ext[2 + component, window, :]

    def store(ref):
        def put(level, component, plane, value):
            ref[level, component, plane - shift] = value

        return put

    stages = Stages(
        shape,
        lambda plane: field_ref[plane - HALO_X, 8:, :],
        lambda plane: inverse_ref[plane - HALO_X],
        lambda level, component, plane: p_ref[level, component, plane - shift],
        lambda level, component, plane: w_ref[level, component, plane - shift],
        store(p_ref),
        store(w_ref),
        z_ref,
        mode_ref,
        lift_ref,
        pipe_ref,
    )
    inverse_ref[0] = jnp.zeros((wide, depth), jnp.float32)
    for row in range(1, rows):
        around = field_ref[row - 1, 8:, :] + field_ref[row - 1, 7 : 7 + wide, :]
        around = around + (field_ref[row, 8:, :] + field_ref[row, 7 : 7 + wide, :])
        inverse = inverse_of(ext[1, row * wide : (row + 1) * wide, :], stages.lift_moduli(around))
        inverse_ref[row] = inverse
        for component in range(3):
            p_ref[0, component, row + 1] = w_ref[0, component, row + 1] * inverse
    for row in range(1, rows):
        stages.produce(0, row + HALO_X, row + 1)

    for level in range(BASIS - 1):
        start, count = HALO_X + 1 + level, rows - 2 - 2 * level
        sweep(level, [(stages, start, count, start + 1)], {}, shift)

    first, last = HALO_X + BASIS, HALO_X + rows - 1 - (BASIS - 1)
    totals = [jnp.zeros((cols, depth), jnp.float32)] * (len(PAIR_LIST) + 1)
    before = load_modes(z_ref, first - shift, HALO, cols)
    for plane in range(first, last + 1):
        totals = add_dots(
            totals,
            lambda level, component: p_ref[level, component, plane - shift, HALO : HALO + cols, :],
            lambda level, component: w_ref[level, component, plane - shift, HALO : HALO + cols, :],
        )
        if plane < last:
            after = load_modes(z_ref, plane + 1 - shift, HALO, cols)
            energy = unit_energy(element_modes(before, after))
            totals[-1] = totals[-1] + field_ref[plane - HALO_X, 8 + HALO : 8 + HALO + cols, :] * energy
            before = after
    for index, total in enumerate(totals):
        totals_ref[index] = total


def add_dots(totals, p, w):
    totals = list(totals)
    for component in range(3):
        ps = [p(level, component) for level in range(BASIS)]
        ws = [w(level, component) for level in range(BASIS)]
        for index, (i, j) in enumerate(PAIR_LIST):
            totals[index] = totals[index] + ps[i] * ws[j]
    return totals


def outer_kernel(
    shape, ext, low_x, high_x, first, second, p_in, w_in, field_in, inverse_in, totals_in, p_ref, sums_out, *scratch
):
    rows, cols, depth = shape
    wide, long, shift = cols + 2 * HALO, rows + 2 * HALO_X, HALO_X - 1
    halo_ref, field_ref, inverse_ref, w_ref, z_ref, *both = scratch
    cuts = grid_cuts(rows)
    own = range(HALO_X, HALO_X + rows)
    z_ref[:, :, :, wide:, :] = jnp.zeros((3, 2, long, 8, depth), jnp.float32)
    field_ref[:, :8, :] = jnp.zeros((long, 8, depth), jnp.float32)

    def rims(low, high):
        for rim, begin in ((low, 0), (high, HALO_X)):
            for field in range(FIELDS):
                for layer in range(HALO_X):
                    row = layer * 2 * HALO
                    halo_ref[field, begin + layer, :HALO, :] = rim[field, row : row + HALO, :]
                    halo_ref[field, begin + layer, HALO + cols :, :] = rim[field, row + HALO : row + 2 * HALO, :]

    by_parity("gx", first, second, rims)
    for middle, begin in ((low_x, 0), (high_x, HALO_X)):
        for field in range(FIELDS):
            for layer in range(HALO_X):
                window = slice(layer * cols, (layer + 1) * cols)
                halo_ref[field, begin + layer, HALO : HALO + cols, :] = middle[field, window, :]

    def given(field, plane, begin=0, count=wide):
        if plane in own:
            row = (plane - HALO_X) * wide + begin
            return ext[field, row : row + count, :]
        return halo_ref[field, plane if plane < HALO_X else plane - rows, begin : begin + count, :]

    def fields(plane, begin=0, count=wide):
        if plane in own:
            return field_in[plane - HALO_X, 8 + begin : 8 + begin + count, :]
        return field_ref[plane, 8 + begin : 8 + begin + count, :]

    def inverses(plane):
        return inverse_in[plane - HALO_X] if HALO_X < plane < HALO_X + rows else inverse_ref[plane]

    def is_inner(level, plane):
        return HALO_X + 1 + level <= plane <= HALO_X + rows - 1 - level

    def p(level, component, plane, begin=0, count=wide):
        if is_inner(level, plane):
            return p_in[level, component, plane - shift, begin : begin + count, :]
        return p_ref[level, component, plane, begin : begin + count, :]

    def w(level, component, plane, begin=0, count=wide):
        if is_inner(level, plane):
            return w_in[level, component, plane - shift, begin : begin + count, :]
        if level == 0:
            return given(2 + component, plane, begin, count)
        return w_ref[level, component, plane, begin : begin + count, :]

    def set_p(level, component, plane, value):
        p_ref[level, component, plane] = value

    def set_w(level, component, plane, value):
        w_ref[level, component, plane] = value

    sides = [
        Stages(shape, fields, inverses, p, w, set_p, set_w, z_ref, both[0], both[1], both[2]),
        Stages(shape, fields, inverses, p, w, set_p, set_w, z_ref, both[3], both[4], both[5]),
    ]
    for plane in range(long):
        if plane not in own:
            field_ref[plane, 8:, :] = moduli_of(given(0, plane))
    edge_planes = [*range(1, HALO_X + 1), *range(HALO_X + rows, long)]
    for plane in edge_planes:
        around = fields(plane - 1) + fields(plane - 1, -1)
        if plane - 1 in cuts:
            around = around * cuts[plane - 1]
        around = around + (fields(plane) + fields(plane, -1))
        inverse = inverse_of(given(1, plane), sides[0].lift_moduli(around))
        inverse_ref[plane] = inverse
        for component in range(3):
            set_p(0, component, plane, given(2 + component, plane) * inverse)
    for plane in edge_planes:
        sides[0].produce(0, plane, plane)

    count = HALO_X + 1
    for level in range(BASIS - 1):
        for plane in (HALO_X + 1 + level, HALO_X + 2 + level, HALO_X + rows - 2 - level, HALO_X + rows - 1 - level):
            sides[0].produce(level, plane, plane)
        left, right = 1 + level, HALO_X + rows - 2 - level
        sweep(level, [(sides[0], left, count, left + 1), (sides[1], right, count, right + 1)], cuts, 0)

    last = BASIS - 1
    for plane in (HALO_X + 1 + last, HALO_X + rows - 1 - last):
        sides[0].produce(last, plane, plane)
    totals = [totals_in[index] for index in range(len(PAIR_LIST) + 1)]
    for plane in own:
        if not is_inner(last, plane):
            totals = add_dots(
                totals,
                lambda level, component: p(level, component, plane, HALO, cols),
                lambda level, component: w(level, component, plane, HALO, cols),
            )
        if not (is_inner(last, plane) and is_inner(last, plane + 1)):
            before = load_modes(z_ref, plane, HALO, cols)
            after = cut_off(load_modes(z_ref, plane + 1, HALO, cols), cuts.get(plane))
            energy = unit_energy(element_modes(before, after))
            totals[-1] = totals[-1] + fields(plane, HALO, cols) * energy
    slots = lane_index((1, 128))
    line = jnp.zeros((1, 128), jnp.float32)
    for index, total in enumerate(totals):
        share = jnp.sum(jnp.sum(total, axis=0, keepdims=True), axis=1, keepdims=True)
        line = line + jnp.where(slots == index, share, 0.0)
    sums_out[...] = jnp.broadcast_to(line, sums_out.shape)


def coefficients(shares):
    line = jnp.sum(shares, axis=0, keepdims=True)
    slots = lane_index(line.shape)

    def entry(index):
        return jnp.sum(jnp.where(slots == index, line, 0.0), axis=1, keepdims=True)

    inner = {}
    for index, (i, j) in enumerate(PAIR_LIST):
        inner[i, j] = inner[j, i] = entry(index)
    energy = {(BASIS - 1, BASIS - 1): entry(len(PAIR_LIST))}
    for i in range(BASIS):
        for j in range(min(i + 1, BASIS - 1)):
            energy[i, j] = inner[i, j + 1] + inner[i, j]
    lower, pivot, inverse, solved = {}, {}, {}, {}
    for k in range(BASIS):
        left = energy[k, k]
        for m in range(k):
            left = left - lower[k, m] * lower[k, m] * pivot[m]
        sound = left > 1e-6 * energy[k, k]
        pivot[k] = jnp.where(sound, left, 0.0)
        inverse[k] = jnp.where(sound, 1.0 / jnp.where(sound, left, 1.0), 0.0)
        for i in range(k + 1, BASIS):
            part = energy[i, k]
            for m in range(k):
                part = part - lower[i, m] * lower[k, m] * pivot[m]
            lower[i, k] = part * inverse[k]
    for k in range(BASIS):
        part = inner[k, 0]
        for m in range(k):
            part = part - lower[k, m] * solved[m]
        solved[k] = part
    result = {}
    for k in reversed(range(BASIS)):
        part = solved[k] * inverse[k]
        for m in range(k + 1, BASIS):
            part = part - lower[m, k] * result[m]
        result[k] = part
    return [result[k] for k in range(BASIS)]


def energy_kernel(
    shape, shares, inner, outer, own, low_x, high_x, u_out, weighted, first, second, u_ref, z_ref
):
    rows, cols, depth = shape
    wide, planes = cols + 2 * HALO, rows + 2 * REACH
    keep_last = jnp.where(lane_index((wide, depth)) < depth - 1, 1.0, 0.0)
    parts = [jnp.broadcast_to(part, (wide, depth)) for part in coefficients(shares[...])]
    cuts = grid_cuts(rows)
    for plane in range(planes + 1):
        source = plane + HALO_X - REACH
        for component in range(3):
            total = None
            for level in range(BASIS):
                if HALO_X + 1 + level <= source <= HALO_X + rows - 1 - level:
                    term = parts[level] * inner[level, component, source - HALO_X + 1]
                else:
                    term = parts[level] * outer[level, component, source]
                total = term if total is None else total + term
            lifted = pltpu.roll(total, depth - 1, 1) * keep_last
            z_ref[component, 0, plane] = lifted + total
            z_ref[component, 1, plane] = lifted - total
            row = plane - REACH
            if 0 <= row < rows:
                u_ref[component, row] = total
                u_out[component, row] = u_ref[component, row, HALO : HALO + cols, :]
    before = load_modes(z_ref, 0, HALO, cols)
    for plane in range(planes):
        row = plane - REACH
        after = load_modes(z_ref, plane + 1, HALO, cols)
        energy = unit_energy(element_modes(before, cut_off(after, cuts.get(row + HALO_X))))
        before = after
        if row < 0:
            rho = low_x[0, (row + HALO_X) * cols : (row + HALO_X + 1) * cols, :]
        elif row < rows:
            rho = own[0, row * cols : (row + 1) * cols, :]
        else:
            rho = high_x[0, (row - rows) * cols : (row - rows + 1) * cols, :]
        weighted[plane * cols : (plane + 1) * cols, :] = rho * (3.0 * rho * rho * (1.0 - E_MIN) * energy)

    def outer_rows(low, high):
        for layer in range(REACH):
            low[layer] = weighted[pl.ds(layer, planes, stride=cols), :]
            high[layer] = weighted[pl.ds(cols - REACH + layer, planes, stride=cols), :]

    by_parity("gy", first, second, outer_rows)


def cone_table():
    table, total = {}, 0.0
    for a in range(-2, 3):
        for b in range(-2, 3):
            for c in range(-2, 3):
                total += max(0.0, 3.0 - math.sqrt(a * a + b * b + c * c))
    for flat in (0, 1, 2, 4, 5, 8):
        for c in range(3):
            table[flat, c] = max(0.0, 3.0 - math.sqrt(flat + c * c))
    return table, total


def volume_row(total):
    return jnp.sum(total, axis=0, keepdims=True)


def filter_kernel(shape, weighted, from_first, from_second, own, lower, upper, root, volume, plane_ref):
    rows, cols, depth = shape
    wide, planes = cols + 8, rows + 2 * REACH
    table, total = cone_table()
    for plane in range(planes):
        plane_ref[plane * wide + REACH : plane * wide + REACH + cols, :] = weighted[plane * cols : (plane + 1) * cols, :]

    def neighbour_rows(from_low, from_high):
        for layer in range(REACH):
            plane_ref[pl.ds(layer, planes, stride=wide), :] = from_low[layer]
            plane_ref[pl.ds(REACH + cols + layer, planes, stride=wide), :] = from_high[layer]

    by_parity("gy", from_first, from_second, neighbour_rows)
    volume_sum = jnp.zeros((cols, depth), jnp.float32)
    for row in range(rows):
        spread = {}
        for a in range(-REACH, REACH + 1):
            for b in range(-REACH, REACH + 1):
                key = a * a + b * b
                value = plane_ref[pl.ds((row + REACH + a) * wide + REACH + b, cols), :]
                spread[key] = value if key not in spread else spread[key] + value
        sums = []
        for c in range(3):
            part = None
            for key, value in spread.items():
                if table[key, c] > 0.0:
                    term = table[key, c] * value
                    part = term if part is None else part + term
            sums.append(part)
        convolved = sums[0]
        for c in (1, 2):
            convolved = convolved + (pltpu.roll(sums[c], c, 1) + pltpu.roll(sums[c], depth - c, 1))
        window = slice(row * cols, (row + 1) * cols)
        rho = own[0, window, :]
        base = rho * jnp.sqrt(convolved / (total * rho))
        root[window, :] = base
        volume_sum = volume_sum + jnp.minimum(jnp.maximum(base, lower[window, :]), upper[window, :])
    volume[...] = jnp.broadcast_to(volume_row(volume_sum), volume.shape)


def scale_of(target, volumes):
    scale = None
    for volume in volumes:
        whole = jnp.sum(jnp.sum(volume[...], axis=0, keepdims=True), axis=1, keepdims=True)
        ratio = target / whole
        scale = ratio if scale is None else scale * ratio
    return scale


def trial_of(target, volumes, terms):
    root, lower, upper = terms
    return jnp.minimum(jnp.maximum(root[...] * scale_of(target, volumes), lower[...]), upper[...])


def trial_kernel(target, *refs):
    *volumes, root, lower, upper, out = refs
    out[...] = jnp.broadcast_to(volume_row(trial_of(target, volumes, (root, lower, upper))), out.shape)


def update_kernel(target, u, *refs):
    *volumes, root, lower, upper, new_density, displacement, made, sent = refs
    copies = [
        pltpu.make_async_copy(u, displacement, sent.at[0]),
        pltpu.make_async_copy(made, new_density, sent.at[1]),
    ]
    copies[0].start()
    made[...] = trial_of(target, volumes, (root, lower, upper))
    copies[1].start()
    for copy in copies:
        copy.wait()


def call(kernel, name, out_shapes, *args, scratch=(), flops=0, space=pltpu.VMEM, far=()):
    shapes = [jax.ShapeDtypeStruct(shape, jnp.float32) for shape in out_shapes]
    moved = sum(4 * math.prod(value.shape) for value in [*args, *shapes])
    return pl.pallas_call(
        kernel,
        name=name,
        out_shape=shapes,
        in_specs=[pl.BlockSpec(memory_space=space)] * len(args),
        out_specs=[pl.BlockSpec(memory_space=pltpu.HBM if i in far else pltpu.VMEM) for i in range(len(shapes))],
        scratch_shapes=[pltpu.VMEM(item, jnp.float32) if isinstance(item, tuple) else item for item in scratch],
        compiler_params=pltpu.CompilerParams(vmem_limit_bytes=VMEM_LIMIT),
        cost_estimate=pl.CostEstimate(flops=flops, bytes_accessed=moved, transcendentals=0),
    )(*args)


def exchange(low, high, axis):
    count = lax.axis_size(axis)
    from_low = lax.ppermute(high, axis, [(i, (i + 1) % count) for i in range(count)])
    from_high = lax.ppermute(low, axis, [((i + 1) % count, i) for i in range(count)])
    return from_low, from_high


def swap(first, second, axis, wrap):
    count = lax.axis_size(axis)
    assert count % 2 == 0
    ends = [(i, i + 1) for i in range(1, count - 1, 2)] + ([(count - 1, 0)] if wrap else [])
    pairs = [(i, i + 1) for i in range(0, count, 2)]
    both = lambda links: links + [(j, i) for i, j in links]
    return lax.ppermute(first, axis, both(ends)), lax.ppermute(second, axis, both(pairs))


def everyone(shares):
    return lax.all_to_all(shares, AXES, 0, 0, tiled=True)


def shards(density, void_mask, solid_mask, fixed_mask, load_mask, traction):
    shape = rows, cols, depth = density.shape
    devices = lax.axis_size("gx") * lax.axis_size("gy")
    wide, long = cols + 2 * HALO, rows + 2 * HALO_X
    planes = rows + 2 * REACH
    named = lambda kernel: functools.partial(kernel, shape)
    flat = (rows * cols, depth)
    inputs = [
        pltpu.with_memory_space_constraint(value.reshape(*value.shape[:-3], *flat), pltpu.HBM)
        for value in (density, void_mask, solid_mask, fixed_mask, load_mask, traction)
    ]

    own, lower, upper, first, second, low_x, high_x = call(
        named(fields_kernel),
        "fields",
        [
            (FIELDS, *flat),
            flat,
            flat,
            (HALO, FIELDS, rows, depth),
            (HALO, FIELDS, rows, depth),
            (FIELDS, HALO_X * cols, depth),
            (FIELDS, HALO_X * cols, depth),
        ],
        *inputs,
        scratch=[pltpu.VMEM(value.shape, value.dtype) for value in inputs] + [pltpu.SemaphoreType.DMA((8,))],
        space=pltpu.HBM,
    )
    from_first, from_second = swap(first, second, "gy", False)
    low_x, high_x = exchange(low_x, high_x, "gx")
    ext, first, second = call(
        named(widen_kernel),
        "widen",
        [(FIELDS, rows * wide, depth)] + [(FIELDS, HALO_X * 2 * HALO, depth)] * 2,
        own,
        from_first,
        from_second,
    )
    first_xy, second_xy = swap(first, second, "gx", True)
    side = [(12, wide, depth), (12, wide, depth), (3, 2, wide, depth)]
    inner = call(
        named(inner_kernel),
        "inner",
        [
            (BASIS, 3, rows + 1, wide, depth),
            (BASIS, 3, rows + 1, wide, depth),
            (rows, 8 + wide, depth),
            (rows, wide, depth),
            (len(PAIR_LIST) + 1, cols, depth),
        ],
        ext,
        scratch=[(3, 2, rows + 1, wide + 8, depth), *side],
    )
    outer, sums = call(
        named(outer_kernel),
        "outer",
        [(BASIS, 3, long, wide, depth), (devices, 128)],
        ext,
        low_x,
        high_x,
        first_xy,
        second_xy,
        *inner,
        scratch=[
            (FIELDS, 2 * HALO_X, wide, depth),
            (long, 8 + wide, depth),
            (long, wide, depth),
            (BASIS, 3, long, wide, depth),
            (3, 2, long, wide + 8, depth),
            *side,
            *side,
        ],
    )
    u, weighted, first, second = call(
        named(energy_kernel),
        "energy",
        [(3, rows, cols, depth), (planes * cols, depth), (REACH, planes, depth), (REACH, planes, depth)],
        everyone(sums),
        inner[0],
        outer,
        own,
        low_x,
        high_x,
        scratch=[
            (3, rows, wide, depth),
            (3, 2, planes + 1, wide, depth),
        ],
    )
    from_first, from_second = swap(first, second, "gy", True)
    root, volume = call(
        named(filter_kernel),
        "filter",
        [flat, (devices, depth)],
        weighted,
        from_first,
        from_second,
        own,
        lower,
        upper,
        scratch=[(planes * (cols + 8), depth)],
    )
    target = VOLUME_SHARE * rows * cols * depth * devices
    terms, volumes = (root, lower, upper), [everyone(volume)]
    for _ in range(2):
        (volume,) = call(functools.partial(trial_kernel, target), "trial", [(devices, depth)], *volumes, *terms)
        volumes.append(everyone(volume))
    new_density, displacement = call(
        functools.partial(update_kernel, target),
        "update",
        [flat, u.shape],
        u,
        *volumes,
        *terms,
        scratch=[flat, pltpu.SemaphoreType.DMA((2,))],
        far=(0, 1),
    )
    return new_density.reshape(shape), displacement


def solution(mesh):
    placed = (P("gx", "gy", None),) * 5 + (P(None, "gx", "gy", None),)
    return jax.shard_map(
        shards,
        mesh=mesh,
        in_specs=placed,
        out_specs=(P("gx", "gy", None), P(None, "gx", "gy", None)),
        check_vma=False,
    )
```

```python
import functools
import math

import jax
import jax.numpy as jnp
import numpy as np
from jax import lax
from jax.experimental import pallas as pl
from jax.experimental.pallas import tpu as pltpu
from jax.sharding import PartitionSpec as P

E_MIN = 0.001
RHO_FLOOR = 0.001
MOVE_LIMIT = 0.2
VOLUME_SHARE = 0.4
BASIS = 4
REACH = 2
HALO = BASIS
HALO_X = BASIS + REACH
AXES = ("gx", "gy")
FIELDS = 5
VMEM_LIMIT = 40 * 1024 * 1024

POISSON = 0.3
LAME = POISSON / ((1.0 + POISSON) * (1.0 - 2.0 * POISSON))
SHEAR = 1.0 / (2.0 * (1.0 + POISSON))
NORMAL = 2.0 * SHEAR / 16.0
TRACE = LAME / 16.0
SHEAR_FIRST = SHEAR / 16.0
BEND = (LAME + 3.0 * SHEAR) / 48.0
BEND_MIX = LAME / 48.0
TWIST = SHEAR / 48.0
THIRD = (LAME + 4.0 * SHEAR) / 144.0
DIAGONAL = NORMAL + TRACE + 2.0 * SHEAR_FIRST + 2.0 * BEND + 2.0 * TWIST + THIRD
PAIRS = (("xdds", "zsdd"), ("ydds", "zdsd"), ("xdsd", "ysdd"))
TRIPLE = ("zdds", "ydsd", "xsdd")
CLASSES = [c + y + z for c in "xyz" for y in "sd" for z in "sd"]


def by_parity(axis, first, second, body):
    low_first = lax.rem(lax.axis_index(axis), 2) == (0 if axis == "gx" else 1)
    pl.when(low_first)(lambda: body(first, second))
    pl.when(jnp.logical_not(low_first))(lambda: body(second, first))


def lane_index(shape):
    return lax.broadcasted_iota(jnp.int32, shape, len(shape) - 1)


def load_modes(z_ref, plane, begin, count):
    modes = {}
    for number, component in enumerate("xyz"):
        for index, z in enumerate("sd"):
            low = z_ref[number, index, plane, begin : begin + count, :]
            high = z_ref[number, index, plane, begin + 1 : begin + 1 + count, :]
            modes[component + "s" + z] = high + low
            modes[component + "d" + z] = high - low
    return modes


def element_modes(before, after):
    modes = {}
    for key in CLASSES:
        if key[1:] != "ss":
            modes[key[0] + "s" + key[1:]] = after[key] + before[key]
        modes[key[0] + "d" + key[1:]] = after[key] - before[key]
    return modes


def mode_forces(u, moduli):
    forces = {}
    normal = moduli * NORMAL
    trace = (u["xdss"] + u["ysds"] + u["zssd"]) * (TRACE / NORMAL)
    for key in ("xdss", "ysds", "zssd"):
        forces[key] = normal * (u[key] + trace)
    shear = moduli * SHEAR_FIRST
    for one, other in (("ydss", "xsds"), ("zsds", "yssd"), ("xssd", "zdss")):
        forces[one] = forces[other] = shear * (u[one] + u[other])
    bend = moduli * BEND
    for one, other in PAIRS:
        forces[one] = bend * (u[one] + (BEND_MIX / BEND) * u[other])
        forces[other] = bend * (u[other] + (BEND_MIX / BEND) * u[one])
    twist = moduli * TWIST
    total = u[TRIPLE[0]] + u[TRIPLE[1]] + u[TRIPLE[2]]
    for key in TRIPLE:
        forces[key] = twist * (total + u[key])
    third = moduli * THIRD
    for component in "xyz":
        forces[component + "ddd"] = third * u[component + "ddd"]
    return forces


def unit_energy(u):
    trace = u["xdss"] + u["ysds"] + u["zssd"]
    energy = TRACE * (trace * trace)
    energy += NORMAL * (u["xdss"] ** 2 + u["ysds"] ** 2 + u["zssd"] ** 2)
    shears = [u[a] + u[b] for a, b in (("ydss", "xsds"), ("zsds", "yssd"), ("xssd", "zdss"))]
    energy += SHEAR_FIRST * (shears[0] ** 2 + shears[1] ** 2 + shears[2] ** 2)
    squares, mixed = 0.0, 0.0
    for one, other in PAIRS:
        squares += u[one] ** 2 + u[other] ** 2
        mixed += (u[one] + u[other]) ** 2
    energy += (BEND - BEND_MIX) * squares + BEND_MIX * mixed
    total = u[TRIPLE[0]] + u[TRIPLE[1]] + u[TRIPLE[2]]
    squares = total * total
    for key in TRIPLE:
        squares += u[key] ** 2
    energy += TWIST * squares
    energy += THIRD * (u["xddd"] ** 2 + u["yddd"] ** 2 + u["zddd"] ** 2)
    return energy


def fields_kernel(shape, *refs):
    rows, cols, _ = shape
    (density_in, void_in, solid_in, fixed_in, load_in, traction_in) = refs[:6]
    (own, lower, upper, first, second, low_x, high_x) = refs[6:13]
    density, void, solid, fixed, load, traction, arrived = refs[13:]
    pieces = [(fixed_in, fixed), (load_in, load)]
    pieces += [(traction_in.at[component], traction.at[component]) for component in range(3)]
    pieces += [(density_in, density), (void_in, void), (solid_in, solid)]
    copies = [pltpu.make_async_copy(s, t, arrived.at[i]) for i, (s, t) in enumerate(pieces)]
    for copy in copies:
        copy.start()

    def send(field):
        low_x[field] = own[field, : HALO_X * cols, :]
        high_x[field] = own[field, (rows - HALO_X) * cols :, :]

        def outer_rows(low, high):
            for layer in range(HALO):
                low[layer, field] = own[field, pl.ds(layer, rows, stride=cols), :]
                high[layer, field] = own[field, pl.ds(cols - HALO + layer, rows, stride=cols), :]

        by_parity("gy", first, second, outer_rows)

    copies[0].wait()
    copies[1].wait()
    free = (1 - fixed[...]).astype(jnp.float32)
    own[1] = free
    send(1)
    for component in range(3):
        copies[2 + component].wait()
        own[2 + component] = own[1] * load[...].astype(jnp.float32) * traction[component]
        send(2 + component)
    for copy in copies[5:]:
        copy.wait()
    is_solid, is_void = solid[...] == 1, void[...] == 1
    rho = jnp.where(is_solid, 1.0, jnp.where(is_void, RHO_FLOOR, density[...]))
    own[0] = rho
    send(0)
    least = jnp.maximum(RHO_FLOOR, rho - MOVE_LIMIT)
    most = jnp.minimum(1.0, rho + MOVE_LIMIT)
    lower[...] = jnp.where(is_solid, 1.0, jnp.where(is_void, RHO_FLOOR, least))
    upper[...] = jnp.where(is_solid, 1.0, jnp.where(is_void, RHO_FLOOR, most))


def widen_kernel(shape, own, from_first, from_second, ext, first, second):
    rows, cols, _ = shape
    wide = cols + 2 * HALO

    def neighbour_rows(from_low, from_high):
        for field in range(FIELDS):
            for layer in range(HALO):
                ext[field, pl.ds(layer, rows, stride=wide), :] = from_low[layer, field]
                ext[field, pl.ds(cols + HALO + layer, rows, stride=wide), :] = from_high[layer, field]

    by_parity("gy", from_first, from_second, neighbour_rows)
    for field in range(FIELDS):
        for row in range(rows):
            ext[field, pl.ds(row * wide + HALO, cols), :] = own[field, pl.ds(row * cols, cols), :]

    def corners(low, high):
        for target, begin in ((low, 0), (high, rows - HALO_X)):
            for field in range(FIELDS):
                for layer in range(HALO_X):
                    row, source = layer * 2 * HALO, (begin + layer) * wide
                    target[field, row : row + HALO, :] = ext[field, source : source + HALO, :]
                    source += cols + HALO
                    target[field, row + HALO : row + 2 * HALO, :] = ext[field, source : source + HALO, :]

    by_parity("gx", first, second, corners)


def grid_cuts(rows):
    place, last = lax.axis_index("gx"), lax.axis_size("gx") - 1
    return {
        HALO_X - 1: jnp.where(place == 0, 0.0, 1.0),
        HALO_X + rows - 1: jnp.where(place == last, 0.0, 1.0),
    }


def cut_off(values, keep):
    return values if keep is None else {key: value * keep for key, value in values.items()}


class Stages:
    def __init__(self, shape, fields, inverses, p, w, set_p, set_w, z_ref, mode_ref, lift_ref, pipe_ref):
        self.wide, self.depth = shape[1] + 2 * HALO, shape[2]
        lanes = lane_index((self.wide, self.depth))
        self.keep_last = jnp.where(lanes < self.depth - 1, 1.0, 0.0)
        self.keep_first = jnp.where(lanes > 0, 1.0, 0.0)
        self.fields, self.inverses, self.p, self.w = fields, inverses, p, w
        self.set_p, self.set_w = set_p, set_w
        self.z_ref, self.mode_ref, self.lift_ref, self.pipe_ref = z_ref, mode_ref, lift_ref, pipe_ref

    def lift_moduli(self, around):
        return around + pltpu.roll(around, 1, 1) * self.keep_first

    def produce(self, level, plane, slot):
        for component in range(3):
            value = self.p(level, component, plane)
            lifted = pltpu.roll(value, self.depth - 1, 1) * self.keep_last
            self.z_ref[component, 0, slot, : self.wide] = lifted + value
            self.z_ref[component, 1, slot, : self.wide] = lifted - value

    def begin(self, slot):
        modes = load_modes(self.z_ref, slot, 0, self.wide)
        for index, key in enumerate(CLASSES):
            self.mode_ref[index] = modes[key]
            self.lift_ref[index] = jnp.zeros((self.wide, self.depth), jnp.float32)

    def spread(self, plane, slot, keep=None):
        after = load_modes(self.z_ref, slot, 0, self.wide)
        before = {key: self.mode_ref[index] for index, key in enumerate(CLASSES)}
        lift = {key: self.lift_ref[index] for index, key in enumerate(CLASSES)}
        forces = mode_forces(element_modes(before, cut_off(after, keep)), self.fields(plane))
        for number, component in enumerate("xyz"):
            along_z = {}
            for z in "sd":
                along_y = {}
                for y in "sd":
                    key = component + y + z
                    slope = forces[component + "d" + y + z]
                    if y + z == "ss":
                        along_y[y] = lift[key] - slope
                        lift[key] = slope
                    else:
                        mean = forces[component + "s" + y + z]
                        along_y[y] = lift[key] + (mean - slope)
                        lift[key] = mean + slope
                along_z[z] = (along_y["s"] - along_y["d"]) + pltpu.roll(along_y["s"] + along_y["d"], 1, 0)
            self.pipe_ref[number, 0] = along_z["s"] + along_z["d"]
            self.pipe_ref[number, 1] = along_z["s"] - along_z["d"]
        lift = cut_off(lift, keep)
        for index, key in enumerate(CLASSES):
            self.mode_ref[index] = after[key]
            self.lift_ref[index] = lift[key]

    def finish(self, level, plane):
        for component in range(3):
            shifted = pltpu.roll(self.pipe_ref[component, 0], 1, 1) * self.keep_first
            residual = (self.pipe_ref[component, 1] + shifted) - self.w(level, component, plane)
            self.set_w(level + 1, component, plane, residual)
            self.set_p(level + 1, component, plane, residual * self.inverses(plane))


def sweep(level, sides, cuts, shift):
    for side, start, count, wanted in sides:
        side.begin(start - shift)
    for step in range(max(count for _, _, count, _ in sides) + 2):
        for side, start, count, wanted in sides:
            plane, end = start + step, start + count
            if wanted <= plane - 2 < end:
                side.produce(level + 1, plane - 2, plane - 2 - shift)
            if wanted <= plane - 1 < end:
                side.finish(level, plane - 1)
            if plane < end:
                side.spread(plane, plane + 1 - shift, cuts.get(plane))


def moduli_of(rho):
    return jnp.where(rho > 0.0, E_MIN + rho * rho * rho * (1.0 - E_MIN), 0.0)


def inverse_of(free, around):
    return free / (free * (DIAGONAL * around) + (1.0 - free))


PAIR_LIST = [(i, j) for i in range(BASIS) for j in range(i + 1)]


def inner_kernel(shape, ext, p_ref, w_ref, field_ref, inverse_ref, totals_ref, z_ref, mode_ref, lift_ref, pipe_ref):
    rows, cols, depth = shape
    wide, shift = cols + 2 * HALO, HALO_X - 1
    field_ref[:, :8, :] = jnp.zeros((rows, 8, depth), jnp.float32)
    z_ref[:, :, :, wide:, :] = jnp.zeros((3, 2, z_ref.shape[2], 8, depth), jnp.float32)
    for row in range(rows):
        window = slice(row * wide, (row + 1) * wide)
        field_ref[row, 8:, :] = moduli_of(ext[0, window, :])
        for component in range(3):
            w_ref[0, component, row + 1] = ext[2 + component, window, :]

    def store(ref):
        def put(level, component, plane, value):
            ref[level, component, plane - shift] = value

        return put

    stages = Stages(
        shape,
        lambda plane: field_ref[plane - HALO_X, 8:, :],
        lambda plane: inverse_ref[plane - HALO_X],
        lambda level, component, plane: p_ref[level, component, plane - shift],
        lambda level, component, plane: w_ref[level, component, plane - shift],
        store(p_ref),
        store(w_ref),
        z_ref,
        mode_ref,
        lift_ref,
        pipe_ref,
    )
    inverse_ref[0] = jnp.zeros((wide, depth), jnp.float32)
    for row in range(1, rows):
        around = field_ref[row - 1, 8:, :] + field_ref[row - 1, 7 : 7 + wide, :]
        around = around + (field_ref[row, 8:, :] + field_ref[row, 7 : 7 + wide, :])
        inverse = inverse_of(ext[1, row * wide : (row + 1) * wide, :], stages.lift_moduli(around))
        inverse_ref[row] = inverse
        for component in range(3):
            p_ref[0, component, row + 1] = w_ref[0, component, row + 1] * inverse
    for row in range(1, rows):
        stages.produce(0, row + HALO_X, row + 1)

    for level in range(BASIS - 1):
        start, count = HALO_X + 1 + level, rows - 2 - 2 * level
        sweep(level, [(stages, start, count, start + 1)], {}, shift)

    first, last = HALO_X + BASIS, HALO_X + rows - 1 - (BASIS - 1)
    totals = [jnp.zeros((cols, depth), jnp.float32)] * (len(PAIR_LIST) + 1)
    before = load_modes(z_ref, first - shift, HALO, cols)
    for plane in range(first, last + 1):
        totals = add_dots(
            totals,
            lambda level, component: p_ref[level, component, plane - shift, HALO : HALO + cols, :],
            lambda level, component: w_ref[level, component, plane - shift, HALO : HALO + cols, :],
        )
        if plane < last:
            after = load_modes(z_ref, plane + 1 - shift, HALO, cols)
            energy = unit_energy(element_modes(before, after))
            totals[-1] = totals[-1] + field_ref[plane - HALO_X, 8 + HALO : 8 + HALO + cols, :] * energy
            before = after
    for index, total in enumerate(totals):
        totals_ref[index] = total


def add_dots(totals, p, w):
    totals = list(totals)
    for component in range(3):
        ps = [p(level, component) for level in range(BASIS)]
        ws = [w(level, component) for level in range(BASIS)]
        for index, (i, j) in enumerate(PAIR_LIST):
            totals[index] = totals[index] + ps[i] * ws[j]
    return totals


def outer_kernel(
    shape, ext, low_x, high_x, first, second, p_in, w_in, field_in, inverse_in, totals_in, p_ref, sums_out, *scratch
):
    rows, cols, depth = shape
    wide, long, shift = cols + 2 * HALO, rows + 2 * HALO_X, HALO_X - 1
    halo_ref, field_ref, inverse_ref, w_ref, z_ref, *both = scratch
    cuts = grid_cuts(rows)
    own = range(HALO_X, HALO_X + rows)
    z_ref[:, :, :, wide:, :] = jnp.zeros((3, 2, long, 8, depth), jnp.float32)
    field_ref[:, :8, :] = jnp.zeros((long, 8, depth), jnp.float32)

    def rims(low, high):
        for rim, begin in ((low, 0), (high, HALO_X)):
            for field in range(FIELDS):
                for layer in range(HALO_X):
                    row = layer * 2 * HALO
                    halo_ref[field, begin + layer, :HALO, :] = rim[field, row : row + HALO, :]
                    halo_ref[field, begin + layer, HALO + cols :, :] = rim[field, row + HALO : row + 2 * HALO, :]

    by_parity("gx", first, second, rims)
    for middle, begin in ((low_x, 0), (high_x, HALO_X)):
        for field in range(FIELDS):
            for layer in range(HALO_X):
                window = slice(layer * cols, (layer + 1) * cols)
                halo_ref[field, begin + layer, HALO : HALO + cols, :] = middle[field, window, :]

    def given(field, plane, begin=0, count=wide):
        if plane in own:
            row = (plane - HALO_X) * wide + begin
            return ext[field, row : row + count, :]
        return halo_ref[field, plane if plane < HALO_X else plane - rows, begin : begin + count, :]

    def fields(plane, begin=0, count=wide):
        if plane in own:
            return field_in[plane - HALO_X, 8 + begin : 8 + begin + count, :]
        return field_ref[plane, 8 + begin : 8 + begin + count, :]

    def inverses(plane):
        return inverse_in[plane - HALO_X] if HALO_X < plane < HALO_X + rows else inverse_ref[plane]

    def is_inner(level, plane):
        return HALO_X + 1 + level <= plane <= HALO_X + rows - 1 - level

    def p(level, component, plane, begin=0, count=wide):
        if is_inner(level, plane):
            return p_in[level, component, plane - shift, begin : begin + count, :]
        return p_ref[level, component, plane, begin : begin + count, :]

    def w(level, component, plane, begin=0, count=wide):
        if is_inner(level, plane):
            return w_in[level, component, plane - shift, begin : begin + count, :]
        if level == 0:
            return given(2 + component, plane, begin, count)
        return w_ref[level, component, plane, begin : begin + count, :]

    def set_p(level, component, plane, value):
        p_ref[level, component, plane] = value

    def set_w(level, component, plane, value):
        w_ref[level, component, plane] = value

    sides = [
        Stages(shape, fields, inverses, p, w, set_p, set_w, z_ref, both[0], both[1], both[2]),
        Stages(shape, fields, inverses, p, w, set_p, set_w, z_ref, both[3], both[4], both[5]),
    ]
    for plane in range(long):
        if plane not in own:
            field_ref[plane, 8:, :] = moduli_of(given(0, plane))
    edge_planes = [*range(1, HALO_X + 1), *range(HALO_X + rows, long)]
    for plane in edge_planes:
        around = fields(plane - 1) + fields(plane - 1, -1)
        if plane - 1 in cuts:
            around = around * cuts[plane - 1]
        around = around + (fields(plane) + fields(plane, -1))
        inverse = inverse_of(given(1, plane), sides[0].lift_moduli(around))
        inverse_ref[plane] = inverse
        for component in range(3):
            set_p(0, component, plane, given(2 + component, plane) * inverse)
    for plane in edge_planes:
        sides[0].produce(0, plane, plane)

    count = HALO_X + 1
    for level in range(BASIS - 1):
        for plane in (HALO_X + 1 + level, HALO_X + 2 + level, HALO_X + rows - 2 - level, HALO_X + rows - 1 - level):
            sides[0].produce(level, plane, plane)
        left, right = 1 + level, HALO_X + rows - 2 - level
        sweep(level, [(sides[0], left, count, left + 1), (sides[1], right, count, right + 1)], cuts, 0)

    last = BASIS - 1
    for plane in (HALO_X + 1 + last, HALO_X + rows - 1 - last):
        sides[0].produce(last, plane, plane)
    totals = [totals_in[index] for index in range(len(PAIR_LIST) + 1)]
    for plane in own:
        if not is_inner(last, plane):
            totals = add_dots(
                totals,
                lambda level, component: p(level, component, plane, HALO, cols),
                lambda level, component: w(level, component, plane, HALO, cols),
            )
        if not (is_inner(last, plane) and is_inner(last, plane + 1)):
            before = load_modes(z_ref, plane, HALO, cols)
            after = cut_off(load_modes(z_ref, plane + 1, HALO, cols), cuts.get(plane))
            energy = unit_energy(element_modes(before, after))
            totals[-1] = totals[-1] + fields(plane, HALO, cols) * energy
    slots = lane_index((1, 128))
    line = jnp.zeros((1, 128), jnp.float32)
    for index, total in enumerate(totals):
        share = jnp.sum(jnp.sum(total, axis=0, keepdims=True), axis=1, keepdims=True)
        line = line + jnp.where(slots == index, share, 0.0)
    sums_out[...] = jnp.broadcast_to(line, sums_out.shape)


def coefficients(shares):
    line = jnp.sum(shares, axis=0, keepdims=True)
    slots = lane_index(line.shape)

    def entry(index):
        return jnp.sum(jnp.where(slots == index, line, 0.0), axis=1, keepdims=True)

    inner = {}
    for index, (i, j) in enumerate(PAIR_LIST):
        inner[i, j] = inner[j, i] = entry(index)
    energy = {(BASIS - 1, BASIS - 1): entry(len(PAIR_LIST))}
    for i in range(BASIS):
        for j in range(min(i + 1, BASIS - 1)):
            energy[i, j] = inner[i, j + 1] + inner[i, j]
    lower, pivot, inverse, solved = {}, {}, {}, {}
    for k in range(BASIS):
        left = energy[k, k]
        for m in range(k):
            left = left - lower[k, m] * lower[k, m] * pivot[m]
        sound = left > 1e-6 * energy[k, k]
        pivot[k] = jnp.where(sound, left, 0.0)
        inverse[k] = jnp.where(sound, 1.0 / jnp.where(sound, left, 1.0), 0.0)
        for i in range(k + 1, BASIS):
            part = energy[i, k]
            for m in range(k):
                part = part - lower[i, m] * lower[k, m] * pivot[m]
            lower[i, k] = part * inverse[k]
    for k in range(BASIS):
        part = inner[k, 0]
        for m in range(k):
            part = part - lower[k, m] * solved[m]
        solved[k] = part
    result = {}
    for k in reversed(range(BASIS)):
        part = solved[k] * inverse[k]
        for m in range(k + 1, BASIS):
            part = part - lower[m, k] * result[m]
        result[k] = part
    return [result[k] for k in range(BASIS)]


def energy_kernel(
    shape, shares, inner, outer, own, low_x, high_x, u_out, weighted, first, second, u_ref, z_ref
):
    rows, cols, depth = shape
    wide, planes = cols + 2 * HALO, rows + 2 * REACH
    keep_last = jnp.where(lane_index((wide, depth)) < depth - 1, 1.0, 0.0)
    parts = [jnp.broadcast_to(part, (wide, depth)) for part in coefficients(shares[...])]
    cuts = grid_cuts(rows)
    for plane in range(planes + 1):
        source = plane + HALO_X - REACH
        for component in range(3):
            total = None
            for level in range(BASIS):
                if HALO_X + 1 + level <= source <= HALO_X + rows - 1 - level:
                    term = parts[level] * inner[level, component, source - HALO_X + 1]
                else:
                    term = parts[level] * outer[level, component, source]
                total = term if total is None else total + term
            lifted = pltpu.roll(total, depth - 1, 1) * keep_last
            z_ref[component, 0, plane] = lifted + total
            z_ref[component, 1, plane] = lifted - total
            row = plane - REACH
            if 0 <= row < rows:
                u_ref[component, row] = total
                u_out[component, row] = u_ref[component, row, HALO : HALO + cols, :]
    before = load_modes(z_ref, 0, HALO, cols)
    for plane in range(planes):
        row = plane - REACH
        after = load_modes(z_ref, plane + 1, HALO, cols)
        energy = unit_energy(element_modes(before, cut_off(after, cuts.get(row + HALO_X))))
        before = after
        if row < 0:
            rho = low_x[0, (row + HALO_X) * cols : (row + HALO_X + 1) * cols, :]
        elif row < rows:
            rho = own[0, row * cols : (row + 1) * cols, :]
        else:
            rho = high_x[0, (row - rows) * cols : (row - rows + 1) * cols, :]
        weighted[plane * cols : (plane + 1) * cols, :] = rho * (3.0 * rho * rho * (1.0 - E_MIN) * energy)

    def outer_rows(low, high):
        for layer in range(REACH):
            low[layer] = weighted[pl.ds(layer, planes, stride=cols), :]
            high[layer] = weighted[pl.ds(cols - REACH + layer, planes, stride=cols), :]

    by_parity("gy", first, second, outer_rows)


def cone_table():
    table, total = {}, 0.0
    for a in range(-2, 3):
        for b in range(-2, 3):
            for c in range(-2, 3):
                total += max(0.0, 3.0 - math.sqrt(a * a + b * b + c * c))
    for flat in (0, 1, 2, 4, 5, 8):
        for c in range(3):
            table[flat, c] = max(0.0, 3.0 - math.sqrt(flat + c * c))
    return table, total


def volume_row(total):
    return jnp.sum(total, axis=0, keepdims=True)


def filter_kernel(shape, weighted, from_first, from_second, own, lower, upper, root, volume, plane_ref):
    rows, cols, depth = shape
    wide, planes = cols + 8, rows + 2 * REACH
    table, total = cone_table()
    for plane in range(planes):
        plane_ref[plane * wide + REACH : plane * wide + REACH + cols, :] = weighted[plane * cols : (plane + 1) * cols, :]

    def neighbour_rows(from_low, from_high):
        for layer in range(REACH):
            plane_ref[pl.ds(layer, planes, stride=wide), :] = from_low[layer]
            plane_ref[pl.ds(REACH + cols + layer, planes, stride=wide), :] = from_high[layer]

    by_parity("gy", from_first, from_second, neighbour_rows)
    volume_sum = jnp.zeros((cols, depth), jnp.float32)
    for row in range(rows):
        spread = {}
        for a in range(-REACH, REACH + 1):
            for b in range(-REACH, REACH + 1):
                key = a * a + b * b
                value = plane_ref[pl.ds((row + REACH + a) * wide + REACH + b, cols), :]
                spread[key] = value if key not in spread else spread[key] + value
        sums = []
        for c in range(3):
            part = None
            for key, value in spread.items():
                if table[key, c] > 0.0:
                    term = table[key, c] * value
                    part = term if part is None else part + term
            sums.append(part)
        convolved = sums[0]
        for c in (1, 2):
            convolved = convolved + (pltpu.roll(sums[c], c, 1) + pltpu.roll(sums[c], depth - c, 1))
        window = slice(row * cols, (row + 1) * cols)
        rho = own[0, window, :]
        base = rho * jnp.sqrt(convolved / (total * rho))
        root[window, :] = base
        volume_sum = volume_sum + jnp.minimum(jnp.maximum(base, lower[window, :]), upper[window, :])
    volume[...] = jnp.broadcast_to(volume_row(volume_sum), volume.shape)


def scale_of(target, volumes):
    scale = None
    for volume in volumes:
        whole = jnp.sum(jnp.sum(volume[...], axis=0, keepdims=True), axis=1, keepdims=True)
        ratio = target / whole
        scale = ratio if scale is None else scale * ratio
    return scale


def trial_of(target, volumes, terms):
    root, lower, upper = terms
    return jnp.minimum(jnp.maximum(root[...] * scale_of(target, volumes), lower[...]), upper[...])


def trial_kernel(target, *refs):
    *volumes, root, lower, upper, out = refs
    out[...] = jnp.broadcast_to(volume_row(trial_of(target, volumes, (root, lower, upper))), out.shape)


def update_kernel(target, u, *refs):
    *volumes, root, lower, upper, new_density, displacement, made, sent = refs
    copies = [
        pltpu.make_async_copy(u, displacement, sent.at[0]),
        pltpu.make_async_copy(made, new_density, sent.at[1]),
    ]
    copies[0].start()
    made[...] = trial_of(target, volumes, (root, lower, upper))
    copies[1].start()
    for copy in copies:
        copy.wait()


def call(kernel, name, out_shapes, *args, scratch=(), flops=0, space=pltpu.VMEM, far=()):
    shapes = [jax.ShapeDtypeStruct(shape, jnp.float32) for shape in out_shapes]
    moved = sum(4 * math.prod(value.shape) for value in [*args, *shapes])
    return pl.pallas_call(
        kernel,
        name=name,
        out_shape=shapes,
        in_specs=[pl.BlockSpec(memory_space=space)] * len(args),
        out_specs=[pl.BlockSpec(memory_space=pltpu.HBM if i in far else pltpu.VMEM) for i in range(len(shapes))],
        scratch_shapes=[pltpu.VMEM(item, jnp.float32) if isinstance(item, tuple) else item for item in scratch],
        compiler_params=pltpu.CompilerParams(vmem_limit_bytes=VMEM_LIMIT),
        cost_estimate=pl.CostEstimate(flops=flops, bytes_accessed=moved, transcendentals=0),
    )(*args)


def exchange(low, high, axis):
    count = lax.axis_size(axis)
    from_low = lax.ppermute(high, axis, [(i, (i + 1) % count) for i in range(count)])
    from_high = lax.ppermute(low, axis, [((i + 1) % count, i) for i in range(count)])
    return from_low, from_high


def swap(first, second, axis, wrap):
    count = lax.axis_size(axis)
    assert count % 2 == 0
    ends = [(i, i + 1) for i in range(1, count - 1, 2)] + ([(count - 1, 0)] if wrap else [])
    pairs = [(i, i + 1) for i in range(0, count, 2)]
    both = lambda links: links + [(j, i) for i, j in links]
    order = (ends, pairs) if axis == "gx" else (pairs, ends)
    return tuple(lax.ppermute(value, axis, both(links)) for value, links in zip((first, second), order))


def everyone(shares):
    return lax.all_to_all(shares, AXES, 0, 0, tiled=True)


def shards(density, void_mask, solid_mask, fixed_mask, load_mask, traction):
    shape = rows, cols, depth = density.shape
    devices = lax.axis_size("gx") * lax.axis_size("gy")
    wide, long = cols + 2 * HALO, rows + 2 * HALO_X
    planes = rows + 2 * REACH
    named = lambda kernel: functools.partial(kernel, shape)
    flat = (rows * cols, depth)
    inputs = [
        pltpu.with_memory_space_constraint(value.reshape(*value.shape[:-3], *flat), pltpu.HBM)
        for value in (density, void_mask, solid_mask, fixed_mask, load_mask, traction)
    ]

    own, lower, upper, first, second, low_x, high_x = call(
        named(fields_kernel),
        "fields",
        [
            (FIELDS, *flat),
            flat,
            flat,
            (HALO, FIELDS, rows, depth),
            (HALO, FIELDS, rows, depth),
            (FIELDS, HALO_X * cols, depth),
            (FIELDS, HALO_X * cols, depth),
        ],
        *inputs,
        scratch=[pltpu.VMEM(value.shape, value.dtype) for value in inputs] + [pltpu.SemaphoreType.DMA((8,))],
        space=pltpu.HBM,
    )
    from_first, from_second = swap(first, second, "gy", False)
    low_x, high_x = exchange(low_x, high_x, "gx")
    ext, first, second = call(
        named(widen_kernel),
        "widen",
        [(FIELDS, rows * wide, depth)] + [(FIELDS, HALO_X * 2 * HALO, depth)] * 2,
        own,
        from_first,
        from_second,
    )
    first_xy, second_xy = swap(first, second, "gx", True)
    side = [(12, wide, depth), (12, wide, depth), (3, 2, wide, depth)]
    inner = call(
        named(inner_kernel),
        "inner",
        [
            (BASIS, 3, rows + 1, wide, depth),
            (BASIS, 3, rows + 1, wide, depth),
            (rows, 8 + wide, depth),
            (rows, wide, depth),
            (len(PAIR_LIST) + 1, cols, depth),
        ],
        ext,
        scratch=[(3, 2, rows + 1, wide + 8, depth), *side],
    )
    outer, sums = call(
        named(outer_kernel),
        "outer",
        [(BASIS, 3, long, wide, depth), (devices, 128)],
        ext,
        low_x,
        high_x,
        first_xy,
        second_xy,
        *inner,
        scratch=[
            (FIELDS, 2 * HALO_X, wide, depth),
            (long, 8 + wide, depth),
            (long, wide, depth),
            (BASIS, 3, long, wide, depth),
            (3, 2, long, wide + 8, depth),
            *side,
            *side,
        ],
    )
    u, weighted, first, second = call(
        named(energy_kernel),
        "energy",
        [(3, rows, cols, depth), (planes * cols, depth), (REACH, planes, depth), (REACH, planes, depth)],
        everyone(sums),
        inner[0],
        outer,
        own,
        low_x,
        high_x,
        scratch=[
            (3, rows, wide, depth),
            (3, 2, planes + 1, wide, depth),
        ],
    )
    from_first, from_second = swap(first, second, "gy", True)
    root, volume = call(
        named(filter_kernel),
        "filter",
        [flat, (devices, depth)],
        weighted,
        from_first,
        from_second,
        own,
        lower,
        upper,
        scratch=[(planes * (cols + 8), depth)],
    )
    target = VOLUME_SHARE * rows * cols * depth * devices
    terms, volumes = (root, lower, upper), [everyone(volume)]
    for _ in range(2):
        (volume,) = call(functools.partial(trial_kernel, target), "trial", [(devices, depth)], *volumes, *terms)
        volumes.append(everyone(volume))
    new_density, displacement = call(
        functools.partial(update_kernel, target),
        "update",
        [flat, u.shape],
        u,
        *volumes,
        *terms,
        scratch=[flat, pltpu.SemaphoreType.DMA((2,))],
        far=(0, 1),
    )
    return new_density.reshape(shape), displacement


def solution(mesh):
    placed = (P("gx", "gy", None),) * 5 + (P(None, "gx", "gy", None),)
    return jax.shard_map(
        shards,
        mesh=mesh,
        in_specs=placed,
        out_specs=(P("gx", "gy", None), P(None, "gx", "gy", None)),
        check_vma=False,
    )
```

```python
import functools
import math

import jax
import jax.numpy as jnp
import numpy as np
from jax import lax
from jax.experimental import pallas as pl
from jax.experimental.pallas import tpu as pltpu
from jax.sharding import PartitionSpec as P

E_MIN = 0.001
RHO_FLOOR = 0.001
MOVE_LIMIT = 0.2
VOLUME_SHARE = 0.4
BASIS = 4
REACH = 2
HALO = BASIS
HALO_X = BASIS + REACH
AXES = ("gx", "gy")
FIELDS = 5
VMEM_LIMIT = 40 * 1024 * 1024

POISSON = 0.3
LAME = POISSON / ((1.0 + POISSON) * (1.0 - 2.0 * POISSON))
SHEAR = 1.0 / (2.0 * (1.0 + POISSON))
NORMAL = 2.0 * SHEAR / 16.0
TRACE = LAME / 16.0
SHEAR_FIRST = SHEAR / 16.0
BEND = (LAME + 3.0 * SHEAR) / 48.0
BEND_MIX = LAME / 48.0
TWIST = SHEAR / 48.0
THIRD = (LAME + 4.0 * SHEAR) / 144.0
DIAGONAL = NORMAL + TRACE + 2.0 * SHEAR_FIRST + 2.0 * BEND + 2.0 * TWIST + THIRD
PAIRS = (("xdds", "zsdd"), ("ydds", "zdsd"), ("xdsd", "ysdd"))
TRIPLE = ("zdds", "ydsd", "xsdd")
CLASSES = [c + y + z for c in "xyz" for y in "sd" for z in "sd"]


def by_parity(axis, first, second, body):
    low_first = lax.rem(lax.axis_index(axis), 2) == (0 if axis == "gx" else 1)
    pl.when(low_first)(lambda: body(first, second))
    pl.when(jnp.logical_not(low_first))(lambda: body(second, first))


def lane_index(shape):
    return lax.broadcasted_iota(jnp.int32, shape, len(shape) - 1)


def load_modes(z_ref, plane, begin, count):
    modes = {}
    for number, component in enumerate("xyz"):
        for index, z in enumerate("sd"):
            low = z_ref[number, index, plane, begin : begin + count, :]
            high = z_ref[number, index, plane, begin + 1 : begin + 1 + count, :]
            modes[component + "s" + z] = high + low
            modes[component + "d" + z] = high - low
    return modes


def element_modes(before, after):
    modes = {}
    for key in CLASSES:
        if key[1:] != "ss":
            modes[key[0] + "s" + key[1:]] = after[key] + before[key]
        modes[key[0] + "d" + key[1:]] = after[key] - before[key]
    return modes


def mode_forces(u, moduli):
    forces = {}
    normal = moduli * NORMAL
    trace = (u["xdss"] + u["ysds"] + u["zssd"]) * (TRACE / NORMAL)
    for key in ("xdss", "ysds", "zssd"):
        forces[key] = normal * (u[key] + trace)
    shear = moduli * SHEAR_FIRST
    for one, other in (("ydss", "xsds"), ("zsds", "yssd"), ("xssd", "zdss")):
        forces[one] = forces[other] = shear * (u[one] + u[other])
    bend = moduli * BEND
    for one, other in PAIRS:
        forces[one] = bend * (u[one] + (BEND_MIX / BEND) * u[other])
        forces[other] = bend * (u[other] + (BEND_MIX / BEND) * u[one])
    twist = moduli * TWIST
    total = u[TRIPLE[0]] + u[TRIPLE[1]] + u[TRIPLE[2]]
    for key in TRIPLE:
        forces[key] = twist * (total + u[key])
    third = moduli * THIRD
    for component in "xyz":
        forces[component + "ddd"] = third * u[component + "ddd"]
    return forces


def unit_energy(u):
    trace = u["xdss"] + u["ysds"] + u["zssd"]
    energy = TRACE * (trace * trace)
    energy += NORMAL * (u["xdss"] ** 2 + u["ysds"] ** 2 + u["zssd"] ** 2)
    shears = [u[a] + u[b] for a, b in (("ydss", "xsds"), ("zsds", "yssd"), ("xssd", "zdss"))]
    energy += SHEAR_FIRST * (shears[0] ** 2 + shears[1] ** 2 + shears[2] ** 2)
    squares, mixed = 0.0, 0.0
    for one, other in PAIRS:
        squares += u[one] ** 2 + u[other] ** 2
        mixed += (u[one] + u[other]) ** 2
    energy += (BEND - BEND_MIX) * squares + BEND_MIX * mixed
    total = u[TRIPLE[0]] + u[TRIPLE[1]] + u[TRIPLE[2]]
    squares = total * total
    for key in TRIPLE:
        squares += u[key] ** 2
    energy += TWIST * squares
    energy += THIRD * (u["xddd"] ** 2 + u["yddd"] ** 2 + u["zddd"] ** 2)
    return energy


def low_x_run(field):
    return (0, 0) if field == 0 else (HALO_X + (HALO_X - 1) * (field - 1), 1)


def fields_kernel(shape, *refs):
    rows, cols, _ = shape
    (density_in, void_in, solid_in, fixed_in, load_in, traction_in) = refs[:6]
    (own, lower, upper, first, second, low_x, high_x) = refs[6:13]
    density, void, solid, fixed, load, traction, arrived = refs[13:]
    pieces = [(fixed_in, fixed), (load_in, load)]
    pieces += [(traction_in.at[component], traction.at[component]) for component in range(3)]
    pieces += [(density_in, density), (void_in, void), (solid_in, solid)]
    copies = [pltpu.make_async_copy(s, t, arrived.at[i]) for i, (s, t) in enumerate(pieces)]
    for copy in copies:
        copy.start()

    def send(field):
        low_x[field] = own[field, : HALO_X * cols, :]
        begin, skip = low_x_run(field)
        count = (HALO_X - skip) * cols
        high_x[begin * cols : begin * cols + count, :] = own[field, rows * cols - count :, :]

        def outer_rows(low, high):
            for layer in range(HALO):
                low[layer, field] = own[field, pl.ds(layer, rows, stride=cols), :]
                high[layer, field] = own[field, pl.ds(cols - HALO + layer, rows, stride=cols), :]

        by_parity("gy", first, second, outer_rows)

    copies[0].wait()
    copies[1].wait()
    free = (1 - fixed[...]).astype(jnp.float32)
    own[1] = free
    send(1)
    for component in range(3):
        copies[2 + component].wait()
        own[2 + component] = own[1] * load[...].astype(jnp.float32) * traction[component]
        send(2 + component)
    for copy in copies[5:]:
        copy.wait()
    is_solid, is_void = solid[...] == 1, void[...] == 1
    rho = jnp.where(is_solid, 1.0, jnp.where(is_void, RHO_FLOOR, density[...]))
    own[0] = rho
    send(0)
    least = jnp.maximum(RHO_FLOOR, rho - MOVE_LIMIT)
    most = jnp.minimum(1.0, rho + MOVE_LIMIT)
    lower[...] = jnp.where(is_solid, 1.0, jnp.where(is_void, RHO_FLOOR, least))
    upper[...] = jnp.where(is_solid, 1.0, jnp.where(is_void, RHO_FLOOR, most))


def widen_kernel(shape, own, from_first, from_second, ext, first, second):
    rows, cols, _ = shape
    wide = cols + 2 * HALO

    def neighbour_rows(from_low, from_high):
        for field in range(FIELDS):
            for layer in range(HALO):
                ext[field, pl.ds(layer, rows, stride=wide), :] = from_low[layer, field]
                ext[field, pl.ds(cols + HALO + layer, rows, stride=wide), :] = from_high[layer, field]

    by_parity("gy", from_first, from_second, neighbour_rows)
    for field in range(FIELDS):
        for row in range(rows):
            ext[field, pl.ds(row * wide + HALO, cols), :] = own[field, pl.ds(row * cols, cols), :]

    def corners(low, high):
        for target, begin in ((low, 0), (high, rows - HALO_X)):
            for field in range(FIELDS):
                for layer in range(HALO_X):
                    row, source = layer * 2 * HALO, (begin + layer) * wide
                    target[field, row : row + HALO, :] = ext[field, source : source + HALO, :]
                    source += cols + HALO
                    target[field, row + HALO : row + 2 * HALO, :] = ext[field, source : source + HALO, :]

    by_parity("gx", first, second, corners)


def grid_cuts(rows):
    place, last = lax.axis_index("gx"), lax.axis_size("gx") - 1
    return {
        HALO_X - 1: jnp.where(place == 0, 0.0, 1.0),
        HALO_X + rows - 1: jnp.where(place == last, 0.0, 1.0),
    }


def cut_off(values, keep):
    return values if keep is None else {key: value * keep for key, value in values.items()}


class Stages:
    def __init__(self, shape, fields, inverses, p, w, set_p, set_w, z_ref, mode_ref, lift_ref, pipe_ref):
        self.wide, self.depth = shape[1] + 2 * HALO, shape[2]
        lanes = lane_index((self.wide, self.depth))
        self.keep_last = jnp.where(lanes < self.depth - 1, 1.0, 0.0)
        self.keep_first = jnp.where(lanes > 0, 1.0, 0.0)
        self.fields, self.inverses, self.p, self.w = fields, inverses, p, w
        self.set_p, self.set_w = set_p, set_w
        self.z_ref, self.mode_ref, self.lift_ref, self.pipe_ref = z_ref, mode_ref, lift_ref, pipe_ref

    def lift_moduli(self, around):
        return around + pltpu.roll(around, 1, 1) * self.keep_first

    def produce(self, level, plane, slot):
        for component in range(3):
            value = self.p(level, component, plane)
            lifted = pltpu.roll(value, self.depth - 1, 1) * self.keep_last
            self.z_ref[component, 0, slot, : self.wide] = lifted + value
            self.z_ref[component, 1, slot, : self.wide] = lifted - value

    def begin(self, slot):
        modes = load_modes(self.z_ref, slot, 0, self.wide)
        for index, key in enumerate(CLASSES):
            self.mode_ref[index] = modes[key]
            self.lift_ref[index] = jnp.zeros((self.wide, self.depth), jnp.float32)

    def spread(self, plane, slot, keep=None):
        after = load_modes(self.z_ref, slot, 0, self.wide)
        before = {key: self.mode_ref[index] for index, key in enumerate(CLASSES)}
        lift = {key: self.lift_ref[index] for index, key in enumerate(CLASSES)}
        forces = mode_forces(element_modes(before, cut_off(after, keep)), self.fields(plane))
        for number, component in enumerate("xyz"):
            along_z = {}
            for z in "sd":
                along_y = {}
                for y in "sd":
                    key = component + y + z
                    slope = forces[component + "d" + y + z]
                    if y + z == "ss":
                        along_y[y] = lift[key] - slope
                        lift[key] = slope
                    else:
                        mean = forces[component + "s" + y + z]
                        along_y[y] = lift[key] + (mean - slope)
                        lift[key] = mean + slope
                along_z[z] = (along_y["s"] - along_y["d"]) + pltpu.roll(along_y["s"] + along_y["d"], 1, 0)
            self.pipe_ref[number, 0] = along_z["s"] + along_z["d"]
            self.pipe_ref[number, 1] = along_z["s"] - along_z["d"]
        lift = cut_off(lift, keep)
        for index, key in enumerate(CLASSES):
            self.mode_ref[index] = after[key]
            self.lift_ref[index] = lift[key]

    def finish(self, level, plane):
        for component in range(3):
            shifted = pltpu.roll(self.pipe_ref[component, 0], 1, 1) * self.keep_first
            residual = (self.pipe_ref[component, 1] + shifted) - self.w(level, component, plane)
            self.set_w(level + 1, component, plane, residual)
            self.set_p(level + 1, component, plane, residual * self.inverses(plane))


def sweep(level, sides, cuts, shift):
    for side, start, count, wanted in sides:
        side.begin(start - shift)
    for step in range(max(count for _, _, count, _ in sides) + 2):
        for side, start, count, wanted in sides:
            plane, end = start + step, start + count
            if wanted <= plane - 2 < end:
                side.produce(level + 1, plane - 2, plane - 2 - shift)
            if wanted <= plane - 1 < end:
                side.finish(level, plane - 1)
            if plane < end:
                side.spread(plane, plane + 1 - shift, cuts.get(plane))


def moduli_of(rho):
    return jnp.where(rho > 0.0, E_MIN + rho * rho * rho * (1.0 - E_MIN), 0.0)


def inverse_of(free, around):
    return free / (free * (DIAGONAL * around) + (1.0 - free))


PAIR_LIST = [(i, j) for i in range(BASIS) for j in range(i + 1)]


def inner_kernel(shape, ext, p_ref, w_ref, field_ref, inverse_ref, totals_ref, z_ref, mode_ref, lift_ref, pipe_ref):
    rows, cols, depth = shape
    wide, shift = cols + 2 * HALO, HALO_X - 1
    field_ref[:, :8, :] = jnp.zeros((rows, 8, depth), jnp.float32)
    z_ref[:, :, :, wide:, :] = jnp.zeros((3, 2, z_ref.shape[2], 8, depth), jnp.float32)
    for row in range(rows):
        window = slice(row * wide, (row + 1) * wide)
        field_ref[row, 8:, :] = moduli_of(ext[0, window, :])
        for component in range(3):
            w_ref[0, component, row + 1] = ext[2 + component, window, :]

    def store(ref):
        def put(level, component, plane, value):
            ref[level, component, plane - shift] = value

        return put

    stages = Stages(
        shape,
        lambda plane: field_ref[plane - HALO_X, 8:, :],
        lambda plane: inverse_ref[plane - HALO_X],
        lambda level, component, plane: p_ref[level, component, plane - shift],
        lambda level, component, plane: w_ref[level, component, plane - shift],
        store(p_ref),
        store(w_ref),
        z_ref,
        mode_ref,
        lift_ref,
        pipe_ref,
    )
    inverse_ref[0] = jnp.zeros((wide, depth), jnp.float32)
    for row in range(1, rows):
        around = field_ref[row - 1, 8:, :] + field_ref[row - 1, 7 : 7 + wide, :]
        around = around + (field_ref[row, 8:, :] + field_ref[row, 7 : 7 + wide, :])
        inverse = inverse_of(ext[1, row * wide : (row + 1) * wide, :], stages.lift_moduli(around))
        inverse_ref[row] = inverse
        for component in range(3):
            p_ref[0, component, row + 1] = w_ref[0, component, row + 1] * inverse
    for row in range(1, rows):
        stages.produce(0, row + HALO_X, row + 1)

    for level in range(BASIS - 1):
        start, count = HALO_X + 1 + level, rows - 2 - 2 * level
        sweep(level, [(stages, start, count, start + 1)], {}, shift)

    first, last = HALO_X + BASIS, HALO_X + rows - 1 - (BASIS - 1)
    totals = [jnp.zeros((cols, depth), jnp.float32)] * (len(PAIR_LIST) + 1)
    before = load_modes(z_ref, first - shift, HALO, cols)
    for plane in range(first, last + 1):
        totals = add_dots(
            totals,
            lambda level, component: p_ref[level, component, plane - shift, HALO : HALO + cols, :],
            lambda level, component: w_ref[level, component, plane - shift, HALO : HALO + cols, :],
        )
        if plane < last:
            after = load_modes(z_ref, plane + 1 - shift, HALO, cols)
            energy = unit_energy(element_modes(before, after))
            totals[-1] = totals[-1] + field_ref[plane - HALO_X, 8 + HALO : 8 + HALO + cols, :] * energy
            before = after
    for index, total in enumerate(totals):
        totals_ref[index] = total


def add_dots(totals, p, w):
    totals = list(totals)
    for component in range(3):
        ps = [p(level, component) for level in range(BASIS)]
        ws = [w(level, component) for level in range(BASIS)]
        for index, (i, j) in enumerate(PAIR_LIST):
            totals[index] = totals[index] + ps[i] * ws[j]
    return totals


def outer_kernel(
    shape, ext, low_x, high_x, first, second, p_in, w_in, field_in, inverse_in, totals_in, p_ref, sums_out, *scratch
):
    rows, cols, depth = shape
    wide, long, shift = cols + 2 * HALO, rows + 2 * HALO_X, HALO_X - 1
    halo_ref, field_ref, inverse_ref, w_ref, z_ref, *both = scratch
    cuts = grid_cuts(rows)
    own = range(HALO_X, HALO_X + rows)
    z_ref[:, :, :, wide:, :] = jnp.zeros((3, 2, long, 8, depth), jnp.float32)
    field_ref[:, :8, :] = jnp.zeros((long, 8, depth), jnp.float32)

    def rims(low, high):
        for rim, begin in ((low, 0), (high, HALO_X)):
            for field in range(FIELDS):
                for layer in range(HALO_X):
                    row = layer * 2 * HALO
                    halo_ref[field, begin + layer, :HALO, :] = rim[field, row : row + HALO, :]
                    halo_ref[field, begin + layer, HALO + cols :, :] = rim[field, row + HALO : row + 2 * HALO, :]

    by_parity("gx", first, second, rims)
    for field in range(FIELDS):
        begin, skip = low_x_run(field)
        for layer in range(HALO_X):
            if layer >= skip:
                row = (begin + layer - skip) * cols
                halo_ref[field, layer, HALO : HALO + cols, :] = low_x[row : row + cols, :]
            window = slice(layer * cols, (layer + 1) * cols)
            halo_ref[field, HALO_X + layer, HALO : HALO + cols, :] = high_x[field, window, :]

    def given(field, plane, begin=0, count=wide):
        if plane in own:
            row = (plane - HALO_X) * wide + begin
            return ext[field, row : row + count, :]
        return halo_ref[field, plane if plane < HALO_X else plane - rows, begin : begin + count, :]

    def fields(plane, begin=0, count=wide):
        if plane in own:
            return field_in[plane - HALO_X, 8 + begin : 8 + begin + count, :]
        return field_ref[plane, 8 + begin : 8 + begin + count, :]

    def inverses(plane):
        return inverse_in[plane - HALO_X] if HALO_X < plane < HALO_X + rows else inverse_ref[plane]

    def is_inner(level, plane):
        return HALO_X + 1 + level <= plane <= HALO_X + rows - 1 - level

    def p(level, component, plane, begin=0, count=wide):
        if is_inner(level, plane):
            return p_in[level, component, plane - shift, begin : begin + count, :]
        return p_ref[level, component, plane, begin : begin + count, :]

    def w(level, component, plane, begin=0, count=wide):
        if is_inner(level, plane):
            return w_in[level, component, plane - shift, begin : begin + count, :]
        if level == 0:
            return given(2 + component, plane, begin, count)
        return w_ref[level, component, plane, begin : begin + count, :]

    def set_p(level, component, plane, value):
        p_ref[level, component, plane] = value

    def set_w(level, component, plane, value):
        w_ref[level, component, plane] = value

    sides = [
        Stages(shape, fields, inverses, p, w, set_p, set_w, z_ref, both[0], both[1], both[2]),
        Stages(shape, fields, inverses, p, w, set_p, set_w, z_ref, both[3], both[4], both[5]),
    ]
    for plane in range(long):
        if plane not in own:
            field_ref[plane, 8:, :] = moduli_of(given(0, plane))
    edge_planes = [*range(1, HALO_X + 1), *range(HALO_X + rows, long)]
    for plane in edge_planes:
        around = fields(plane - 1) + fields(plane - 1, -1)
        if plane - 1 in cuts:
            around = around * cuts[plane - 1]
        around = around + (fields(plane) + fields(plane, -1))
        inverse = inverse_of(given(1, plane), sides[0].lift_moduli(around))
        inverse_ref[plane] = inverse
        for component in range(3):
            set_p(0, component, plane, given(2 + component, plane) * inverse)
    for plane in edge_planes:
        sides[0].produce(0, plane, plane)

    count = HALO_X + 1
    for level in range(BASIS - 1):
        for plane in (HALO_X + 1 + level, HALO_X + 2 + level, HALO_X + rows - 2 - level, HALO_X + rows - 1 - level):
            sides[0].produce(level, plane, plane)
        left, right = 1 + level, HALO_X + rows - 2 - level
        sweep(level, [(sides[0], left, count, left + 1), (sides[1], right, count, right + 1)], cuts, 0)

    last = BASIS - 1
    for plane in (HALO_X + 1 + last, HALO_X + rows - 1 - last):
        sides[0].produce(last, plane, plane)
    totals = [totals_in[index] for index in range(len(PAIR_LIST) + 1)]
    for plane in own:
        if not is_inner(last, plane):
            totals = add_dots(
                totals,
                lambda level, component: p(level, component, plane, HALO, cols),
                lambda level, component: w(level, component, plane, HALO, cols),
            )
        if not (is_inner(last, plane) and is_inner(last, plane + 1)):
            before = load_modes(z_ref, plane, HALO, cols)
            after = cut_off(load_modes(z_ref, plane + 1, HALO, cols), cuts.get(plane))
            energy = unit_energy(element_modes(before, after))
            totals[-1] = totals[-1] + fields(plane, HALO, cols) * energy
    slots = lane_index((1, 128))
    line = jnp.zeros((1, 128), jnp.float32)
    for index, total in enumerate(totals):
        share = jnp.sum(jnp.sum(total, axis=0, keepdims=True), axis=1, keepdims=True)
        line = line + jnp.where(slots == index, share, 0.0)
    sums_out[...] = jnp.broadcast_to(line, sums_out.shape)


def coefficients(shares):
    line = jnp.sum(shares, axis=0, keepdims=True)
    slots = lane_index(line.shape)

    def entry(index):
        return jnp.sum(jnp.where(slots == index, line, 0.0), axis=1, keepdims=True)

    inner = {}
    for index, (i, j) in enumerate(PAIR_LIST):
        inner[i, j] = inner[j, i] = entry(index)
    energy = {(BASIS - 1, BASIS - 1): entry(len(PAIR_LIST))}
    for i in range(BASIS):
        for j in range(min(i + 1, BASIS - 1)):
            energy[i, j] = inner[i, j + 1] + inner[i, j]
    lower, pivot, inverse, solved = {}, {}, {}, {}
    for k in range(BASIS):
        left = energy[k, k]
        for m in range(k):
            left = left - lower[k, m] * lower[k, m] * pivot[m]
        sound = left > 1e-6 * energy[k, k]
        pivot[k] = jnp.where(sound, left, 0.0)
        inverse[k] = jnp.where(sound, 1.0 / jnp.where(sound, left, 1.0), 0.0)
        for i in range(k + 1, BASIS):
            part = energy[i, k]
            for m in range(k):
                part = part - lower[i, m] * lower[k, m] * pivot[m]
            lower[i, k] = part * inverse[k]
    for k in range(BASIS):
        part = inner[k, 0]
        for m in range(k):
            part = part - lower[k, m] * solved[m]
        solved[k] = part
    result = {}
    for k in reversed(range(BASIS)):
        part = solved[k] * inverse[k]
        for m in range(k + 1, BASIS):
            part = part - lower[m, k] * result[m]
        result[k] = part
    return [result[k] for k in range(BASIS)]


def energy_kernel(
    shape, shares, inner, outer, own, low_x, high_x, u_out, weighted, first, second, u_ref, z_ref
):
    rows, cols, depth = shape
    wide, planes = cols + 2 * HALO, rows + 2 * REACH
    keep_last = jnp.where(lane_index((wide, depth)) < depth - 1, 1.0, 0.0)
    parts = [jnp.broadcast_to(part, (wide, depth)) for part in coefficients(shares[...])]
    cuts = grid_cuts(rows)
    for plane in range(planes + 1):
        source = plane + HALO_X - REACH
        for component in range(3):
            total = None
            for level in range(BASIS):
                if HALO_X + 1 + level <= source <= HALO_X + rows - 1 - level:
                    term = parts[level] * inner[level, component, source - HALO_X + 1]
                else:
                    term = parts[level] * outer[level, component, source]
                total = term if total is None else total + term
            lifted = pltpu.roll(total, depth - 1, 1) * keep_last
            z_ref[component, 0, plane] = lifted + total
            z_ref[component, 1, plane] = lifted - total
            row = plane - REACH
            if 0 <= row < rows:
                u_ref[component, row] = total
                u_out[component, row] = u_ref[component, row, HALO : HALO + cols, :]
    before = load_modes(z_ref, 0, HALO, cols)
    for plane in range(planes):
        row = plane - REACH
        after = load_modes(z_ref, plane + 1, HALO, cols)
        energy = unit_energy(element_modes(before, cut_off(after, cuts.get(row + HALO_X))))
        before = after
        if row < 0:
            rho = low_x[(row + HALO_X) * cols : (row + HALO_X + 1) * cols, :]
        elif row < rows:
            rho = own[0, row * cols : (row + 1) * cols, :]
        else:
            rho = high_x[0, (row - rows) * cols : (row - rows + 1) * cols, :]
        weighted[plane * cols : (plane + 1) * cols, :] = rho * (3.0 * rho * rho * (1.0 - E_MIN) * energy)

    def outer_rows(low, high):
        for layer in range(REACH):
            low[layer] = weighted[pl.ds(layer, planes, stride=cols), :]
            high[layer] = weighted[pl.ds(cols - REACH + layer, planes, stride=cols), :]

    by_parity("gy", first, second, outer_rows)


def cone_table():
    table, total = {}, 0.0
    for a in range(-2, 3):
        for b in range(-2, 3):
            for c in range(-2, 3):
                total += max(0.0, 3.0 - math.sqrt(a * a + b * b + c * c))
    for flat in (0, 1, 2, 4, 5, 8):
        for c in range(3):
            table[flat, c] = max(0.0, 3.0 - math.sqrt(flat + c * c))
    return table, total


def volume_row(total):
    return jnp.sum(total, axis=0, keepdims=True)


def filter_kernel(shape, weighted, from_first, from_second, own, lower, upper, root, volume, plane_ref):
    rows, cols, depth = shape
    wide, planes = cols + 8, rows + 2 * REACH
    table, total = cone_table()
    for plane in range(planes):
        plane_ref[plane * wide + REACH : plane * wide + REACH + cols, :] = weighted[plane * cols : (plane + 1) * cols, :]

    def neighbour_rows(from_low, from_high):
        for layer in range(REACH):
            plane_ref[pl.ds(layer, planes, stride=wide), :] = from_low[layer]
            plane_ref[pl.ds(REACH + cols + layer, planes, stride=wide), :] = from_high[layer]

    by_parity("gy", from_first, from_second, neighbour_rows)
    volume_sum = jnp.zeros((cols, depth), jnp.float32)
    for row in range(rows):
        spread = {}
        for a in range(-REACH, REACH + 1):
            for b in range(-REACH, REACH + 1):
                key = a * a + b * b
                value = plane_ref[pl.ds((row + REACH + a) * wide + REACH + b, cols), :]
                spread[key] = value if key not in spread else spread[key] + value
        sums = []
        for c in range(3):
            part = None
            for key, value in spread.items():
                if table[key, c] > 0.0:
                    term = table[key, c] * value
                    part = term if part is None else part + term
            sums.append(part)
        convolved = sums[0]
        for c in (1, 2):
            convolved = convolved + (pltpu.roll(sums[c], c, 1) + pltpu.roll(sums[c], depth - c, 1))
        window = slice(row * cols, (row + 1) * cols)
        rho = own[0, window, :]
        base = rho * jnp.sqrt(convolved / (total * rho))
        root[window, :] = base
        volume_sum = volume_sum + jnp.minimum(jnp.maximum(base, lower[window, :]), upper[window, :])
    volume[...] = jnp.broadcast_to(volume_row(volume_sum), volume.shape)


def scale_of(target, volumes):
    scale = None
    for volume in volumes:
        whole = jnp.sum(jnp.sum(volume[...], axis=0, keepdims=True), axis=1, keepdims=True)
        ratio = target / whole
        scale = ratio if scale is None else scale * ratio
    return scale


def trial_of(target, volumes, terms):
    root, lower, upper = terms
    return jnp.minimum(jnp.maximum(root[...] * scale_of(target, volumes), lower[...]), upper[...])


def trial_kernel(target, *refs):
    *volumes, root, lower, upper, out = refs
    out[...] = jnp.broadcast_to(volume_row(trial_of(target, volumes, (root, lower, upper))), out.shape)


def update_kernel(target, u, *refs):
    *volumes, root, lower, upper, new_density, displacement, made, sent = refs
    copies = [
        pltpu.make_async_copy(u, displacement, sent.at[0]),
        pltpu.make_async_copy(made, new_density, sent.at[1]),
    ]
    copies[0].start()
    made[...] = trial_of(target, volumes, (root, lower, upper))
    copies[1].start()
    for copy in copies:
        copy.wait()


def call(kernel, name, out_shapes, *args, scratch=(), flops=0, space=pltpu.VMEM, far=()):
    shapes = [jax.ShapeDtypeStruct(shape, jnp.float32) for shape in out_shapes]
    moved = sum(4 * math.prod(value.shape) for value in [*args, *shapes])
    return pl.pallas_call(
        kernel,
        name=name,
        out_shape=shapes,
        in_specs=[pl.BlockSpec(memory_space=space)] * len(args),
        out_specs=[pl.BlockSpec(memory_space=pltpu.HBM if i in far else pltpu.VMEM) for i in range(len(shapes))],
        scratch_shapes=[pltpu.VMEM(item, jnp.float32) if isinstance(item, tuple) else item for item in scratch],
        compiler_params=pltpu.CompilerParams(vmem_limit_bytes=VMEM_LIMIT),
        cost_estimate=pl.CostEstimate(flops=flops, bytes_accessed=moved, transcendentals=0),
    )(*args)


def exchange(low, high, axis):
    count = lax.axis_size(axis)
    from_low = lax.ppermute(high, axis, [(i, (i + 1) % count) for i in range(count)])
    from_high = lax.ppermute(low, axis, [((i + 1) % count, i) for i in range(count)])
    return from_low, from_high


def swap(first, second, axis, wrap):
    count = lax.axis_size(axis)
    assert count % 2 == 0
    ends = [(i, i + 1) for i in range(1, count - 1, 2)] + ([(count - 1, 0)] if wrap else [])
    pairs = [(i, i + 1) for i in range(0, count, 2)]
    both = lambda links: links + [(j, i) for i, j in links]
    order = (ends, pairs) if axis == "gx" else (pairs, ends)
    return tuple(lax.ppermute(value, axis, both(links)) for value, links in zip((first, second), order))


def everyone(shares):
    return lax.all_to_all(shares, AXES, 0, 0, tiled=True)


def shards(density, void_mask, solid_mask, fixed_mask, load_mask, traction):
    shape = rows, cols, depth = density.shape
    devices = lax.axis_size("gx") * lax.axis_size("gy")
    wide, long = cols + 2 * HALO, rows + 2 * HALO_X
    planes = rows + 2 * REACH
    named = lambda kernel: functools.partial(kernel, shape)
    flat = (rows * cols, depth)
    inputs = [
        pltpu.with_memory_space_constraint(value.reshape(*value.shape[:-3], *flat), pltpu.HBM)
        for value in (density, void_mask, solid_mask, fixed_mask, load_mask, traction)
    ]

    own, lower, upper, first, second, low_x, high_x = call(
        named(fields_kernel),
        "fields",
        [
            (FIELDS, *flat),
            flat,
            flat,
            (HALO, FIELDS, rows, depth),
            (HALO, FIELDS, rows, depth),
            (FIELDS, HALO_X * cols, depth),
            ((HALO_X + (FIELDS - 1) * (HALO_X - 1)) * cols, depth),
        ],
        *inputs,
        scratch=[pltpu.VMEM(value.shape, value.dtype) for value in inputs] + [pltpu.SemaphoreType.DMA((8,))],
        space=pltpu.HBM,
    )
    from_first, from_second = swap(first, second, "gy", False)
    low_x, high_x = exchange(low_x, high_x, "gx")
    ext, first, second = call(
        named(widen_kernel),
        "widen",
        [(FIELDS, rows * wide, depth)] + [(FIELDS, HALO_X * 2 * HALO, depth)] * 2,
        own,
        from_first,
        from_second,
    )
    first_xy, second_xy = swap(first, second, "gx", True)
    side = [(12, wide, depth), (12, wide, depth), (3, 2, wide, depth)]
    inner = call(
        named(inner_kernel),
        "inner",
        [
            (BASIS, 3, rows + 1, wide, depth),
            (BASIS, 3, rows + 1, wide, depth),
            (rows, 8 + wide, depth),
            (rows, wide, depth),
            (len(PAIR_LIST) + 1, cols, depth),
        ],
        ext,
        scratch=[(3, 2, rows + 1, wide + 8, depth), *side],
    )
    outer, sums = call(
        named(outer_kernel),
        "outer",
        [(BASIS, 3, long, wide, depth), (devices, 128)],
        ext,
        low_x,
        high_x,
        first_xy,
        second_xy,
        *inner,
        scratch=[
            (FIELDS, 2 * HALO_X, wide, depth),
            (long, 8 + wide, depth),
            (long, wide, depth),
            (BASIS, 3, long, wide, depth),
            (3, 2, long, wide + 8, depth),
            *side,
            *side,
        ],
    )
    u, weighted, first, second = call(
        named(energy_kernel),
        "energy",
        [(3, rows, cols, depth), (planes * cols, depth), (REACH, planes, depth), (REACH, planes, depth)],
        everyone(sums),
        inner[0],
        outer,
        own,
        low_x,
        high_x,
        scratch=[
            (3, rows, wide, depth),
            (3, 2, planes + 1, wide, depth),
        ],
    )
    from_first, from_second = swap(first, second, "gy", True)
    root, volume = call(
        named(filter_kernel),
        "filter",
        [flat, (devices, depth)],
        weighted,
        from_first,
        from_second,
        own,
        lower,
        upper,
        scratch=[(planes * (cols + 8), depth)],
    )
    target = VOLUME_SHARE * rows * cols * depth * devices
    terms, volumes = (root, lower, upper), [everyone(volume)]
    for _ in range(2):
        (volume,) = call(functools.partial(trial_kernel, target), "trial", [(devices, depth)], *volumes, *terms)
        volumes.append(everyone(volume))
    new_density, displacement = call(
        functools.partial(update_kernel, target),
        "update",
        [flat, u.shape],
        u,
        *volumes,
        *terms,
        scratch=[flat, pltpu.SemaphoreType.DMA((2,))],
        far=(0, 1),
    )
    return new_density.reshape(shape), displacement


def solution(mesh):
    placed = (P("gx", "gy", None),) * 5 + (P(None, "gx", "gy", None),)
    return jax.shard_map(
        shards,
        mesh=mesh,
        in_specs=placed,
        out_specs=(P("gx", "gy", None), P(None, "gx", "gy", None)),
        check_vma=False,
    )
```

```python
import functools
import math

import jax
import jax.numpy as jnp
import numpy as np
from jax import lax
from jax.experimental import pallas as pl
from jax.experimental.pallas import tpu as pltpu
from jax.sharding import PartitionSpec as P

E_MIN = 0.001
RHO_FLOOR = 0.001
MOVE_LIMIT = 0.2
VOLUME_SHARE = 0.4
BASIS = 4
REACH = 2
HALO = BASIS
HALO_X = BASIS + REACH
AXES = ("gx", "gy")
FIELDS = 5
VMEM_LIMIT = 40 * 1024 * 1024

POISSON = 0.3
LAME = POISSON / ((1.0 + POISSON) * (1.0 - 2.0 * POISSON))
SHEAR = 1.0 / (2.0 * (1.0 + POISSON))
NORMAL = 2.0 * SHEAR / 16.0
TRACE = LAME / 16.0
SHEAR_FIRST = SHEAR / 16.0
BEND = (LAME + 3.0 * SHEAR) / 48.0
BEND_MIX = LAME / 48.0
TWIST = SHEAR / 48.0
THIRD = (LAME + 4.0 * SHEAR) / 144.0
DIAGONAL = NORMAL + TRACE + 2.0 * SHEAR_FIRST + 2.0 * BEND + 2.0 * TWIST + THIRD
PAIRS = (("xdds", "zsdd"), ("ydds", "zdsd"), ("xdsd", "ysdd"))
TRIPLE = ("zdds", "ydsd", "xsdd")
CLASSES = [c + y + z for c in "xyz" for y in "sd" for z in "sd"]


def by_parity(axis, first, second, body):
    low_first = lax.rem(lax.axis_index(axis), 2) == (0 if axis == "gx" else 1)
    pl.when(low_first)(lambda: body(first, second))
    pl.when(jnp.logical_not(low_first))(lambda: body(second, first))


def lane_index(shape):
    return lax.broadcasted_iota(jnp.int32, shape, len(shape) - 1)


def load_modes(z_ref, plane, begin, count):
    modes = {}
    for number, component in enumerate("xyz"):
        for index, z in enumerate("sd"):
            low = z_ref[number, index, plane, begin : begin + count, :]
            high = z_ref[number, index, plane, begin + 1 : begin + 1 + count, :]
            modes[component + "s" + z] = high + low
            modes[component + "d" + z] = high - low
    return modes


def element_modes(before, after):
    modes = {}
    for key in CLASSES:
        if key[1:] != "ss":
            modes[key[0] + "s" + key[1:]] = after[key] + before[key]
        modes[key[0] + "d" + key[1:]] = after[key] - before[key]
    return modes


def mode_forces(u, moduli):
    forces = {}
    normal = moduli * NORMAL
    trace = (u["xdss"] + u["ysds"] + u["zssd"]) * (TRACE / NORMAL)
    for key in ("xdss", "ysds", "zssd"):
        forces[key] = normal * (u[key] + trace)
    shear = moduli * SHEAR_FIRST
    for one, other in (("ydss", "xsds"), ("zsds", "yssd"), ("xssd", "zdss")):
        forces[one] = forces[other] = shear * (u[one] + u[other])
    bend = moduli * BEND
    for one, other in PAIRS:
        forces[one] = bend * (u[one] + (BEND_MIX / BEND) * u[other])
        forces[other] = bend * (u[other] + (BEND_MIX / BEND) * u[one])
    twist = moduli * TWIST
    total = u[TRIPLE[0]] + u[TRIPLE[1]] + u[TRIPLE[2]]
    for key in TRIPLE:
        forces[key] = twist * (total + u[key])
    third = moduli * THIRD
    for component in "xyz":
        forces[component + "ddd"] = third * u[component + "ddd"]
    return forces


def unit_energy(u):
    trace = u["xdss"] + u["ysds"] + u["zssd"]
    energy = TRACE * (trace * trace)
    energy += NORMAL * (u["xdss"] ** 2 + u["ysds"] ** 2 + u["zssd"] ** 2)
    shears = [u[a] + u[b] for a, b in (("ydss", "xsds"), ("zsds", "yssd"), ("xssd", "zdss"))]
    energy += SHEAR_FIRST * (shears[0] ** 2 + shears[1] ** 2 + shears[2] ** 2)
    squares, mixed = 0.0, 0.0
    for one, other in PAIRS:
        squares += u[one] ** 2 + u[other] ** 2
        mixed += (u[one] + u[other]) ** 2
    energy += (BEND - BEND_MIX) * squares + BEND_MIX * mixed
    total = u[TRIPLE[0]] + u[TRIPLE[1]] + u[TRIPLE[2]]
    squares = total * total
    for key in TRIPLE:
        squares += u[key] ** 2
    energy += TWIST * squares
    energy += THIRD * (u["xddd"] ** 2 + u["yddd"] ** 2 + u["zddd"] ** 2)
    return energy


def low_x_run(field):
    return (0, 0) if field == 0 else (HALO_X + (HALO_X - 1) * (field - 1), 1)


def corner_run(field, layer):
    side = 2 * HALO
    return (layer * side, 0) if field == 0 else (HALO_X * side + (HALO_X * (field - 1) + layer) * (side - 1), 1)


def fields_kernel(shape, *refs):
    rows, cols, _ = shape
    (density_in, void_in, solid_in, fixed_in, load_in, traction_in) = refs[:6]
    (own, lower, upper, first, second, low_x, high_x) = refs[6:13]
    density, void, solid, fixed, load, traction, arrived = refs[13:]
    pieces = [(fixed_in, fixed), (load_in, load)]
    pieces += [(traction_in.at[component], traction.at[component]) for component in range(3)]
    pieces += [(density_in, density), (void_in, void), (solid_in, solid)]
    copies = [pltpu.make_async_copy(s, t, arrived.at[i]) for i, (s, t) in enumerate(pieces)]
    for copy in copies:
        copy.start()

    def send(field):
        low_x[field] = own[field, : HALO_X * cols, :]
        begin, skip = low_x_run(field)
        count = (HALO_X - skip) * cols
        high_x[begin * cols : begin * cols + count, :] = own[field, rows * cols - count :, :]

        def outer_rows(low, high):
            for layer in range(HALO):
                low[layer, field] = own[field, pl.ds(layer, rows, stride=cols), :]
                high[layer, field] = own[field, pl.ds(cols - HALO + layer, rows, stride=cols), :]

        by_parity("gy", first, second, outer_rows)

    copies[0].wait()
    copies[1].wait()
    free = (1 - fixed[...]).astype(jnp.float32)
    own[1] = free
    send(1)
    for component in range(3):
        copies[2 + component].wait()
        own[2 + component] = own[1] * load[...].astype(jnp.float32) * traction[component]
        send(2 + component)
    for copy in copies[5:]:
        copy.wait()
    is_solid, is_void = solid[...] == 1, void[...] == 1
    rho = jnp.where(is_solid, 1.0, jnp.where(is_void, RHO_FLOOR, density[...]))
    own[0] = rho
    send(0)
    least = jnp.maximum(RHO_FLOOR, rho - MOVE_LIMIT)
    most = jnp.minimum(1.0, rho + MOVE_LIMIT)
    lower[...] = jnp.where(is_solid, 1.0, jnp.where(is_void, RHO_FLOOR, least))
    upper[...] = jnp.where(is_solid, 1.0, jnp.where(is_void, RHO_FLOOR, most))


def widen_kernel(shape, own, from_first, from_second, ext, first, second):
    rows, cols, _ = shape
    wide = cols + 2 * HALO

    def neighbour_rows(from_low, from_high):
        for field in range(FIELDS):
            for layer in range(HALO):
                ext[field, pl.ds(layer, rows, stride=wide), :] = from_low[layer, field]
                ext[field, pl.ds(cols + HALO + layer, rows, stride=wide), :] = from_high[layer, field]

    by_parity("gy", from_first, from_second, neighbour_rows)
    for field in range(FIELDS):
        for row in range(rows):
            ext[field, pl.ds(row * wide + HALO, cols), :] = own[field, pl.ds(row * cols, cols), :]

    def corners(low, high):
        for target, begin in ((low, 0), (high, rows - HALO_X)):
            for field in range(FIELDS):
                for layer in range(HALO_X):
                    row, skip = corner_run(field, layer)
                    middle, source = row + HALO - skip, (begin + layer) * wide
                    target[row:middle, :] = ext[field, source + skip : source + HALO, :]
                    source += cols + HALO
                    target[middle : middle + HALO, :] = ext[field, source : source + HALO, :]

    by_parity("gx", first, second, corners)


def grid_cuts(rows):
    place, last = lax.axis_index("gx"), lax.axis_size("gx") - 1
    return {
        HALO_X - 1: jnp.where(place == 0, 0.0, 1.0),
        HALO_X + rows - 1: jnp.where(place == last, 0.0, 1.0),
    }


def cut_off(values, keep):
    return values if keep is None else {key: value * keep for key, value in values.items()}


class Stages:
    def __init__(self, shape, fields, inverses, p, w, set_p, set_w, z_ref, mode_ref, lift_ref, pipe_ref):
        self.wide, self.depth = shape[1] + 2 * HALO, shape[2]
        lanes = lane_index((self.wide, self.depth))
        self.keep_last = jnp.where(lanes < self.depth - 1, 1.0, 0.0)
        self.keep_first = jnp.where(lanes > 0, 1.0, 0.0)
        self.fields, self.inverses, self.p, self.w = fields, inverses, p, w
        self.set_p, self.set_w = set_p, set_w
        self.z_ref, self.mode_ref, self.lift_ref, self.pipe_ref = z_ref, mode_ref, lift_ref, pipe_ref

    def lift_moduli(self, around):
        return around + pltpu.roll(around, 1, 1) * self.keep_first

    def produce(self, level, plane, slot):
        for component in range(3):
            value = self.p(level, component, plane)
            lifted = pltpu.roll(value, self.depth - 1, 1) * self.keep_last
            self.z_ref[component, 0, slot, : self.wide] = lifted + value
            self.z_ref[component, 1, slot, : self.wide] = lifted - value

    def begin(self, slot):
        modes = load_modes(self.z_ref, slot, 0, self.wide)
        for index, key in enumerate(CLASSES):
            self.mode_ref[index] = modes[key]
            self.lift_ref[index] = jnp.zeros((self.wide, self.depth), jnp.float32)

    def spread(self, plane, slot, keep=None):
        after = load_modes(self.z_ref, slot, 0, self.wide)
        before = {key: self.mode_ref[index] for index, key in enumerate(CLASSES)}
        lift = {key: self.lift_ref[index] for index, key in enumerate(CLASSES)}
        forces = mode_forces(element_modes(before, cut_off(after, keep)), self.fields(plane))
        for number, component in enumerate("xyz"):
            along_z = {}
            for z in "sd":
                along_y = {}
                for y in "sd":
                    key = component + y + z
                    slope = forces[component + "d" + y + z]
                    if y + z == "ss":
                        along_y[y] = lift[key] - slope
                        lift[key] = slope
                    else:
                        mean = forces[component + "s" + y + z]
                        along_y[y] = lift[key] + (mean - slope)
                        lift[key] = mean + slope
                along_z[z] = (along_y["s"] - along_y["d"]) + pltpu.roll(along_y["s"] + along_y["d"], 1, 0)
            self.pipe_ref[number, 0] = along_z["s"] + along_z["d"]
            self.pipe_ref[number, 1] = along_z["s"] - along_z["d"]
        lift = cut_off(lift, keep)
        for index, key in enumerate(CLASSES):
            self.mode_ref[index] = after[key]
            self.lift_ref[index] = lift[key]

    def finish(self, level, plane):
        for component in range(3):
            shifted = pltpu.roll(self.pipe_ref[component, 0], 1, 1) * self.keep_first
            residual = (self.pipe_ref[component, 1] + shifted) - self.w(level, component, plane)
            self.set_w(level + 1, component, plane, residual)
            self.set_p(level + 1, component, plane, residual * self.inverses(plane))


def sweep(level, sides, cuts, shift):
    for side, start, count, wanted in sides:
        side.begin(start - shift)
    for step in range(max(count for _, _, count, _ in sides) + 2):
        for side, start, count, wanted in sides:
            plane, end = start + step, start + count
            if wanted <= plane - 2 < end:
                side.produce(level + 1, plane - 2, plane - 2 - shift)
            if wanted <= plane - 1 < end:
                side.finish(level, plane - 1)
            if plane < end:
                side.spread(plane, plane + 1 - shift, cuts.get(plane))


def moduli_of(rho):
    return jnp.where(rho > 0.0, E_MIN + rho * rho * rho * (1.0 - E_MIN), 0.0)


def inverse_of(free, around):
    return free / (free * (DIAGONAL * around) + (1.0 - free))


PAIR_LIST = [(i, j) for i in range(BASIS) for j in range(i + 1)]


def inner_kernel(shape, ext, p_ref, w_ref, field_ref, inverse_ref, totals_ref, z_ref, mode_ref, lift_ref, pipe_ref):
    rows, cols, depth = shape
    wide, shift = cols + 2 * HALO, HALO_X - 1
    field_ref[:, :8, :] = jnp.zeros((rows, 8, depth), jnp.float32)
    z_ref[:, :, :, wide:, :] = jnp.zeros((3, 2, z_ref.shape[2], 8, depth), jnp.float32)
    for row in range(rows):
        window = slice(row * wide, (row + 1) * wide)
        field_ref[row, 8:, :] = moduli_of(ext[0, window, :])
        for component in range(3):
            w_ref[0, component, row + 1] = ext[2 + component, window, :]

    def store(ref):
        def put(level, component, plane, value):
            ref[level, component, plane - shift] = value

        return put

    stages = Stages(
        shape,
        lambda plane: field_ref[plane - HALO_X, 8:, :],
        lambda plane: inverse_ref[plane - HALO_X],
        lambda level, component, plane: p_ref[level, component, plane - shift],
        lambda level, component, plane: w_ref[level, component, plane - shift],
        store(p_ref),
        store(w_ref),
        z_ref,
        mode_ref,
        lift_ref,
        pipe_ref,
    )
    inverse_ref[0] = jnp.zeros((wide, depth), jnp.float32)
    for row in range(1, rows):
        around = field_ref[row - 1, 8:, :] + field_ref[row - 1, 7 : 7 + wide, :]
        around = around + (field_ref[row, 8:, :] + field_ref[row, 7 : 7 + wide, :])
        inverse = inverse_of(ext[1, row * wide : (row + 1) * wide, :], stages.lift_moduli(around))
        inverse_ref[row] = inverse
        for component in range(3):
            p_ref[0, component, row + 1] = w_ref[0, component, row + 1] * inverse
    for row in range(1, rows):
        stages.produce(0, row + HALO_X, row + 1)

    for level in range(BASIS - 1):
        start, count = HALO_X + 1 + level, rows - 2 - 2 * level
        sweep(level, [(stages, start, count, start + 1)], {}, shift)

    first, last = HALO_X + BASIS, HALO_X + rows - 1 - (BASIS - 1)
    totals = [jnp.zeros((cols, depth), jnp.float32)] * (len(PAIR_LIST) + 1)
    before = load_modes(z_ref, first - shift, HALO, cols)
    for plane in range(first, last + 1):
        totals = add_dots(
            totals,
            lambda level, component: p_ref[level, component, plane - shift, HALO : HALO + cols, :],
            lambda level, component: w_ref[level, component, plane - shift, HALO : HALO + cols, :],
        )
        if plane < last:
            after = load_modes(z_ref, plane + 1 - shift, HALO, cols)
            energy = unit_energy(element_modes(before, after))
            totals[-1] = totals[-1] + field_ref[plane - HALO_X, 8 + HALO : 8 + HALO + cols, :] * energy
            before = after
    for index, total in enumerate(totals):
        totals_ref[index] = total


def add_dots(totals, p, w):
    totals = list(totals)
    for component in range(3):
        ps = [p(level, component) for level in range(BASIS)]
        ws = [w(level, component) for level in range(BASIS)]
        for index, (i, j) in enumerate(PAIR_LIST):
            totals[index] = totals[index] + ps[i] * ws[j]
    return totals


def outer_kernel(
    shape, ext, low_x, high_x, first, second, p_in, w_in, field_in, inverse_in, totals_in, p_ref, sums_out, *scratch
):
    rows, cols, depth = shape
    wide, long, shift = cols + 2 * HALO, rows + 2 * HALO_X, HALO_X - 1
    halo_ref, field_ref, inverse_ref, w_ref, z_ref, *both = scratch
    cuts = grid_cuts(rows)
    own = range(HALO_X, HALO_X + rows)
    z_ref[:, :, :, wide:, :] = jnp.zeros((3, 2, long, 8, depth), jnp.float32)
    field_ref[:, :8, :] = jnp.zeros((long, 8, depth), jnp.float32)

    def rims(low, high):
        for rim, begin in ((low, 0), (high, HALO_X)):
            for field in range(FIELDS):
                for layer in range(HALO_X):
                    row, skip = corner_run(field, layer)
                    middle = row + HALO - skip
                    if skip:
                        halo_ref[field, begin + layer, :skip, :] = jnp.zeros((skip, depth), jnp.float32)
                    halo_ref[field, begin + layer, skip:HALO, :] = rim[row:middle, :]
                    halo_ref[field, begin + layer, HALO + cols :, :] = rim[middle : middle + HALO, :]

    by_parity("gx", first, second, rims)
    for field in range(FIELDS):
        begin, skip = low_x_run(field)
        for layer in range(HALO_X):
            if layer >= skip:
                row = (begin + layer - skip) * cols
                halo_ref[field, layer, HALO : HALO + cols, :] = low_x[row : row + cols, :]
            window = slice(layer * cols, (layer + 1) * cols)
            halo_ref[field, HALO_X + layer, HALO : HALO + cols, :] = high_x[field, window, :]

    def given(field, plane, begin=0, count=wide):
        if plane in own:
            row = (plane - HALO_X) * wide + begin
            return ext[field, row : row + count, :]
        return halo_ref[field, plane if plane < HALO_X else plane - rows, begin : begin + count, :]

    def fields(plane, begin=0, count=wide):
        if plane in own:
            return field_in[plane - HALO_X, 8 + begin : 8 + begin + count, :]
        return field_ref[plane, 8 + begin : 8 + begin + count, :]

    def inverses(plane):
        return inverse_in[plane - HALO_X] if HALO_X < plane < HALO_X + rows else inverse_ref[plane]

    def is_inner(level, plane):
        return HALO_X + 1 + level <= plane <= HALO_X + rows - 1 - level

    def p(level, component, plane, begin=0, count=wide):
        if is_inner(level, plane):
            return p_in[level, component, plane - shift, begin : begin + count, :]
        return p_ref[level, component, plane, begin : begin + count, :]

    def w(level, component, plane, begin=0, count=wide):
        if is_inner(level, plane):
            return w_in[level, component, plane - shift, begin : begin + count, :]
        if level == 0:
            return given(2 + component, plane, begin, count)
        return w_ref[level, component, plane, begin : begin + count, :]

    def set_p(level, component, plane, value):
        p_ref[level, component, plane] = value

    def set_w(level, component, plane, value):
        w_ref[level, component, plane] = value

    sides = [
        Stages(shape, fields, inverses, p, w, set_p, set_w, z_ref, both[0], both[1], both[2]),
        Stages(shape, fields, inverses, p, w, set_p, set_w, z_ref, both[3], both[4], both[5]),
    ]
    for plane in range(long):
        if plane not in own:
            field_ref[plane, 8:, :] = moduli_of(given(0, plane))
    edge_planes = [*range(1, HALO_X + 1), *range(HALO_X + rows, long)]
    for plane in edge_planes:
        around = fields(plane - 1) + fields(plane - 1, -1)
        if plane - 1 in cuts:
            around = around * cuts[plane - 1]
        around = around + (fields(plane) + fields(plane, -1))
        inverse = inverse_of(given(1, plane), sides[0].lift_moduli(around))
        inverse_ref[plane] = inverse
        for component in range(3):
            set_p(0, component, plane, given(2 + component, plane) * inverse)
    for plane in edge_planes:
        sides[0].produce(0, plane, plane)

    count = HALO_X + 1
    for level in range(BASIS - 1):
        for plane in (HALO_X + 1 + level, HALO_X + 2 + level, HALO_X + rows - 2 - level, HALO_X + rows - 1 - level):
            sides[0].produce(level, plane, plane)
        left, right = 1 + level, HALO_X + rows - 2 - level
        sweep(level, [(sides[0], left, count, left + 1), (sides[1], right, count, right + 1)], cuts, 0)

    last = BASIS - 1
    for plane in (HALO_X + 1 + last, HALO_X + rows - 1 - last):
        sides[0].produce(last, plane, plane)
    totals = [totals_in[index] for index in range(len(PAIR_LIST) + 1)]
    for plane in own:
        if not is_inner(last, plane):
            totals = add_dots(
                totals,
                lambda level, component: p(level, component, plane, HALO, cols),
                lambda level, component: w(level, component, plane, HALO, cols),
            )
        if not (is_inner(last, plane) and is_inner(last, plane + 1)):
            before = load_modes(z_ref, plane, HALO, cols)
            after = cut_off(load_modes(z_ref, plane + 1, HALO, cols), cuts.get(plane))
            energy = unit_energy(element_modes(before, after))
            totals[-1] = totals[-1] + fields(plane, HALO, cols) * energy
    slots = lane_index((1, 128))
    line = jnp.zeros((1, 128), jnp.float32)
    for index, total in enumerate(totals):
        share = jnp.sum(jnp.sum(total, axis=0, keepdims=True), axis=1, keepdims=True)
        line = line + jnp.where(slots == index, share, 0.0)
    sums_out[...] = jnp.broadcast_to(line, sums_out.shape)


def coefficients(shares):
    line = jnp.sum(shares, axis=0, keepdims=True)
    slots = lane_index(line.shape)

    def entry(index):
        return jnp.sum(jnp.where(slots == index, line, 0.0), axis=1, keepdims=True)

    inner = {}
    for index, (i, j) in enumerate(PAIR_LIST):
        inner[i, j] = inner[j, i] = entry(index)
    energy = {(BASIS - 1, BASIS - 1): entry(len(PAIR_LIST))}
    for i in range(BASIS):
        for j in range(min(i + 1, BASIS - 1)):
            energy[i, j] = inner[i, j + 1] + inner[i, j]
    lower, pivot, inverse, solved = {}, {}, {}, {}
    for k in range(BASIS):
        left = energy[k, k]
        for m in range(k):
            left = left - lower[k, m] * lower[k, m] * pivot[m]
        sound = left > 1e-6 * energy[k, k]
        pivot[k] = jnp.where(sound, left, 0.0)
        inverse[k] = jnp.where(sound, 1.0 / jnp.where(sound, left, 1.0), 0.0)
        for i in range(k + 1, BASIS):
            part = energy[i, k]
            for m in range(k):
                part = part - lower[i, m] * lower[k, m] * pivot[m]
            lower[i, k] = part * inverse[k]
    for k in range(BASIS):
        part = inner[k, 0]
        for m in range(k):
            part = part - lower[k, m] * solved[m]
        solved[k] = part
    result = {}
    for k in reversed(range(BASIS)):
        part = solved[k] * inverse[k]
        for m in range(k + 1, BASIS):
            part = part - lower[m, k] * result[m]
        result[k] = part
    return [result[k] for k in range(BASIS)]


def energy_kernel(
    shape, shares, inner, outer, own, low_x, high_x, u_out, weighted, first, second, u_ref, z_ref
):
    rows, cols, depth = shape
    wide, planes = cols + 2 * HALO, rows + 2 * REACH
    keep_last = jnp.where(lane_index((wide, depth)) < depth - 1, 1.0, 0.0)
    parts = [jnp.broadcast_to(part, (wide, depth)) for part in coefficients(shares[...])]
    cuts = grid_cuts(rows)
    for plane in range(planes + 1):
        source = plane + HALO_X - REACH
        for component in range(3):
            total = None
            for level in range(BASIS):
                if HALO_X + 1 + level <= source <= HALO_X + rows - 1 - level:
                    term = parts[level] * inner[level, component, source - HALO_X + 1]
                else:
                    term = parts[level] * outer[level, component, source]
                total = term if total is None else total + term
            lifted = pltpu.roll(total, depth - 1, 1) * keep_last
            z_ref[component, 0, plane] = lifted + total
            z_ref[component, 1, plane] = lifted - total
            row = plane - REACH
            if 0 <= row < rows:
                u_ref[component, row] = total
                u_out[component, row] = u_ref[component, row, HALO : HALO + cols, :]
    before = load_modes(z_ref, 0, HALO, cols)
    for plane in range(planes):
        row = plane - REACH
        after = load_modes(z_ref, plane + 1, HALO, cols)
        energy = unit_energy(element_modes(before, cut_off(after, cuts.get(row + HALO_X))))
        before = after
        if row < 0:
            rho = low_x[(row + HALO_X) * cols : (row + HALO_X + 1) * cols, :]
        elif row < rows:
            rho = own[0, row * cols : (row + 1) * cols, :]
        else:
            rho = high_x[0, (row - rows) * cols : (row - rows + 1) * cols, :]
        weighted[plane * cols : (plane + 1) * cols, :] = rho * (3.0 * rho * rho * (1.0 - E_MIN) * energy)

    def outer_rows(low, high):
        for layer in range(REACH):
            low[layer] = weighted[pl.ds(layer, planes, stride=cols), :]
            high[layer] = weighted[pl.ds(cols - REACH + layer, planes, stride=cols), :]

    by_parity("gy", first, second, outer_rows)


def cone_table():
    table, total = {}, 0.0
    for a in range(-2, 3):
        for b in range(-2, 3):
            for c in range(-2, 3):
                total += max(0.0, 3.0 - math.sqrt(a * a + b * b + c * c))
    for flat in (0, 1, 2, 4, 5, 8):
        for c in range(3):
            table[flat, c] = max(0.0, 3.0 - math.sqrt(flat + c * c))
    return table, total


def volume_row(total):
    return jnp.sum(total, axis=0, keepdims=True)


def filter_kernel(shape, weighted, from_first, from_second, own, lower, upper, root, volume, plane_ref):
    rows, cols, depth = shape
    wide, planes = cols + 8, rows + 2 * REACH
    table, total = cone_table()
    for plane in range(planes):
        plane_ref[plane * wide + REACH : plane * wide + REACH + cols, :] = weighted[plane * cols : (plane + 1) * cols, :]

    def neighbour_rows(from_low, from_high):
        for layer in range(REACH):
            plane_ref[pl.ds(layer, planes, stride=wide), :] = from_low[layer]
            plane_ref[pl.ds(REACH + cols + layer, planes, stride=wide), :] = from_high[layer]

    by_parity("gy", from_first, from_second, neighbour_rows)
    volume_sum = jnp.zeros((cols, depth), jnp.float32)
    for row in range(rows):
        spread = {}
        for a in range(-REACH, REACH + 1):
            for b in range(-REACH, REACH + 1):
                key = a * a + b * b
                value = plane_ref[pl.ds((row + REACH + a) * wide + REACH + b, cols), :]
                spread[key] = value if key not in spread else spread[key] + value
        sums = []
        for c in range(3):
            part = None
            for key, value in spread.items():
                if table[key, c] > 0.0:
                    term = table[key, c] * value
                    part = term if part is None else part + term
            sums.append(part)
        convolved = sums[0]
        for c in (1, 2):
            convolved = convolved + (pltpu.roll(sums[c], c, 1) + pltpu.roll(sums[c], depth - c, 1))
        window = slice(row * cols, (row + 1) * cols)
        rho = own[0, window, :]
        base = rho * jnp.sqrt(convolved / (total * rho))
        root[window, :] = base
        volume_sum = volume_sum + jnp.minimum(jnp.maximum(base, lower[window, :]), upper[window, :])
    volume[...] = jnp.broadcast_to(volume_row(volume_sum), volume.shape)


def scale_of(target, volumes):
    scale = None
    for volume in volumes:
        whole = jnp.sum(jnp.sum(volume[...], axis=0, keepdims=True), axis=1, keepdims=True)
        ratio = target / whole
        scale = ratio if scale is None else scale * ratio
    return scale


def trial_of(target, volumes, terms):
    root, lower, upper = terms
    return jnp.minimum(jnp.maximum(root[...] * scale_of(target, volumes), lower[...]), upper[...])


def trial_kernel(target, *refs):
    *volumes, root, lower, upper, out = refs
    out[...] = jnp.broadcast_to(volume_row(trial_of(target, volumes, (root, lower, upper))), out.shape)


def update_kernel(target, u, *refs):
    *volumes, root, lower, upper, new_density, displacement, made, sent = refs
    copies = [
        pltpu.make_async_copy(u, displacement, sent.at[0]),
        pltpu.make_async_copy(made, new_density, sent.at[1]),
    ]
    copies[0].start()
    made[...] = trial_of(target, volumes, (root, lower, upper))
    copies[1].start()
    for copy in copies:
        copy.wait()


def call(kernel, name, out_shapes, *args, scratch=(), flops=0, space=pltpu.VMEM, far=()):
    shapes = [jax.ShapeDtypeStruct(shape, jnp.float32) for shape in out_shapes]
    moved = sum(4 * math.prod(value.shape) for value in [*args, *shapes])
    return pl.pallas_call(
        kernel,
        name=name,
        out_shape=shapes,
        in_specs=[pl.BlockSpec(memory_space=space)] * len(args),
        out_specs=[pl.BlockSpec(memory_space=pltpu.HBM if i in far else pltpu.VMEM) for i in range(len(shapes))],
        scratch_shapes=[pltpu.VMEM(item, jnp.float32) if isinstance(item, tuple) else item for item in scratch],
        compiler_params=pltpu.CompilerParams(vmem_limit_bytes=VMEM_LIMIT),
        cost_estimate=pl.CostEstimate(flops=flops, bytes_accessed=moved, transcendentals=0),
    )(*args)


def exchange(low, high, axis):
    count = lax.axis_size(axis)
    from_low = lax.ppermute(high, axis, [(i, (i + 1) % count) for i in range(count)])
    from_high = lax.ppermute(low, axis, [((i + 1) % count, i) for i in range(count)])
    return from_low, from_high


def swap(first, second, axis, wrap):
    count = lax.axis_size(axis)
    assert count % 2 == 0
    ends = [(i, i + 1) for i in range(1, count - 1, 2)] + ([(count - 1, 0)] if wrap else [])
    pairs = [(i, i + 1) for i in range(0, count, 2)]
    both = lambda links: links + [(j, i) for i, j in links]
    order = (ends, pairs) if axis == "gx" else (pairs, ends)
    return tuple(lax.ppermute(value, axis, both(links)) for value, links in zip((first, second), order))


def everyone(shares):
    return lax.all_to_all(shares, AXES, 0, 0, tiled=True)


def shards(density, void_mask, solid_mask, fixed_mask, load_mask, traction):
    shape = rows, cols, depth = density.shape
    devices = lax.axis_size("gx") * lax.axis_size("gy")
    wide, long = cols + 2 * HALO, rows + 2 * HALO_X
    planes = rows + 2 * REACH
    named = lambda kernel: functools.partial(kernel, shape)
    flat = (rows * cols, depth)
    inputs = [
        pltpu.with_memory_space_constraint(value.reshape(*value.shape[:-3], *flat), pltpu.HBM)
        for value in (density, void_mask, solid_mask, fixed_mask, load_mask, traction)
    ]

    own, lower, upper, first, second, low_x, high_x = call(
        named(fields_kernel),
        "fields",
        [
            (FIELDS, *flat),
            flat,
            flat,
            (HALO, FIELDS, rows, depth),
            (HALO, FIELDS, rows, depth),
            (FIELDS, HALO_X * cols, depth),
            ((HALO_X + (FIELDS - 1) * (HALO_X - 1)) * cols, depth),
        ],
        *inputs,
        scratch=[pltpu.VMEM(value.shape, value.dtype) for value in inputs] + [pltpu.SemaphoreType.DMA((8,))],
        space=pltpu.HBM,
    )
    from_first, from_second = swap(first, second, "gy", False)
    low_x, high_x = exchange(low_x, high_x, "gx")
    ext, first, second = call(
        named(widen_kernel),
        "widen",
        [(FIELDS, rows * wide, depth)] + [(corner_run(FIELDS, 0)[0], depth)] * 2,
        own,
        from_first,
        from_second,
    )
    first_xy, second_xy = swap(first, second, "gx", True)
    side = [(12, wide, depth), (12, wide, depth), (3, 2, wide, depth)]
    inner = call(
        named(inner_kernel),
        "inner",
        [
            (BASIS, 3, rows + 1, wide, depth),
            (BASIS, 3, rows + 1, wide, depth),
            (rows, 8 + wide, depth),
            (rows, wide, depth),
            (len(PAIR_LIST) + 1, cols, depth),
        ],
        ext,
        scratch=[(3, 2, rows + 1, wide + 8, depth), *side],
    )
    outer, sums = call(
        named(outer_kernel),
        "outer",
        [(BASIS, 3, long, wide, depth), (devices, 128)],
        ext,
        low_x,
        high_x,
        first_xy,
        second_xy,
        *inner,
        scratch=[
            (FIELDS, 2 * HALO_X, wide, depth),
            (long, 8 + wide, depth),
            (long, wide, depth),
            (BASIS, 3, long, wide, depth),
            (3, 2, long, wide + 8, depth),
            *side,
            *side,
        ],
    )
    u, weighted, first, second = call(
        named(energy_kernel),
        "energy",
        [(3, rows, cols, depth), (planes * cols, depth), (REACH, planes, depth), (REACH, planes, depth)],
        everyone(sums),
        inner[0],
        outer,
        own,
        low_x,
        high_x,
        scratch=[
            (3, rows, wide, depth),
            (3, 2, planes + 1, wide, depth),
        ],
    )
    from_first, from_second = swap(first, second, "gy", True)
    root, volume = call(
        named(filter_kernel),
        "filter",
        [flat, (devices, depth)],
        weighted,
        from_first,
        from_second,
        own,
        lower,
        upper,
        scratch=[(planes * (cols + 8), depth)],
    )
    target = VOLUME_SHARE * rows * cols * depth * devices
    terms, volumes = (root, lower, upper), [everyone(volume)]
    for _ in range(2):
        (volume,) = call(functools.partial(trial_kernel, target), "trial", [(devices, depth)], *volumes, *terms)
        volumes.append(everyone(volume))
    new_density, displacement = call(
        functools.partial(update_kernel, target),
        "update",
        [flat, u.shape],
        u,
        *volumes,
        *terms,
        scratch=[flat, pltpu.SemaphoreType.DMA((2,))],
        far=(0, 1),
    )
    return new_density.reshape(shape), displacement


def solution(mesh):
    placed = (P("gx", "gy", None),) * 5 + (P(None, "gx", "gy", None),)
    return jax.shard_map(
        shards,
        mesh=mesh,
        in_specs=placed,
        out_specs=(P("gx", "gy", None), P(None, "gx", "gy", None)),
        check_vma=False,
    )
```
